32 devices in a mesh: copies: 2 (over y), grid: 4 (over z), slab: 4 (over x, core).
Axes of the slice: x: 2, y: 2, z: 4, core: 2. Of those that a mesh axis runs over, the one named last changes fastest.
Arguments:
- field: float32 [8, 128, 64, 128], P(('copies', 'grid'), 'slab'), parts along dimension 0, may hold values from -6 to 6
- levels: int32 [8, 5], P(('copies', 'grid')), parts along dimension 0, may hold values from 1 to 3
- owner: int32 [256], P('copies'), parts along dimension 0, may hold values from 0 to 127, each once
Outputs:
- combined: float32 [256, 64, 128], P(('copies', 'grid'), 'slab'), parts along dimension 0
The draws below stay inside these ranges and needn't reach their ends.
There are 2 independent parts, one for each index of `copies`. The reference program is written for one: setup_inputs(seed, part) draws one part's arguments, and reference() takes and returns one part's arrays. A program takes and returns all parts, laid end to end along the dimension named above; each array names one. Nothing has to cross between parts.
All inputs are finite; a program needn't handle non-finite values.
Results may differ from the reference program's by a relative error of at most 0.0003.
Values sent between devices are 32-bit elements; how exact they have to be, the bound alone decides.
No kernel may reach another device: no remote copies, remote signals or barrier semaphores. Data moves between devices by JAX's collectives and lax.ppermute only.
A program may use at most 64 MiB of HBM per device.

```python
import jax
import jax.numpy as jnp
import numpy as np
from jax import lax

N0 = 128
N1 = 2
N2 = 8
N3 = 4
N4 = 128
STEPS = 4
Q = 64
GRIDS = 4


def touch_ends(values, key, smallest, top_value):
    longest = values.shape.index(max(values.shape))
    spots = []
    for shift in (0, 1):
        where = [jax.random.randint(jax.random.fold_in(key, axis), (), 0, length) for axis, length in enumerate(values.shape)]
        where[longest] = (where[longest] + shift) % values.shape[longest]
        spots.append(tuple(where))
    return values.at[spots[0]].set(smallest).at[spots[1]].set(top_value)


def steps_of(own_key, extent, cuts, low, high):
    def one(axis_at, shards_of):
        steps = jax.random.uniform(jax.random.fold_in(jax.random.fold_in(own_key, 6), axis_at), (shards_of,), jnp.float32, low / len(cuts), high / len(cuts))
        return jnp.repeat(jnp.exp(steps), extent[axis_at] // shards_of).reshape((-1,) + (1,) * (len(extent) - axis_at - 1))

    loudness = one(*cuts[0])
    for cut in cuts[1:]:
        loudness = loudness * one(*cut)
    return loudness


def bell_draw(own_key, dims, width, most, cuts=(), held_as=jnp.bfloat16):
    loudness = steps_of(own_key, dims, cuts, -0.22, 0.18) if cuts else 1.0
    entries = jax.random.normal(own_key, dims, jnp.float32) * width * loudness
    return jnp.minimum(jnp.maximum(entries, -most), most).astype(held_as)


def setup_inputs(seed: int = 0, part: int = 0) -> dict:
    splits = jax.random.split(jax.random.key(seed), 4)
    part_splits = jax.random.split(jax.random.fold_in(splits[3], part), 4)
    return {
        "field": bell_draw(part_splits[0], (GRIDS, N0, Q, N4), 1.0, 6.0, ((0, 4), (1, 4)), jnp.float32),
        "levels": touch_ends(jax.random.randint(part_splits[1], (GRIDS, 5), 1, 4), jax.random.fold_in(part_splits[1], 1), 1, 3).astype(jnp.int32),
        "owner": jax.random.permutation(part_splits[2], N0).astype(jnp.int32),
    }


ADVECT = 0.08
DIFFUSE = 0.03

def build_tables(count):
    depth = count.bit_length() - 1
    matrix = np.eye(count)
    inverse = np.zeros((count, count))
    inverse[0, 0] = 1.0
    level_rows = np.zeros(count, np.int32)
    for index in range(1, count):
        zeros = (index & -index).bit_length() - 1
        spacing = 1 << zeros
        matrix[index, index - spacing] -= 0.5
        matrix[index, (index + spacing) % count] -= 0.5
        level_rows[index] = depth - zeros
    for zeros in range(depth - 1, -1, -1):
        spacing = 1 << zeros
        for index in range(spacing, count, 2 * spacing):
            inverse[index] = 0.5 * (inverse[index - spacing] + inverse[(index + spacing) % count])
            inverse[index, index] += 1.0
    return (matrix.astype(np.float32), inverse.astype(np.float32), level_rows)

def advance_full(state, scales):
    speed = 1.0 + 0.5 * jnp.tanh(state)
    change = jnp.zeros_like(state)
    for axis in range(5):
        back = jnp.roll(state, 1, axis)
        ahead = jnp.roll(state, -1, axis)
        change = change - ADVECT * scales[axis] * speed * (state - back) + DIFFUSE * scales[axis] ** 2 * (ahead - 2.0 * state + back)
    return state + change

def reference(field, levels, owner):
    matrix, inverse, level_rows = build_tables(N0)
    matrix = jnp.asarray(matrix).astype(jnp.float32)
    inverse = jnp.asarray(inverse).astype(jnp.float32)
    level_rows = jnp.asarray(level_rows).astype(jnp.int32)
    depth = N0.bit_length() - 1

    def keep_of(level_vec):
        return (level_rows <= depth - 3 + level_vec[0]).astype(jnp.float32)[:, None, None]

    def grid_terms(inputs):
        state, level_vec = inputs
        scales = jnp.exp2(level_vec.astype(jnp.float32)) / 8.0
        grid5 = state.reshape(N0, N1, N2, N3, N4)
        for step in range(STEPS):
            grid5 = advance_full(grid5, scales)
        hier = jnp.dot(matrix, grid5.reshape(N0, -1), precision=lax.Precision.HIGHEST).reshape(N0, Q, N4)
        weight = jnp.where(jnp.sum(level_vec) % 2 == 0, 1.0, -1.0).astype(jnp.float32) / jnp.sqrt(jnp.float32(GRIDS))
        return weight * keep_of(level_vec) * hier
    sums = lax.optimization_barrier(jnp.sum(lax.map(grid_terms, (field, levels)), axis=0))

    def restart(level_vec):
        masked = (keep_of(level_vec) * sums).reshape(N0, -1)
        return jnp.dot(inverse, masked, precision=lax.Precision.HIGHEST).reshape(N0, Q, N4)
    restarted = lax.map(restart, levels)
    sums = lax.optimization_barrier(jnp.sum(lax.map(grid_terms, (restarted, levels)), axis=0))
    return sums[owner]
```

```python
import functools
import math

import jax
import jax.numpy as jnp
import numpy as np
from jax import lax
from jax.experimental import pallas as pl
from jax.experimental.pallas import tpu as pltpu
from jax.sharding import PartitionSpec as P

N0 = 128
N1 = 2
N2 = 8
N3 = 4
N4 = 128
STEPS = 4
Q = 64

ADVECT = 0.08
DIFFUSE = 0.03

LOW = STEPS
HIGH = STEPS + 1
TILES = N1 * N3


def extended_2(value, sides, width):
    for axis, dim in sides:
        count, length = (lax.axis_size(axis), value.shape[dim])
        up = [(i, (i + 1) % count) for i in range(count)]
        down = [(j, i) for i, j in up]
        last = lax.slice_in_dim(value, length - width, length, axis=dim)
        first = lax.slice_in_dim(value, 0, width, axis=dim)
        before = lax.ppermute(last, axis, up)
        after = lax.ppermute(first, axis, down)
        value = jnp.concatenate([before, value, after], axis=dim)
    return value


def build_tables(count):
    depth = count.bit_length() - 1
    matrix = np.eye(count)
    inverse = np.zeros((count, count))
    inverse[0, 0] = 1.0
    level_rows = np.zeros(count, np.int32)
    for index in range(1, count):
        zeros = (index & -index).bit_length() - 1
        spacing = 1 << zeros
        matrix[index, index - spacing] -= 0.5
        matrix[index, (index + spacing) % count] -= 0.5
        level_rows[index] = depth - zeros
    for zeros in range(depth - 1, -1, -1):
        spacing = 1 << zeros
        for index in range(spacing, count, 2 * spacing):
            inverse[index] = 0.5 * (inverse[index - spacing] + inverse[(index + spacing) % count])
            inverse[index, index] += 1.0
    return (matrix.astype(np.float32), inverse.astype(np.float32), level_rows)


def advance(extended, scales, padded):
    length = extended.shape[padded] - 2
    centre = lax.slice_in_dim(extended, 1, length + 1, axis=padded)
    speed = 1.0 + 0.5 * jnp.tanh(centre)
    change = jnp.zeros_like(centre)
    for axis in range(5):
        if axis == padded:
            back = lax.slice_in_dim(extended, 0, length, axis=padded)
            ahead = lax.slice_in_dim(extended, 2, length + 2, axis=padded)
        else:
            back = jnp.roll(centre, 1, axis)
            ahead = jnp.roll(centre, -1, axis)
        change = (
            change
            - ADVECT * scales[axis] * speed * (centre - back)
            + DIFFUSE * scales[axis] ** 2 * (ahead - 2.0 * centre + back)
        )
    return centre + change


def regroup_rows(stepped):
    return lax.all_to_all(stepped, "slab", split_axis=1, concat_axis=0, tiled=True)


def local_general(field, levels, owner):
    matrix, inverse, level_rows = build_tables(N0)
    matrix = jnp.asarray(matrix)
    inverse = jnp.asarray(inverse)
    depth = N0.bit_length() - 1
    level_vec = levels[0]
    scales = jnp.exp2(level_vec.astype(jnp.float32)) / 8.0
    weight = jnp.where(jnp.sum(level_vec) % 2 == 0, 1.0, -1.0).astype(jnp.float32) / math.sqrt(
        lax.axis_size("grid")
    )
    keep = (jnp.asarray(level_rows) <= depth - 3 + level_vec[0]).astype(jnp.float32)[:, None, None]

    def evolve_rows(state):
        rows = state.shape[0]
        grid5 = state.reshape(rows, N1, N2, N3, N4)
        for step in range(STEPS):
            extended = extended_2(grid5, (("slab", 0),), 1)
            grid5 = advance(extended, scales, 0)
        return grid5.reshape(rows, Q, N4)

    def hierarchise(whole):
        hier = jnp.dot(matrix, whole.reshape(N0, -1), precision=lax.Precision.HIGHEST)
        return weight * keep * hier.reshape(whole.shape)

    def reduce_terms(terms):
        return lax.psum_scatter(terms[owner], "grid", scatter_dimension=0, tiled=True)

    stepped = evolve_rows(field[0])
    summed = reduce_terms(hierarchise(regroup_rows(stepped)))
    ordered = lax.all_gather(summed, "grid", axis=0, tiled=True)
    position = jnp.zeros((N0,), jnp.int32).at[owner].set(jnp.arange(N0, dtype=jnp.int32))
    combined = ordered[position]
    masked = (keep * combined).reshape(N0, -1)
    nodal = jnp.dot(inverse, masked, precision=lax.Precision.HIGHEST).reshape(combined.shape)
    state = lax.all_to_all(nodal, "slab", split_axis=0, concat_axis=1, tiled=True)
    stepped = evolve_rows(state)
    summed = reduce_terms(hierarchise(regroup_rows(stepped)))
    return summed


def step_rows(src, dst, first, groups, unroll, get):
    advect, spread, centre_spread, centre_advect = get

    def body(group, carry):
        base = first + group * unroll
        for offset in range(unroll):
            row = base + offset
            tiles = [src[row, t] for t in range(TILES)]
            for n1 in range(N1):
                for n3 in range(N3):
                    t = n1 * N3 + n3
                    u = tiles[t]
                    neighbours = (
                        (src[row - 1, t], src[row + 1, t]),
                        (tiles[(1 - n1) * N3 + n3], None),
                        (pltpu.roll(u, 1, 0), pltpu.roll(u, N2 - 1, 0)),
                        (tiles[n1 * N3 + (n3 - 1) % N3], tiles[n1 * N3 + (n3 + 1) % N3]),
                        (pltpu.roll(u, 1, 1), pltpu.roll(u, N4 - 1, 1)),
                    )
                    drift = -centre_advect * u
                    update = centre_spread * u
                    for d, (back, ahead) in enumerate(neighbours):
                        drift = drift + advect[d] * back
                        if ahead is None:
                            update = update + (spread[d] + spread[d]) * back
                        else:
                            update = update + spread[d] * (back + ahead)
                    dst[row, t] = update + (2.0 + jnp.tanh(u)) * drift
        return carry

    lax.fori_loop(0, groups, body, 0)


def coefficients(coef, g):
    advect = [coef[g, d] for d in range(5)]
    spread = [coef[g, 5 + d] for d in range(5)]
    return advect, spread, coef[g, 10], coef[g, 11]


def interpolate(nodes, level):
    u0, u1, u2, u3, u4 = nodes
    fine, middle = level >= 3, level >= 2
    v2 = jnp.where(middle, u2, 0.5 * (u0 + u4))
    v1 = jnp.where(fine, u1, 0.5 * (u0 + v2))
    v3 = jnp.where(fine, u3, 0.5 * (v2 + u4))
    return u0, v1, v2, v3


def padded_rows(rows, unroll):
    return rows + LOW + HIGH + unroll


def run_steps(bufs, rows, unroll, get):
    for step in range(STEPS):
        count = rows + LOW + HIGH - 2 * (step + 1)
        step_rows(bufs[step % 2], bufs[(step + 1) % 2], step + 1, -(-count // unroll), unroll, get)
    return bufs[STEPS % 2]


def first_kernel(rows, pieces, unroll, coef, level, order, before, field, after, *rest):
    outs, bufs = rest[:pieces], rest[pieces:]
    start = bufs[0]

    def load(ref, at):
        def body(i, carry):
            for n1 in range(N1):
                for n3 in range(N3):
                    start[at + i, n1 * N3 + n3] = ref[i, pl.ds(n1 * N2 * N3 + n3, N2, stride=N3), :]
            return carry

        lax.fori_loop(0, ref.shape[0], body, 0)

    load(before, 0)
    load(field, LOW)
    load(after, LOW + rows)
    done = run_steps(bufs, rows, unroll, coefficients(coef, 0))
    weight = coef[0, 12]
    piece = rows // pieces
    for j, out in enumerate(outs):
        for quad in range(0, piece, 4):
            base = LOW + order[j] * piece + quad
            for t in range(TILES):
                values = interpolate([done[base + i, t] for i in range(5)], level[0])
                for i, value in enumerate(values):
                    out[quad + i, t] = weight * value


def second_kernel(rows, grids, unroll, coef, level, before, own, after, out, total, wide, *bufs):
    extent = rows + LOW + HIGH
    wide[0:LOW] = before[...]
    wide[LOW : LOW + rows] = own[...]
    wide[LOW + rows : extent] = after[...]
    for g in range(grids):
        start = bufs[0]
        for quad in range(0, extent - 1, 4):
            for t in range(TILES):
                values = interpolate([wide[quad + i, t] for i in range(5)], level[g])
                for i, value in enumerate(values):
                    start[quad + i, t] = value
        start[extent - 1] = wide[extent - 1]
        done = run_steps(bufs, rows, unroll, coefficients(coef, g))
        weight = coef[g, 12]
        for quad in range(0, rows, 4):
            for t in range(TILES):
                values = interpolate([done[LOW + quad + i, t] for i in range(5)], level[g])
                for i, value in enumerate(values):
                    at = pl.ds(((quad + i) * TILES + t) * N2, N2)
                    total[at, :] = weight * value + (total[at, :] if g else 0.0)
    half = N2 // 2
    for n3 in range(N3):
        for n1 in range(N1):
            for n2 in range(N2):
                at = (n3 * N1 + n1) * 2 + n2 // half
                out[at, n2 % half] = total[pl.ds((n1 * N3 + n3) * N2 + n2, rows, stride=TILES * N2), :]


def hier_kernel(groups, matrix, rows, out):
    parts, lanes = rows.shape[1], rows.shape[3]
    for n in range(parts):
        whole = rows[:, n].reshape(matrix.shape[1], lanes)
        hier = jnp.dot(matrix[...], whole, precision=lax.Precision.HIGHEST, preferred_element_type=jnp.float32)
        out[:, n] = hier.reshape(groups, -1, lanes)


def place_kernel(parts, received, out):
    count = received.shape[2]
    for n3 in range(received.shape[0]):
        for n in range(parts):
            q = n * N3 + n3
            out[pl.ds(q, count, stride=parts * N3), :] = received[n3, n]


VMEM = pl.BlockSpec(memory_space=pltpu.VMEM)
SMEM = pl.BlockSpec(memory_space=pltpu.SMEM)


def coefficient_table(levels):
    scales = jnp.exp2(levels.astype(jnp.float32)) / 8.0
    advect = 0.5 * ADVECT * scales
    spread = DIFFUSE * scales**2
    return advect, spread


def table_of(levels, grids):
    advect, spread = coefficient_table(levels)
    weight = jnp.where(jnp.sum(levels, 1) % 2 == 0, 1.0, -1.0).astype(jnp.float32) / math.sqrt(grids)
    centre_spread = 1.0 - 2.0 * jnp.sum(spread, 1)
    centre_advect = jnp.sum(advect, 1)
    return jnp.concatenate(
        [advect, spread, centre_spread[:, None], centre_advect[:, None], weight[:, None]], axis=1
    )


def row_tile(rows):
    return jax.ShapeDtypeStruct((rows, TILES, N2, N4), jnp.float32)


def fast_sizes(grids, slabs):
    rows = N0 // slabs
    block = rows // grids
    return rows, block


def fast_fits(grids, slabs):
    rows, block = fast_sizes(grids, slabs)
    return grids == 4 and grids == N3 and slabs == 2 * N1 and block >= HIGH and block % 4 == 0


def local_fast(field, levels, owner):
    grids, slabs = lax.axis_size("grid"), lax.axis_size("slab")
    rows, block = fast_sizes(grids, slabs)
    me, at = lax.axis_index("grid"), lax.axis_index("slab")
    state = field[0]

    up = [(i, (i + 1) % slabs) for i in range(slabs)]
    down = [(j, i) for i, j in up]
    before = lax.ppermute(state[rows - LOW :], "slab", up)
    after = lax.ppermute(state[:HIGH], "slab", down)

    shift = lambda d: lax.ppermute(levels, "grid", [(i, (i + d) % grids) for i in range(grids)])
    every = jnp.concatenate([levels] + [shift(d) for d in range(1, grids)], axis=0)

    def block_of(g):
        return jnp.where(at % 2 == 0, g, grids - 1 - g)

    low = me < grids // 2
    targets = jnp.stack(
        [
            block_of(jnp.where(low, 3, 0)),
            block_of(jnp.where(low, 2, 1)),
            block_of(jnp.where(low, 1, 2)),
            block_of(jnp.where(low, 0, 3)),
        ]
    ).astype(jnp.int32)

    unroll = 2
    space = lambda r: pltpu.VMEM((padded_rows(r, unroll), TILES, N2, N4), jnp.float32)
    far, middle, near, rear = pl.pallas_call(
        functools.partial(first_kernel, rows, grids, unroll),
        out_shape=[row_tile(block)] * grids,
        in_specs=[SMEM, SMEM, SMEM, VMEM, VMEM, VMEM],
        out_specs=[VMEM] * grids,
        scratch_shapes=[space(rows), space(rows)],
        name="first_cycle",
    )(table_of(levels, grids), levels[:, 0], targets, before, state, after)

    inwards, across, outwards = [(0, 1), (3, 2)], [(1, 2), (2, 1)], [(1, 0), (2, 3)]
    a1 = lax.ppermute(far, "grid", inwards)
    a2 = lax.ppermute(middle, "grid", inwards)
    a3 = lax.ppermute(near, "grid", inwards)
    b1 = lax.ppermute(a1 + far, "grid", across)
    b2 = lax.ppermute(a2 + middle, "grid", across)
    c1 = lax.ppermute(b1 + rear, "grid", outwards)
    inner = (me == 1) | (me == 2)
    own = jnp.where(inner, near + a3 + b2, rear + c1)

    chain = []
    for k in range(slabs):
        chain += [(g if k % 2 == 0 else grids - 1 - g) * slabs + k for g in range(grids)]
    forward = [(chain[i], chain[(i + 1) % len(chain)]) for i in range(len(chain))]
    backward = [(j, i) for i, j in forward]
    both = ("grid", "slab")
    before = lax.ppermute(own[block - LOW :], both, forward)
    after = lax.ppermute(own[:HIGH], both, backward)

    half = N2 // 2
    sent = pl.pallas_call(
        functools.partial(second_kernel, block, grids, unroll),
        out_shape=jax.ShapeDtypeStruct((N3 * N1 * 2, half, block, N4), jnp.float32),
        in_specs=[SMEM, SMEM, VMEM, VMEM, VMEM],
        out_specs=VMEM,
        scratch_shapes=[
            pltpu.VMEM((block * TILES * N2, N4), jnp.float32),
            pltpu.VMEM((block + LOW + HIGH, TILES, N2, N4), jnp.float32),
            space(block),
            space(block),
        ],
        name="second_cycle",
    )(table_of(every, grids), every[:, 0], before, own, after)

    spread = lax.all_to_all(sent, both, split_axis=0, concat_axis=0, tiled=True)

    source = np.zeros(N0, np.int32)
    for place, device in enumerate(chain):
        source[device * block : (device + 1) * block] = place * block + np.arange(block)
    column = jnp.asarray(source)[None, :]
    row = owner[:, None]
    reach = jnp.where(row > 0, row & -row, 0)
    part = jnp.where(row > 0, -0.5, 0.0)
    matrix = (
        (column == row).astype(jnp.float32)
        + part * (column == row - reach)
        + part * (column == (row + reach) % N0)
    )
    group = N0 // grids
    hier = pl.pallas_call(
        functools.partial(hier_kernel, grids),
        out_shape=jax.ShapeDtypeStruct((grids, half, group, N4), jnp.float32),
        in_specs=[VMEM, VMEM],
        out_specs=VMEM,
        name="hierarchise",
    )(matrix, spread)
    received = lax.all_to_all(hier, "grid", split_axis=0, concat_axis=0, tiled=True)
    out = pl.pallas_call(
        functools.partial(place_kernel, half),
        out_shape=jax.ShapeDtypeStruct((group * half * N3, N4), jnp.float32),
        in_specs=[VMEM],
        out_specs=VMEM,
        name="place",
    )(received)
    return out.reshape(group, Q // slabs, N4)


def local(field, levels, owner):
    if fast_fits(lax.axis_size("grid"), lax.axis_size("slab")):
        return local_fast(field, levels, owner)
    return local_general(field, levels, owner)


def solution(mesh):
    in_specs = (P(("copies", "grid"), "slab", None, None), P(("copies", "grid"), None), P("copies"))
    out_specs = P(("copies", "grid"), "slab", None)
    return jax.shard_map(local, mesh=mesh, in_specs=in_specs, out_specs=out_specs, check_vma=False)
```

```python
import functools
import math

import jax
import jax.numpy as jnp
import numpy as np
from jax import lax
from jax.experimental import pallas as pl
from jax.experimental.pallas import tpu as pltpu
from jax.sharding import PartitionSpec as P

N0 = 128
N1 = 2
N2 = 8
N3 = 4
N4 = 128
STEPS = 4
Q = 64

ADVECT = 0.08
DIFFUSE = 0.03

LOW = STEPS
HIGH = STEPS + 1
TILES = N1 * N3


def extended_2(value, sides, width):
    for axis, dim in sides:
        count, length = (lax.axis_size(axis), value.shape[dim])
        up = [(i, (i + 1) % count) for i in range(count)]
        down = [(j, i) for i, j in up]
        last = lax.slice_in_dim(value, length - width, length, axis=dim)
        first = lax.slice_in_dim(value, 0, width, axis=dim)
        before = lax.ppermute(last, axis, up)
        after = lax.ppermute(first, axis, down)
        value = jnp.concatenate([before, value, after], axis=dim)
    return value


def build_tables(count):
    depth = count.bit_length() - 1
    matrix = np.eye(count)
    inverse = np.zeros((count, count))
    inverse[0, 0] = 1.0
    level_rows = np.zeros(count, np.int32)
    for index in range(1, count):
        zeros = (index & -index).bit_length() - 1
        spacing = 1 << zeros
        matrix[index, index - spacing] -= 0.5
        matrix[index, (index + spacing) % count] -= 0.5
        level_rows[index] = depth - zeros
    for zeros in range(depth - 1, -1, -1):
        spacing = 1 << zeros
        for index in range(spacing, count, 2 * spacing):
            inverse[index] = 0.5 * (inverse[index - spacing] + inverse[(index + spacing) % count])
            inverse[index, index] += 1.0
    return (matrix.astype(np.float32), inverse.astype(np.float32), level_rows)


def advance(extended, scales, padded):
    length = extended.shape[padded] - 2
    centre = lax.slice_in_dim(extended, 1, length + 1, axis=padded)
    speed = 1.0 + 0.5 * jnp.tanh(centre)
    change = jnp.zeros_like(centre)
    for axis in range(5):
        if axis == padded:
            back = lax.slice_in_dim(extended, 0, length, axis=padded)
            ahead = lax.slice_in_dim(extended, 2, length + 2, axis=padded)
        else:
            back = jnp.roll(centre, 1, axis)
            ahead = jnp.roll(centre, -1, axis)
        change = (
            change
            - ADVECT * scales[axis] * speed * (centre - back)
            + DIFFUSE * scales[axis] ** 2 * (ahead - 2.0 * centre + back)
        )
    return centre + change


def regroup_rows(stepped):
    return lax.all_to_all(stepped, "slab", split_axis=1, concat_axis=0, tiled=True)


def local_general(field, levels, owner):
    matrix, inverse, level_rows = build_tables(N0)
    matrix = jnp.asarray(matrix)
    inverse = jnp.asarray(inverse)
    depth = N0.bit_length() - 1
    level_vec = levels[0]
    scales = jnp.exp2(level_vec.astype(jnp.float32)) / 8.0
    weight = jnp.where(jnp.sum(level_vec) % 2 == 0, 1.0, -1.0).astype(jnp.float32) / math.sqrt(
        lax.axis_size("grid")
    )
    keep = (jnp.asarray(level_rows) <= depth - 3 + level_vec[0]).astype(jnp.float32)[:, None, None]

    def evolve_rows(state):
        rows = state.shape[0]
        grid5 = state.reshape(rows, N1, N2, N3, N4)
        for step in range(STEPS):
            extended = extended_2(grid5, (("slab", 0),), 1)
            grid5 = advance(extended, scales, 0)
        return grid5.reshape(rows, Q, N4)

    def hierarchise(whole):
        hier = jnp.dot(matrix, whole.reshape(N0, -1), precision=lax.Precision.HIGHEST)
        return weight * keep * hier.reshape(whole.shape)

    def reduce_terms(terms):
        return lax.psum_scatter(terms[owner], "grid", scatter_dimension=0, tiled=True)

    stepped = evolve_rows(field[0])
    summed = reduce_terms(hierarchise(regroup_rows(stepped)))
    ordered = lax.all_gather(summed, "grid", axis=0, tiled=True)
    position = jnp.zeros((N0,), jnp.int32).at[owner].set(jnp.arange(N0, dtype=jnp.int32))
    combined = ordered[position]
    masked = (keep * combined).reshape(N0, -1)
    nodal = jnp.dot(inverse, masked, precision=lax.Precision.HIGHEST).reshape(combined.shape)
    state = lax.all_to_all(nodal, "slab", split_axis=0, concat_axis=1, tiled=True)
    stepped = evolve_rows(state)
    summed = reduce_terms(hierarchise(regroup_rows(stepped)))
    return summed


VMEM = pl.BlockSpec(memory_space=pltpu.VMEM)
SMEM = pl.BlockSpec(memory_space=pltpu.SMEM)
HBM = pl.BlockSpec(memory_space=pltpu.HBM)
UNROLL = 2


def step_rows(src, dst, first, groups, factors):
    advect, spread, centre_spread, centre_advect = factors
    twice = spread[1] + spread[1]

    def body(group, carry):
        base = first + group * UNROLL
        for offset in range(UNROLL):
            row = base + offset
            tiles = [src[row, t] for t in range(TILES)]
            for n1 in range(N1):
                for n3 in range(N3):
                    t = n1 * N3 + n3
                    u = tiles[t]
                    other = tiles[(1 - n1) * N3 + n3]
                    neighbours = (
                        (0, src[row - 1, t], src[row + 1, t]),
                        (2, pltpu.roll(u, 1, 0), pltpu.roll(u, N2 - 1, 0)),
                        (3, tiles[n1 * N3 + (n3 - 1) % N3], tiles[n1 * N3 + (n3 + 1) % N3]),
                        (4, pltpu.roll(u, 1, 1), pltpu.roll(u, N4 - 1, 1)),
                    )
                    drift = advect[1] * other - centre_advect * u
                    update = twice * other + centre_spread * u
                    for d, back, ahead in neighbours:
                        drift = drift + advect[d] * back
                        update = update + spread[d] * (back + ahead)
                    dst[row, t] = update + (2.0 + jnp.tanh(u)) * drift
        return carry

    lax.fori_loop(0, groups, body, 0)


def factors_of(scales):
    advect = [(0.5 * ADVECT) * s for s in scales]
    spread = [DIFFUSE * (s * s) for s in scales]
    total = spread[0]
    for value in spread[1:]:
        total = total + value
    centre = advect[0]
    for value in advect[1:]:
        centre = centre + value
    return advect, spread, 1.0 - 2.0 * total, centre


def interpolate(nodes, fine, middle):
    u0, u1, u2, u3, u4 = nodes
    v2 = jnp.where(middle, u2, 0.5 * (u0 + u4))
    v1 = jnp.where(fine, u1, 0.5 * (u0 + v2))
    v3 = jnp.where(fine, u3, 0.5 * (v2 + u4))
    return u0, v1, v2, v3


def state_space(rows):
    return pltpu.VMEM((rows + LOW + HIGH + UNROLL, TILES, N2, N4), jnp.float32)


def run_steps(bufs, rows, factors):
    for step in range(STEPS):
        count = rows + LOW + HIGH - 2 * (step + 1)
        step_rows(bufs[step % 2], bufs[(step + 1) % 2], step + 1, -(-count // UNROLL), factors)
    return bufs[STEPS % 2]


def ends_kernel(field, last, first, sems):
    rows = field.shape[0]
    one = pltpu.make_async_copy(field.at[pl.ds(rows - LOW, LOW)], last, sems.at[0])
    two = pltpu.make_async_copy(field.at[pl.ds(0, HIGH)], first, sems.at[1])
    one.start()
    two.start()
    one.wait()
    two.wait()


def first_kernel(rows, later, level, before, field, after, outer, inner, *bufs):
    half, start = field.shape[0] // 2, bufs[0]
    me = lax.axis_index("grid")
    upper = lax.rem(me + lax.axis_index("slab") + later, 2) == 0

    def load(ref, first, count, at):
        def body(i, carry):
            for n1 in range(N1):
                for n3 in range(N3):
                    start[at + i, n1 * N3 + n3] = ref[first + i, pl.ds(n1 * N2 * N3 + n3, N2, stride=N3), :]
            return carry

        lax.fori_loop(0, count, body, 0)

    @pl.when(upper)
    def _():
        load(field, half - LOW, half + LOW, 0)
        load(after, 0, HIGH, LOW + half)

    @pl.when(jnp.logical_not(upper))
    def _():
        load(before, 0, LOW, 0)
        load(field, 0, half + HIGH, LOW)

    levels = [level[0, d] for d in range(5)]
    scales = [lax.shift_left(1, v).astype(jnp.float32) * 0.125 for v in levels]
    parity = lax.rem(levels[0] + levels[1] + levels[2] + levels[3] + levels[4], 2)
    weight = (1 - 2 * parity).astype(jnp.float32) * (1.0 / math.sqrt(lax.axis_size("grid")))
    done = run_steps(bufs, half, factors_of(scales))
    fine, middle = levels[0] >= 3, levels[0] >= 2
    block = half // 2
    edge = jnp.where(upper, block, 0)
    for out, first in ((outer, edge), (inner, block - edge)):
        for quad in range(0, block, 4):
            base = LOW + first + quad
            for t in range(TILES):
                values = interpolate([done[base + i, t] for i in range(5)], fine, middle)
                for i, value in enumerate(values):
                    out[(quad + i) * TILES + t] = weight * value
        lane = lax.broadcasted_iota(jnp.int32, (N2, N4), 1)
        tile = jnp.zeros((N2, N4), jnp.float32)
        for d, value in enumerate(scales + [levels[0].astype(jnp.float32), weight]):
            tile = jnp.where(lane == d, value, tile)
        sublane = lax.broadcasted_iota(jnp.int32, (N2, N4), 0)
        out[block * TILES] = jnp.where(sublane == me, tile, 0.0)


def second_kernel(rows, grids, before, own, after, out, total, wide, *bufs):
    extent = rows + LOW + HIGH
    for i in range(LOW * TILES):
        wide[i] = before[i]
    for i in range(rows * TILES):
        wide[LOW * TILES + i] = own[i]
    for i in range(HIGH * TILES):
        wide[(LOW + rows) * TILES + i] = after[i]
    for g in range(grids):
        spread = lambda d: jnp.broadcast_to(own[rows * TILES, g : g + 1, d : d + 1], (N2, N4))
        factors = factors_of([spread(d) for d in range(5)])
        fine, middle, weight = spread(5) > 2.5, spread(5) > 1.5, spread(6)
        start = bufs[0]
        for quad in range(0, extent - 1, 4):
            for t in range(TILES):
                values = interpolate([wide[(quad + i) * TILES + t] for i in range(5)], fine, middle)
                for i, value in enumerate(values):
                    start[quad + i, t] = value
        for t in range(TILES):
            start[extent - 1, t] = wide[(extent - 1) * TILES + t]
        done = run_steps(bufs, rows, factors)
        for quad in range(0, rows, 4):
            for t in range(TILES):
                values = interpolate([done[LOW + quad + i, t] for i in range(5)], fine, middle)
                for i, value in enumerate(values):
                    at = pl.ds(((quad + i) * TILES + t) * N2, N2)
                    total[at, :] = weight * value + (total[at, :] if g else 0.0)
    half = N2 // 2
    for n3 in range(N3):
        for n1 in range(N1):
            for n2 in range(N2):
                at = (n3 * N1 + n1) * 2 + n2 // half
                out[at, n2 % half] = total[pl.ds((n1 * N3 + n3) * N2 + n2, rows, stride=TILES * N2), :]


def hier_kernel(groups, matrix, rows, *outs):
    me = lax.axis_index("grid")
    lanes = rows.shape[3]
    count = matrix.shape[0] // groups
    for n in range(rows.shape[1]):
        whole = rows[:, n].reshape(matrix.shape[1], lanes)
        high = whole.astype(jnp.bfloat16)
        rest = (whole - high.astype(jnp.float32)).astype(jnp.bfloat16)
        for d, out in enumerate(outs):
            part = matrix[pl.ds(lax.rem(me + d, groups) * count, count), :]
            out[n] = jnp.dot(part, high, preferred_element_type=jnp.float32) + jnp.dot(
                part, rest, preferred_element_type=jnp.float32
            )


def place_kernel(groups, *refs):
    received, out = refs[:-1], refs[-1]
    me = lax.axis_index("grid")
    parts, count = received[0].shape[0], received[0].shape[1]
    for d, ref in enumerate(received):
        n3 = lax.rem(me + groups - d, groups)
        for n in range(parts):
            out[pl.ds(n * N3 + n3, count, stride=parts * N3), :] = ref[n]


def kernel(body, name, out_shape, in_specs, scratch=(), limit=4, flops=0):
    single = not isinstance(out_shape, (list, tuple))
    return pl.pallas_call(
        body,
        out_shape=out_shape,
        in_specs=in_specs,
        out_specs=VMEM if single else [VMEM] * len(out_shape),
        scratch_shapes=list(scratch),
        compiler_params=pltpu.CompilerParams(vmem_limit_bytes=limit << 20),
        cost_estimate=pl.CostEstimate(flops=flops, bytes_accessed=1 << 20, transcendentals=flops // 30),
        name=name,
    )


def fast_sizes(grids, slabs):
    rows = N0 // slabs
    return rows, rows // grids


def fast_fits(grids, slabs):
    rows, block = fast_sizes(grids, slabs)
    return grids == 4 and grids == N3 and slabs == 2 * N1 and block >= HIGH and block % 4 == 0


def floats(*shape):
    return jax.ShapeDtypeStruct(shape, jnp.float32)


def local_fast(field, levels, owner):
    grids, slabs = lax.axis_size("grid"), lax.axis_size("slab")
    rows, block = fast_sizes(grids, slabs)
    me = lax.axis_index("grid")
    state = field[0]

    up = [(i, (i + 1) % slabs) for i in range(slabs)]
    down = [(j, i) for i, j in up]
    last, first = kernel(
        ends_kernel,
        "ends",
        [floats(LOW, Q, N4), floats(HIGH, Q, N4)],
        [HBM],
        [pltpu.SemaphoreType.DMA((2,))],
    )(state)
    before = lax.ppermute(last, "slab", up)
    after = lax.ppermute(first, "slab", down)

    piece = floats(block * TILES + 1, N2, N4)

    def half_slab(later):
        return kernel(
            functools.partial(first_kernel, rows, later),
            "first_cycle",
            [piece, piece],
            [SMEM, VMEM, VMEM, VMEM],
            [state_space(rows // 2)] * 2,
            limit=8,
            flops=160 * 8192 * 40,
        )(levels, before, state, after)

    edge = (me == 0) | (me == grids - 1)
    a_outer, a_inner = half_slab(0)
    swapped = lax.ppermute(a_outer, "grid", [(0, 1), (1, 0), (2, 3), (3, 2)])
    b_outer, b_inner = half_slab(1)
    inwards = lax.ppermute(b_inner, "grid", [(0, 1), (3, 2)])
    across = lax.ppermute(b_inner, "grid", [(1, 2), (2, 1)])
    joined = swapped + b_outer
    passed = lax.ppermute(jnp.where(edge, a_inner, joined), "grid", [(0, 2), (3, 1), (1, 3), (2, 0)])
    own = jnp.where(edge, joined, a_inner) + inwards + across + passed

    chain = []
    for k in range(slabs):
        chain += [(g if k % 2 == 0 else grids - 1 - g) * slabs + k for g in range(grids)]
    forward = [(chain[i], chain[(i + 1) % len(chain)]) for i in range(len(chain))]
    backward = [(j, i) for i, j in forward]
    both = ("grid", "slab")
    before = lax.ppermute(own[(block - LOW) * TILES : block * TILES], both, forward)
    after = lax.ppermute(own[: HIGH * TILES], both, backward)

    half = N2 // 2
    sent = kernel(
        functools.partial(second_kernel, block, grids),
        "second_cycle",
        floats(N3 * N1 * 2, half, block, N4),
        [VMEM, VMEM, VMEM],
        [
            pltpu.VMEM((block * TILES * N2, N4), jnp.float32),
            pltpu.VMEM(((block + LOW + HIGH) * TILES, N2, N4), jnp.float32),
            state_space(block),
            state_space(block),
        ],
        limit=8,
        flops=400 * 8192 * 40,
    )(before, own, after)

    spread = lax.all_to_all(sent, both, split_axis=0, concat_axis=0, tiled=True)

    source = np.zeros(N0, np.int32)
    for place, device in enumerate(chain):
        source[device * block : (device + 1) * block] = place * block + np.arange(block)
    column = jnp.asarray(source)[None, :]
    row = owner[:, None]
    reach = jnp.where(row > 0, row & -row, 0)
    part = jnp.where(row > 0, -0.5, 0.0)
    matrix = (
        (column == row).astype(jnp.float32)
        + part * (column == row - reach)
        + part * (column == (row + reach) % N0)
    ).astype(jnp.bfloat16)
    group = N0 // grids
    hier = kernel(
        functools.partial(hier_kernel, grids),
        "hierarchise",
        [floats(half, group, N4)] * grids,
        [VMEM, VMEM],
    )(matrix, spread)
    others = lax.optimization_barrier(tuple(hier[1:]))
    received = [hier[0]] + [
        lax.ppermute(value, "grid", [(i, (i + d) % grids) for i in range(grids)])
        for d, value in enumerate(others, 1)
    ]
    out = kernel(
        functools.partial(place_kernel, grids),
        "place",
        floats(group * half * N3, N4),
        [VMEM] * grids,
    )(*received)
    return out.reshape(group, Q // slabs, N4)


def local(field, levels, owner):
    if fast_fits(lax.axis_size("grid"), lax.axis_size("slab")):
        return local_fast(field, levels, owner)
    return local_general(field, levels, owner)


def solution(mesh):
    in_specs = (P(("copies", "grid"), "slab", None, None), P(("copies", "grid"), None), P("copies"))
    out_specs = P(("copies", "grid"), "slab", None)
    return jax.shard_map(local, mesh=mesh, in_specs=in_specs, out_specs=out_specs, check_vma=False)
```

```python
import functools
import math

import jax
import jax.numpy as jnp
import numpy as np
from jax import lax
from jax.experimental import pallas as pl
from jax.experimental.pallas import tpu as pltpu
from jax.sharding import PartitionSpec as P

N0 = 128
N1 = 2
N2 = 8
N3 = 4
N4 = 128
STEPS = 4
Q = 64

ADVECT = 0.08
DIFFUSE = 0.03

LOW = STEPS
HIGH = STEPS + 1
TILES = N1 * N3


def extended_2(value, sides, width):
    for axis, dim in sides:
        count, length = (lax.axis_size(axis), value.shape[dim])
        up = [(i, (i + 1) % count) for i in range(count)]
        down = [(j, i) for i, j in up]
        last = lax.slice_in_dim(value, length - width, length, axis=dim)
        first = lax.slice_in_dim(value, 0, width, axis=dim)
        before = lax.ppermute(last, axis, up)
        after = lax.ppermute(first, axis, down)
        value = jnp.concatenate([before, value, after], axis=dim)
    return value


def build_tables(count):
    depth = count.bit_length() - 1
    matrix = np.eye(count)
    inverse = np.zeros((count, count))
    inverse[0, 0] = 1.0
    level_rows = np.zeros(count, np.int32)
    for index in range(1, count):
        zeros = (index & -index).bit_length() - 1
        spacing = 1 << zeros
        matrix[index, index - spacing] -= 0.5
        matrix[index, (index + spacing) % count] -= 0.5
        level_rows[index] = depth - zeros
    for zeros in range(depth - 1, -1, -1):
        spacing = 1 << zeros
        for index in range(spacing, count, 2 * spacing):
            inverse[index] = 0.5 * (inverse[index - spacing] + inverse[(index + spacing) % count])
            inverse[index, index] += 1.0
    return (matrix.astype(np.float32), inverse.astype(np.float32), level_rows)


def advance(extended, scales, padded):
    length = extended.shape[padded] - 2
    centre = lax.slice_in_dim(extended, 1, length + 1, axis=padded)
    speed = 1.0 + 0.5 * jnp.tanh(centre)
    change = jnp.zeros_like(centre)
    for axis in range(5):
        if axis == padded:
            back = lax.slice_in_dim(extended, 0, length, axis=padded)
            ahead = lax.slice_in_dim(extended, 2, length + 2, axis=padded)
        else:
            back = jnp.roll(centre, 1, axis)
            ahead = jnp.roll(centre, -1, axis)
        change = (
            change
            - ADVECT * scales[axis] * speed * (centre - back)
            + DIFFUSE * scales[axis] ** 2 * (ahead - 2.0 * centre + back)
        )
    return centre + change


def regroup_rows(stepped):
    return lax.all_to_all(stepped, "slab", split_axis=1, concat_axis=0, tiled=True)


def local_general(field, levels, owner):
    matrix, inverse, level_rows = build_tables(N0)
    matrix = jnp.asarray(matrix)
    inverse = jnp.asarray(inverse)
    depth = N0.bit_length() - 1
    level_vec = levels[0]
    scales = jnp.exp2(level_vec.astype(jnp.float32)) / 8.0
    weight = jnp.where(jnp.sum(level_vec) % 2 == 0, 1.0, -1.0).astype(jnp.float32) / math.sqrt(
        lax.axis_size("grid")
    )
    keep = (jnp.asarray(level_rows) <= depth - 3 + level_vec[0]).astype(jnp.float32)[:, None, None]

    def evolve_rows(state):
        rows = state.shape[0]
        grid5 = state.reshape(rows, N1, N2, N3, N4)
        for step in range(STEPS):
            extended = extended_2(grid5, (("slab", 0),), 1)
            grid5 = advance(extended, scales, 0)
        return grid5.reshape(rows, Q, N4)

    def hierarchise(whole):
        hier = jnp.dot(matrix, whole.reshape(N0, -1), precision=lax.Precision.HIGHEST)
        return weight * keep * hier.reshape(whole.shape)

    def reduce_terms(terms):
        return lax.psum_scatter(terms[owner], "grid", scatter_dimension=0, tiled=True)

    stepped = evolve_rows(field[0])
    summed = reduce_terms(hierarchise(regroup_rows(stepped)))
    ordered = lax.all_gather(summed, "grid", axis=0, tiled=True)
    position = jnp.zeros((N0,), jnp.int32).at[owner].set(jnp.arange(N0, dtype=jnp.int32))
    combined = ordered[position]
    masked = (keep * combined).reshape(N0, -1)
    nodal = jnp.dot(inverse, masked, precision=lax.Precision.HIGHEST).reshape(combined.shape)
    state = lax.all_to_all(nodal, "slab", split_axis=0, concat_axis=1, tiled=True)
    stepped = evolve_rows(state)
    summed = reduce_terms(hierarchise(regroup_rows(stepped)))
    return summed


VMEM = pl.BlockSpec(memory_space=pltpu.VMEM)
SMEM = pl.BlockSpec(memory_space=pltpu.SMEM)
HBM = pl.BlockSpec(memory_space=pltpu.HBM)
UNROLL = 2


def step_rows(src, dst, first, groups, factors):
    advect, spread, centre_spread, centre_advect = factors
    twice = spread[1] + spread[1]

    def body(group, carry):
        base = first + group * UNROLL
        for offset in range(UNROLL):
            row = base + offset
            tiles = [src[row, t] for t in range(TILES)]
            for n1 in range(N1):
                for n3 in range(N3):
                    t = n1 * N3 + n3
                    u = tiles[t]
                    other = tiles[(1 - n1) * N3 + n3]
                    neighbours = (
                        (0, src[row - 1, t], src[row + 1, t]),
                        (2, pltpu.roll(u, 1, 0), pltpu.roll(u, N2 - 1, 0)),
                        (3, tiles[n1 * N3 + (n3 - 1) % N3], tiles[n1 * N3 + (n3 + 1) % N3]),
                        (4, pltpu.roll(u, 1, 1), pltpu.roll(u, N4 - 1, 1)),
                    )
                    drift = advect[1] * other - centre_advect * u
                    update = twice * other + centre_spread * u
                    for d, back, ahead in neighbours:
                        drift = drift + advect[d] * back
                        update = update + spread[d] * (back + ahead)
                    dst[row, t] = update + (2.0 + jnp.tanh(u)) * drift
        return carry

    lax.fori_loop(0, groups, body, 0)


def factors_of(scales):
    advect = [(0.5 * ADVECT) * s for s in scales]
    spread = [DIFFUSE * (s * s) for s in scales]
    total = spread[0]
    for value in spread[1:]:
        total = total + value
    centre = advect[0]
    for value in advect[1:]:
        centre = centre + value
    return advect, spread, 1.0 - 2.0 * total, centre


def interpolate(nodes, fine, middle):
    u0, u1, u2, u3, u4 = nodes
    v2 = jnp.where(middle, u2, 0.5 * (u0 + u4))
    v1 = jnp.where(fine, u1, 0.5 * (u0 + v2))
    v3 = jnp.where(fine, u3, 0.5 * (v2 + u4))
    return u0, v1, v2, v3


def state_space(rows):
    return pltpu.VMEM((rows + LOW + HIGH + UNROLL, TILES, N2, N4), jnp.float32)


def run_steps(bufs, rows, factors):
    for step in range(STEPS):
        count = rows + LOW + HIGH - 2 * (step + 1)
        step_rows(bufs[step % 2], bufs[(step + 1) % 2], step + 1, -(-count // UNROLL), factors)
    return bufs[STEPS % 2]


def ends_kernel(field, last, first, sems):
    rows = field.shape[0]
    one = pltpu.make_async_copy(field.at[pl.ds(rows - LOW, LOW)], last, sems.at[0])
    two = pltpu.make_async_copy(field.at[pl.ds(0, HIGH)], first, sems.at[1])
    one.start()
    two.start()
    one.wait()
    two.wait()


def first_kernel(later, level, before, field, after, one, two, *bufs):
    half, start = field.shape[0] // 2, bufs[0]
    me, grids = lax.axis_index("grid"), lax.axis_size("grid")
    upper = lax.rem(lax.div(2 * me, grids) + lax.axis_index("slab") + later, 2) == 0

    def load(ref, first, count, at):
        def body(i, carry):
            for n1 in range(N1):
                for n3 in range(N3):
                    start[at + i, n1 * N3 + n3] = ref[first + i, pl.ds(n1 * N2 * N3 + n3, N2, stride=N3), :]
            return carry

        lax.fori_loop(0, count, body, 0)

    @pl.when(upper)
    def _():
        load(field, half - LOW, half + LOW, 0)
        load(after, 0, HIGH, LOW + half)

    @pl.when(jnp.logical_not(upper))
    def _():
        load(before, 0, LOW, 0)
        load(field, 0, half + HIGH, LOW)

    levels = [level[0, d] for d in range(5)]
    scales = [lax.shift_left(1, v).astype(jnp.float32) * 0.125 for v in levels]
    parity = lax.rem(levels[0] + levels[1] + levels[2] + levels[3] + levels[4], 2)
    weight = (1 - 2 * parity).astype(jnp.float32) * (1.0 / math.sqrt(lax.axis_size("grid")))
    done = run_steps(bufs, half, factors_of(scales))
    fine, middle = levels[0] >= 3, levels[0] >= 2
    block = half // 2
    ends = jnp.logical_or(me == 0, me == grids - 1)
    at = jnp.where(upper, block, 0)
    if later:
        at = jnp.where(ends, block - at, at)
    for out, first in ((one, at), (two, block - at)):
        for quad in range(0, block, 4):
            base = LOW + first + quad
            for t in range(TILES):
                values = interpolate([done[base + i, t] for i in range(5)], fine, middle)
                for i, value in enumerate(values):
                    out[(quad + i) * TILES + t] = weight * value
        lane = lax.broadcasted_iota(jnp.int32, (N2, N4), 1)
        tile = jnp.zeros((N2, N4), jnp.float32)
        for d, value in enumerate(scales + [levels[0].astype(jnp.float32), weight]):
            tile = jnp.where(lane == d, value, tile)
        sublane = lax.broadcasted_iota(jnp.int32, (N2, N4), 0)
        out[block * TILES] = jnp.where(sublane == me, tile, 0.0)


def second_kernel(rows, grids, before, own, after, out, total, wide, *bufs):
    extent = rows + LOW + HIGH
    for i in range(LOW * TILES):
        wide[i] = before[i]
    for i in range(rows * TILES):
        wide[LOW * TILES + i] = own[i]
    for i in range(HIGH * TILES):
        wide[(LOW + rows) * TILES + i] = after[i]
    for g in range(grids):
        spread = lambda d: jnp.broadcast_to(own[rows * TILES, g : g + 1, d : d + 1], (N2, N4))
        factors = factors_of([spread(d) for d in range(5)])
        fine, middle, weight = spread(5) > 2.5, spread(5) > 1.5, spread(6)
        start = bufs[0]
        for quad in range(0, extent - 1, 4):
            for t in range(TILES):
                values = interpolate([wide[(quad + i) * TILES + t] for i in range(5)], fine, middle)
                for i, value in enumerate(values):
                    start[quad + i, t] = value
        for t in range(TILES):
            start[extent - 1, t] = wide[(extent - 1) * TILES + t]
        done = run_steps(bufs, rows, factors)
        for quad in range(0, rows, 4):
            for t in range(TILES):
                values = interpolate([done[LOW + quad + i, t] for i in range(5)], fine, middle)
                for i, value in enumerate(values):
                    at = pl.ds(((quad + i) * TILES + t) * N2, N2)
                    total[at, :] = weight * value + (total[at, :] if g else 0.0)
    half = N2 // 2
    for n3 in range(N3):
        for n1 in range(N1):
            for n2 in range(N2):
                at = (n3 * N1 + n1) * 2 + n2 // half
                out[at, n2 % half] = total[pl.ds((n1 * N3 + n3) * N2 + n2, rows, stride=TILES * N2), :]


def hier_kernel(groups, matrix, rows, *outs):
    me = lax.axis_index("grid")
    lanes = rows.shape[3]
    count = matrix.shape[0] // groups
    for n in range(rows.shape[1]):
        whole = rows[:, n].reshape(matrix.shape[1], lanes)
        high = whole.astype(jnp.bfloat16)
        rest = (whole - high.astype(jnp.float32)).astype(jnp.bfloat16)
        for d, out in enumerate(outs):
            part = matrix[pl.ds(lax.rem(me + d, groups) * count, count), :]
            out[n] = jnp.dot(part, high, preferred_element_type=jnp.float32) + jnp.dot(
                part, rest, preferred_element_type=jnp.float32
            )


def place_kernel(groups, *refs):
    received, out = refs[:-1], refs[-1]
    me = lax.axis_index("grid")
    parts, count = received[0].shape[0], received[0].shape[1]
    for d, ref in enumerate(received):
        n3 = lax.rem(me + groups - d, groups)
        for n in range(parts):
            out[pl.ds(n * N3 + n3, count, stride=parts * N3), :] = ref[n]


def kernel(body, name, out_shape, in_specs, scratch=(), limit=4, flops=0):
    single = not isinstance(out_shape, (list, tuple))
    return pl.pallas_call(
        body,
        out_shape=out_shape,
        in_specs=in_specs,
        out_specs=VMEM if single else [VMEM] * len(out_shape),
        scratch_shapes=list(scratch),
        compiler_params=pltpu.CompilerParams(vmem_limit_bytes=limit << 20),
        cost_estimate=pl.CostEstimate(flops=flops, bytes_accessed=1 << 20, transcendentals=flops // 30),
        name=name,
    )


def fast_sizes(grids, slabs):
    rows = N0 // slabs
    return rows, rows // grids


def fast_fits(grids, slabs):
    rows, block = fast_sizes(grids, slabs)
    return grids == 4 and grids == N3 and slabs == 2 * N1 and block >= HIGH and block % 4 == 0


def floats(*shape):
    return jax.ShapeDtypeStruct(shape, jnp.float32)


def local_fast(field, levels, owner):
    grids, slabs = lax.axis_size("grid"), lax.axis_size("slab")
    rows, block = fast_sizes(grids, slabs)
    state = field[0]

    up = [(i, (i + 1) % slabs) for i in range(slabs)]
    down = [(j, i) for i, j in up]
    last, first = kernel(
        ends_kernel,
        "ends",
        [floats(LOW, Q, N4), floats(HIGH, Q, N4)],
        [HBM],
        [pltpu.SemaphoreType.DMA((2,))],
    )(state)
    before = lax.ppermute(last, "slab", up)
    after = lax.ppermute(first, "slab", down)

    piece = floats(block * TILES + 1, N2, N4)

    def half_slab(later):
        return kernel(
            functools.partial(first_kernel, later),
            "first_cycle",
            [piece, piece],
            [SMEM, VMEM, VMEM, VMEM],
            [state_space(rows // 2)] * 2,
            limit=8,
            flops=160 * 8192 * 40,
        )(levels, before, state, after)

    far, middle = half_slab(0)
    joined = lax.ppermute(far, "grid", [(0, 1), (3, 2)]) + far
    across = lax.ppermute(middle, "grid", [(1, 2), (2, 1)])
    skipped = lax.ppermute(middle, "grid", [(0, 2), (3, 1)])
    near, own = half_slab(1)
    swapped = lax.ppermute(near, "grid", [(0, 1), (1, 0), (2, 3), (3, 2)])
    passed = lax.ppermute(joined, "grid", [(1, 3), (2, 0)])
    own = own + across + skipped + swapped + passed

    chain = []
    for k in range(slabs):
        chain += [(g if k % 2 == 0 else grids - 1 - g) * slabs + k for g in range(grids)]
    forward = [(chain[i], chain[(i + 1) % len(chain)]) for i in range(len(chain))]
    backward = [(j, i) for i, j in forward]
    both = ("grid", "slab")
    before = lax.ppermute(own[(block - LOW) * TILES : block * TILES], both, forward)
    after = lax.ppermute(own[: HIGH * TILES], both, backward)

    half = N2 // 2
    sent = kernel(
        functools.partial(second_kernel, block, grids),
        "second_cycle",
        floats(N3 * N1 * 2, half, block, N4),
        [VMEM, VMEM, VMEM],
        [
            pltpu.VMEM((block * TILES * N2, N4), jnp.float32),
            pltpu.VMEM(((block + LOW + HIGH) * TILES, N2, N4), jnp.float32),
            state_space(block),
            state_space(block),
        ],
        limit=8,
        flops=400 * 8192 * 40,
    )(before, own, after)

    spread = lax.all_to_all(sent, both, split_axis=0, concat_axis=0, tiled=True)

    source = np.zeros(N0, np.int32)
    for place, device in enumerate(chain):
        source[device * block : (device + 1) * block] = place * block + np.arange(block)
    column = jnp.asarray(source)[None, :]
    row = owner[:, None]
    reach = jnp.where(row > 0, row & -row, 0)
    part = jnp.where(row > 0, -0.5, 0.0)
    matrix = (
        (column == row).astype(jnp.float32)
        + part * (column == row - reach)
        + part * (column == (row + reach) % N0)
    ).astype(jnp.bfloat16)
    group = N0 // grids
    hier = kernel(
        functools.partial(hier_kernel, grids),
        "hierarchise",
        [floats(half, group, N4)] * grids,
        [VMEM, VMEM],
    )(matrix, spread)
    others = lax.optimization_barrier(tuple(hier[1:]))
    received = [hier[0]] + [
        lax.ppermute(value, "grid", [(i, (i + d) % grids) for i in range(grids)])
        for d, value in enumerate(others, 1)
    ]
    out = kernel(
        functools.partial(place_kernel, grids),
        "place",
        floats(group * half * N3, N4),
        [VMEM] * grids,
    )(*received)
    return out.reshape(group, Q // slabs, N4)


def local(field, levels, owner):
    if fast_fits(lax.axis_size("grid"), lax.axis_size("slab")):
        return local_fast(field, levels, owner)
    return local_general(field, levels, owner)


def solution(mesh):
    in_specs = (P(("copies", "grid"), "slab", None, None), P(("copies", "grid"), None), P("copies"))
    out_specs = P(("copies", "grid"), "slab", None)
    return jax.shard_map(local, mesh=mesh, in_specs=in_specs, out_specs=out_specs, check_vma=False)
```

```python
import functools
import math

import jax
import jax.numpy as jnp
import numpy as np
from jax import lax
from jax.experimental import pallas as pl
from jax.experimental.pallas import tpu as pltpu
from jax.sharding import PartitionSpec as P

N0 = 128
N1 = 2
N2 = 8
N3 = 4
N4 = 128
STEPS = 4
Q = 64

ADVECT = 0.08
DIFFUSE = 0.03

LOW = STEPS
HIGH = STEPS + 1
TILES = N1 * N3


def extended_2(value, sides, width):
    for axis, dim in sides:
        count, length = (lax.axis_size(axis), value.shape[dim])
        up = [(i, (i + 1) % count) for i in range(count)]
        down = [(j, i) for i, j in up]
        last = lax.slice_in_dim(value, length - width, length, axis=dim)
        first = lax.slice_in_dim(value, 0, width, axis=dim)
        before = lax.ppermute(last, axis, up)
        after = lax.ppermute(first, axis, down)
        value = jnp.concatenate([before, value, after], axis=dim)
    return value


def build_tables(count):
    depth = count.bit_length() - 1
    matrix = np.eye(count)
    inverse = np.zeros((count, count))
    inverse[0, 0] = 1.0
    level_rows = np.zeros(count, np.int32)
    for index in range(1, count):
        zeros = (index & -index).bit_length() - 1
        spacing = 1 << zeros
        matrix[index, index - spacing] -= 0.5
        matrix[index, (index + spacing) % count] -= 0.5
        level_rows[index] = depth - zeros
    for zeros in range(depth - 1, -1, -1):
        spacing = 1 << zeros
        for index in range(spacing, count, 2 * spacing):
            inverse[index] = 0.5 * (inverse[index - spacing] + inverse[(index + spacing) % count])
            inverse[index, index] += 1.0
    return (matrix.astype(np.float32), inverse.astype(np.float32), level_rows)


def advance(extended, scales, padded):
    length = extended.shape[padded] - 2
    centre = lax.slice_in_dim(extended, 1, length + 1, axis=padded)
    speed = 1.0 + 0.5 * jnp.tanh(centre)
    change = jnp.zeros_like(centre)
    for axis in range(5):
        if axis == padded:
            back = lax.slice_in_dim(extended, 0, length, axis=padded)
            ahead = lax.slice_in_dim(extended, 2, length + 2, axis=padded)
        else:
            back = jnp.roll(centre, 1, axis)
            ahead = jnp.roll(centre, -1, axis)
        change = (
            change
            - ADVECT * scales[axis] * speed * (centre - back)
            + DIFFUSE * scales[axis] ** 2 * (ahead - 2.0 * centre + back)
        )
    return centre + change


def regroup_rows(stepped):
    return lax.all_to_all(stepped, "slab", split_axis=1, concat_axis=0, tiled=True)


def local_general(field, levels, owner):
    matrix, inverse, level_rows = build_tables(N0)
    matrix = jnp.asarray(matrix)
    inverse = jnp.asarray(inverse)
    depth = N0.bit_length() - 1
    level_vec = levels[0]
    scales = jnp.exp2(level_vec.astype(jnp.float32)) / 8.0
    weight = jnp.where(jnp.sum(level_vec) % 2 == 0, 1.0, -1.0).astype(jnp.float32) / math.sqrt(
        lax.axis_size("grid")
    )
    keep = (jnp.asarray(level_rows) <= depth - 3 + level_vec[0]).astype(jnp.float32)[:, None, None]

    def evolve_rows(state):
        rows = state.shape[0]
        grid5 = state.reshape(rows, N1, N2, N3, N4)
        for step in range(STEPS):
            extended = extended_2(grid5, (("slab", 0),), 1)
            grid5 = advance(extended, scales, 0)
        return grid5.reshape(rows, Q, N4)

    def hierarchise(whole):
        hier = jnp.dot(matrix, whole.reshape(N0, -1), precision=lax.Precision.HIGHEST)
        return weight * keep * hier.reshape(whole.shape)

    def reduce_terms(terms):
        return lax.psum_scatter(terms[owner], "grid", scatter_dimension=0, tiled=True)

    stepped = evolve_rows(field[0])
    summed = reduce_terms(hierarchise(regroup_rows(stepped)))
    ordered = lax.all_gather(summed, "grid", axis=0, tiled=True)
    position = jnp.zeros((N0,), jnp.int32).at[owner].set(jnp.arange(N0, dtype=jnp.int32))
    combined = ordered[position]
    masked = (keep * combined).reshape(N0, -1)
    nodal = jnp.dot(inverse, masked, precision=lax.Precision.HIGHEST).reshape(combined.shape)
    state = lax.all_to_all(nodal, "slab", split_axis=0, concat_axis=1, tiled=True)
    stepped = evolve_rows(state)
    summed = reduce_terms(hierarchise(regroup_rows(stepped)))
    return summed


VMEM = pl.BlockSpec(memory_space=pltpu.VMEM)
SMEM = pl.BlockSpec(memory_space=pltpu.SMEM)
HBM = pl.BlockSpec(memory_space=pltpu.HBM)
UNROLL = 2


def stencil(scales):
    size = TILES * N2
    shape = (size, 2 * size)
    row = lax.broadcasted_iota(jnp.int32, shape, 0)
    column = lax.bitwise_and(lax.broadcasted_iota(jnp.int32, shape, 1), size - 1)
    total = sum(scales[1:], scales[0])
    squares = [value * value for value in scales]
    square = sum(squares[1:], squares[0])
    drift = jnp.where(row == column, -total, 0.0)
    second = jnp.where(row == column, -2.0 * square, 0.0)
    for d, unit, count in ((1, N3 * N2, N1), (2, 1, N2), (3, N2, N3)):
        digit = lax.bitwise_and(lax.div(row, unit), count - 1)
        rest = row - digit * unit
        back = column == rest + lax.bitwise_and(digit + count - 1, count - 1) * unit
        ahead = column == rest + lax.bitwise_and(digit + 1, count - 1) * unit
        drift = drift + jnp.where(back, scales[d], 0.0)
        second = second + jnp.where(back, squares[d], 0.0) + jnp.where(ahead, squares[d], 0.0)
    return jnp.concatenate([second, drift], axis=0).astype(jnp.bfloat16)


def step_rows(src, dst, first, groups, matrix, factors, products):
    s0, q0, s4, q4 = factors
    size = TILES * N2

    def multiply(group):
        base = first + group * UNROLL
        value = jnp.concatenate([src[base + i].reshape(size, N4) for i in range(UNROLL)], axis=1)
        high = value.astype(jnp.bfloat16)
        rest = (value - high.astype(jnp.float32)).astype(jnp.bfloat16)
        products[group % 2][...] = jnp.dot(
            matrix[...], jnp.concatenate([high, rest], axis=0), preferred_element_type=jnp.float32
        )

    multiply(0)
    for group in range(groups):
        if group + 1 < groups:
            multiply(group + 1)
        product = products[group % 2]
        for i in range(UNROLL):
            row = first + group * UNROLL + i
            lanes = slice(i * N4, (i + 1) * N4)
            for t in range(TILES):
                u, below, above = src[row, t], src[row - 1, t], src[row + 1, t]
                left, right = pltpu.roll(u, 1, 1), pltpu.roll(u, N4 - 1, 1)
                second = product[t * N2 : (t + 1) * N2, lanes] + q0 * (below + above) + q4 * (left + right)
                drift = product[size + t * N2 : size + (t + 1) * N2, lanes] + s0 * below + s4 * left
                speed = ADVECT + (0.5 * ADVECT) * jnp.tanh(u)
                dst[row, t] = (u + DIFFUSE * second) + speed * drift


def interpolate(nodes, fine, middle):
    u0, u1, u2, u3, u4 = nodes
    v2 = jnp.where(middle, u2, 0.5 * (u0 + u4))
    v1 = jnp.where(fine, u1, 0.5 * (u0 + v2))
    v3 = jnp.where(fine, u3, 0.5 * (v2 + u4))
    return u0, v1, v2, v3


def spaces(rows):
    state = pltpu.VMEM((rows + LOW + HIGH + UNROLL, TILES, N2, N4), jnp.float32)
    size = TILES * N2
    product = pltpu.VMEM((2 * size, UNROLL * N4), jnp.float32)
    return [state, state, product, product, pltpu.VMEM((2 * size, 2 * size), jnp.bfloat16)]


def run_steps(bufs, rows, scales):
    states, products, matrix = bufs[0:2], bufs[2:4], bufs[4]
    matrix[...] = stencil(scales)
    factors = (scales[0], scales[0] * scales[0], scales[4], scales[4] * scales[4])
    for step in range(STEPS):
        count = rows + LOW + HIGH - 2 * (step + 1)
        groups = -(-count // UNROLL)
        step_rows(states[step % 2], states[(step + 1) % 2], step + 1, groups, matrix, factors, products)
    return states[STEPS % 2]


def ends_kernel(field, last, first, sems):
    rows = field.shape[0]
    one = pltpu.make_async_copy(field.at[pl.ds(rows - LOW, LOW)], last, sems.at[0])
    two = pltpu.make_async_copy(field.at[pl.ds(0, HIGH)], first, sems.at[1])
    one.start()
    two.start()
    one.wait()
    two.wait()


def first_kernel(later, level, before, field, after, one, two, *bufs):
    half, start = field.shape[0] // 2, bufs[0]
    me, grids = lax.axis_index("grid"), lax.axis_size("grid")
    upper = lax.rem(lax.div(2 * me, grids) + lax.axis_index("slab") + later, 2) == 0

    def load(ref, first, count, at):
        def body(i, carry):
            for n1 in range(N1):
                for n3 in range(N3):
                    start[at + i, n1 * N3 + n3] = ref[first + i, pl.ds(n1 * N2 * N3 + n3, N2, stride=N3), :]
            return carry

        lax.fori_loop(0, count, body, 0)

    @pl.when(upper)
    def _():
        load(field, half - LOW, half + LOW, 0)
        load(after, 0, HIGH, LOW + half)

    @pl.when(jnp.logical_not(upper))
    def _():
        load(before, 0, LOW, 0)
        load(field, 0, half + HIGH, LOW)

    levels = [level[0, d] for d in range(5)]
    scales = [lax.shift_left(1, v).astype(jnp.float32) * 0.125 for v in levels]
    parity = lax.rem(levels[0] + levels[1] + levels[2] + levels[3] + levels[4], 2)
    weight = (1 - 2 * parity).astype(jnp.float32) * (1.0 / math.sqrt(lax.axis_size("grid")))
    done = run_steps(bufs, half, scales)
    fine, middle = levels[0] >= 3, levels[0] >= 2
    block = half // 2
    ends = jnp.logical_or(me == 0, me == grids - 1)
    at = jnp.where(upper, block, 0)
    if later:
        at = jnp.where(ends, block - at, at)
    for out, first in ((one, at), (two, block - at)):
        for quad in range(0, block, 4):
            base = LOW + first + quad
            for t in range(TILES):
                values = interpolate([done[base + i, t] for i in range(5)], fine, middle)
                for i, value in enumerate(values):
                    out[(quad + i) * TILES + t] = weight * value
        lane = lax.broadcasted_iota(jnp.int32, (N2, N4), 1)
        tile = jnp.zeros((N2, N4), jnp.float32)
        for d, value in enumerate(scales + [levels[0].astype(jnp.float32), weight]):
            tile = jnp.where(lane == d, value, tile)
        sublane = lax.broadcasted_iota(jnp.int32, (N2, N4), 0)
        out[block * TILES] = jnp.where(sublane == me, tile, 0.0)


def second_kernel(rows, grids, before, own, after, out, total, wide, *bufs):
    extent = rows + LOW + HIGH
    for i in range(LOW * TILES):
        wide[i] = before[i]
    for i in range(rows * TILES):
        wide[LOW * TILES + i] = own[i]
    for i in range(HIGH * TILES):
        wide[(LOW + rows) * TILES + i] = after[i]
    total[...] = jnp.zeros_like(total)

    def grid(g, carry):
        spread = lambda d: jnp.broadcast_to(own[rows * TILES, pl.ds(g, 1), d : d + 1], (1, N4))
        scales = [spread(d) for d in range(5)]
        wide_of = lambda value: jnp.broadcast_to(value, (N2, N4))
        fine, middle, weight = wide_of(spread(5)) > 2.5, wide_of(spread(5)) > 1.5, wide_of(spread(6))
        start = bufs[0]
        for quad in range(0, extent - 1, 4):
            for t in range(TILES):
                values = interpolate([wide[(quad + i) * TILES + t] for i in range(5)], fine, middle)
                for i, value in enumerate(values):
                    start[quad + i, t] = value
        for t in range(TILES):
            start[extent - 1, t] = wide[(extent - 1) * TILES + t]
        done = run_steps(bufs, rows, scales)
        for quad in range(0, rows, 4):
            for t in range(TILES):
                values = interpolate([done[LOW + quad + i, t] for i in range(5)], fine, middle)
                for i, value in enumerate(values):
                    at = pl.ds(((quad + i) * TILES + t) * N2, N2)
                    total[at, :] = weight * value + total[at, :]
        return carry

    lax.fori_loop(0, grids, grid, 0)
    half = N2 // 2
    for n3 in range(N3):
        for n1 in range(N1):
            for n2 in range(N2):
                at = (n3 * N1 + n1) * 2 + n2 // half
                out[at, n2 % half] = total[pl.ds((n1 * N3 + n3) * N2 + n2, rows, stride=TILES * N2), :]


def hier_kernel(groups, matrix, rows, *outs):
    me = lax.axis_index("grid")
    lanes = rows.shape[3]
    count = matrix.shape[0] // groups
    for n in range(rows.shape[1]):
        whole = rows[:, n].reshape(matrix.shape[1], lanes)
        high = whole.astype(jnp.bfloat16)
        rest = (whole - high.astype(jnp.float32)).astype(jnp.bfloat16)
        for d, out in enumerate(outs):
            part = matrix[pl.ds(lax.rem(me + d, groups) * count, count), :]
            out[n] = jnp.dot(part, high, preferred_element_type=jnp.float32) + jnp.dot(
                part, rest, preferred_element_type=jnp.float32
            )


def place_kernel(groups, *refs):
    received, out = refs[:-1], refs[-1]
    me = lax.axis_index("grid")
    parts, count = received[0].shape[0], received[0].shape[1]
    for d, ref in enumerate(received):
        n3 = lax.rem(me + groups - d, groups)
        for n in range(parts):
            out[pl.ds(n * N3 + n3, count, stride=parts * N3), :] = ref[n]


def kernel(body, name, out_shape, in_specs, scratch=(), limit=4, flops=0):
    single = not isinstance(out_shape, (list, tuple))
    return pl.pallas_call(
        body,
        out_shape=out_shape,
        in_specs=in_specs,
        out_specs=VMEM if single else [VMEM] * len(out_shape),
        scratch_shapes=list(scratch),
        compiler_params=pltpu.CompilerParams(vmem_limit_bytes=limit << 20),
        cost_estimate=pl.CostEstimate(flops=flops, bytes_accessed=1 << 20, transcendentals=flops // 30),
        name=name,
    )


def fast_sizes(grids, slabs):
    rows = N0 // slabs
    return rows, rows // grids


def fast_fits(grids, slabs):
    rows, block = fast_sizes(grids, slabs)
    return grids == 4 and grids == N3 and slabs == 2 * N1 and block >= HIGH and block % 4 == 0


def floats(*shape):
    return jax.ShapeDtypeStruct(shape, jnp.float32)


def local_fast(field, levels, owner):
    grids, slabs = lax.axis_size("grid"), lax.axis_size("slab")
    rows, block = fast_sizes(grids, slabs)
    state = field[0]

    up = [(i, (i + 1) % slabs) for i in range(slabs)]
    down = [(j, i) for i, j in up]
    last, first = kernel(
        ends_kernel,
        "ends",
        [floats(LOW, Q, N4), floats(HIGH, Q, N4)],
        [HBM],
        [pltpu.SemaphoreType.DMA((2,))],
    )(state)
    before = lax.ppermute(last, "slab", up)
    after = lax.ppermute(first, "slab", down)

    piece = floats(block * TILES + 1, N2, N4)

    def half_slab(later):
        return kernel(
            functools.partial(first_kernel, later),
            "first_cycle",
            [piece, piece],
            [SMEM, VMEM, VMEM, VMEM],
            spaces(rows // 2),
            limit=8,
            flops=160 * 8192 * 40,
        )(levels, before, state, after)

    far, middle = half_slab(0)
    joined = lax.ppermute(far, "grid", [(0, 1), (3, 2)]) + far
    across = lax.ppermute(middle, "grid", [(1, 2), (2, 1)])
    skipped = lax.ppermute(middle, "grid", [(0, 2), (3, 1)])
    near, own = half_slab(1)
    swapped = lax.ppermute(near, "grid", [(0, 1), (1, 0), (2, 3), (3, 2)])
    passed = lax.ppermute(joined, "grid", [(1, 3), (2, 0)])
    own = own + across + skipped + swapped + passed

    chain = []
    for k in range(slabs):
        chain += [(g if k % 2 == 0 else grids - 1 - g) * slabs + k for g in range(grids)]
    forward = [(chain[i], chain[(i + 1) % len(chain)]) for i in range(len(chain))]
    backward = [(j, i) for i, j in forward]
    both = ("grid", "slab")
    before = lax.ppermute(own[(block - LOW) * TILES : block * TILES], both, forward)
    after = lax.ppermute(own[: HIGH * TILES], both, backward)

    half = N2 // 2
    sent = kernel(
        functools.partial(second_kernel, block, grids),
        "second_cycle",
        floats(N3 * N1 * 2, half, block, N4),
        [VMEM, VMEM, VMEM],
        [
            pltpu.VMEM((block * TILES * N2, N4), jnp.float32),
            pltpu.VMEM(((block + LOW + HIGH) * TILES, N2, N4), jnp.float32),
        ]
        + spaces(block),
        limit=8,
        flops=400 * 8192 * 40,
    )(before, own, after)

    spread = lax.all_to_all(sent, both, split_axis=0, concat_axis=0, tiled=True)

    source = np.zeros(N0, np.int32)
    for place, device in enumerate(chain):
        source[device * block : (device + 1) * block] = place * block + np.arange(block)
    column = jnp.asarray(source)[None, :]
    row = owner[:, None]
    reach = jnp.where(row > 0, row & -row, 0)
    part = jnp.where(row > 0, -0.5, 0.0)
    matrix = (
        (column == row).astype(jnp.float32)
        + part * (column == row - reach)
        + part * (column == (row + reach) % N0)
    ).astype(jnp.bfloat16)
    group = N0 // grids
    hier = kernel(
        functools.partial(hier_kernel, grids),
        "hierarchise",
        [floats(half, group, N4)] * grids,
        [VMEM, VMEM],
    )(matrix, spread)
    others = lax.optimization_barrier(tuple(hier[1:]))
    received = [hier[0]] + [
        lax.ppermute(value, "grid", [(i, (i + d) % grids) for i in range(grids)])
        for d, value in enumerate(others, 1)
    ]
    out = kernel(
        functools.partial(place_kernel, grids),
        "place",
        floats(group * half * N3, N4),
        [VMEM] * grids,
    )(*received)
    return out.reshape(group, Q // slabs, N4)


def local(field, levels, owner):
    if fast_fits(lax.axis_size("grid"), lax.axis_size("slab")):
        return local_fast(field, levels, owner)
    return local_general(field, levels, owner)


def solution(mesh):
    in_specs = (P(("copies", "grid"), "slab", None, None), P(("copies", "grid"), None), P("copies"))
    out_specs = P(("copies", "grid"), "slab", None)
    return jax.shard_map(local, mesh=mesh, in_specs=in_specs, out_specs=out_specs, check_vma=False)
```

```python
import functools
import math

import jax
import jax.numpy as jnp
import numpy as np
from jax import lax
from jax.experimental import pallas as pl
from jax.experimental.pallas import tpu as pltpu
from jax.sharding import PartitionSpec as P


N0 = 128
N1 = 2
N2 = 8
N3 = 4
N4 = 128
STEPS = 4
Q = 64

ADVECT = 0.08
DIFFUSE = 0.03

LOW = STEPS
HIGH = STEPS + 1
TILES = N1 * N3


def extended_2(value, sides, width):
    for axis, dim in sides:
        count, length = (lax.axis_size(axis), value.shape[dim])
        up = [(i, (i + 1) % count) for i in range(count)]
        down = [(j, i) for i, j in up]
        last = lax.slice_in_dim(value, length - width, length, axis=dim)
        first = lax.slice_in_dim(value, 0, width, axis=dim)
        before = lax.ppermute(last, axis, up)
        after = lax.ppermute(first, axis, down)
        value = jnp.concatenate([before, value, after], axis=dim)
    return value


def build_tables(count):
    depth = count.bit_length() - 1
    matrix = np.eye(count)
    inverse = np.zeros((count, count))
    inverse[0, 0] = 1.0
    level_rows = np.zeros(count, np.int32)
    for index in range(1, count):
        zeros = (index & -index).bit_length() - 1
        spacing = 1 << zeros
        matrix[index, index - spacing] -= 0.5
        matrix[index, (index + spacing) % count] -= 0.5
        level_rows[index] = depth - zeros
    for zeros in range(depth - 1, -1, -1):
        spacing = 1 << zeros
        for index in range(spacing, count, 2 * spacing):
            inverse[index] = 0.5 * (inverse[index - spacing] + inverse[(index + spacing) % count])
            inverse[index, index] += 1.0
    return (matrix.astype(np.float32), inverse.astype(np.float32), level_rows)


def advance(extended, scales, padded):
    length = extended.shape[padded] - 2
    centre = lax.slice_in_dim(extended, 1, length + 1, axis=padded)
    speed = 1.0 + 0.5 * jnp.tanh(centre)
    change = jnp.zeros_like(centre)
    for axis in range(5):
        if axis == padded:
            back = lax.slice_in_dim(extended, 0, length, axis=padded)
            ahead = lax.slice_in_dim(extended, 2, length + 2, axis=padded)
        else:
            back = jnp.roll(centre, 1, axis)
            ahead = jnp.roll(centre, -1, axis)
        change = (
            change
            - ADVECT * scales[axis] * speed * (centre - back)
            + DIFFUSE * scales[axis] ** 2 * (ahead - 2.0 * centre + back)
        )
    return centre + change


def regroup_rows(stepped):
    return lax.all_to_all(stepped, "slab", split_axis=1, concat_axis=0, tiled=True)


def local_general(field, levels, owner):
    matrix, inverse, level_rows = build_tables(N0)
    matrix = jnp.asarray(matrix)
    inverse = jnp.asarray(inverse)
    depth = N0.bit_length() - 1
    level_vec = levels[0]
    scales = jnp.exp2(level_vec.astype(jnp.float32)) / 8.0
    weight = jnp.where(jnp.sum(level_vec) % 2 == 0, 1.0, -1.0).astype(jnp.float32) / math.sqrt(
        lax.axis_size("grid")
    )
    keep = (jnp.asarray(level_rows) <= depth - 3 + level_vec[0]).astype(jnp.float32)[:, None, None]

    def evolve_rows(state):
        rows = state.shape[0]
        grid5 = state.reshape(rows, N1, N2, N3, N4)
        for _ in range(STEPS):
            extended = extended_2(grid5, (("slab", 0),), 1)
            grid5 = advance(extended, scales, 0)
        return grid5.reshape(rows, Q, N4)

    def hierarchise(whole):
        hier = jnp.dot(matrix, whole.reshape(N0, -1), precision=lax.Precision.HIGHEST)
        return weight * keep * hier.reshape(whole.shape)

    def reduce_terms(terms):
        return lax.psum_scatter(terms[owner], "grid", scatter_dimension=0, tiled=True)

    stepped = evolve_rows(field[0])
    summed = reduce_terms(hierarchise(regroup_rows(stepped)))
    ordered = lax.all_gather(summed, "grid", axis=0, tiled=True)
    position = jnp.zeros((N0,), jnp.int32).at[owner].set(jnp.arange(N0, dtype=jnp.int32))
    combined = ordered[position]
    masked = (keep * combined).reshape(N0, -1)
    nodal = jnp.dot(inverse, masked, precision=lax.Precision.HIGHEST).reshape(combined.shape)
    state = lax.all_to_all(nodal, "slab", split_axis=0, concat_axis=1, tiled=True)
    stepped = evolve_rows(state)
    summed = reduce_terms(hierarchise(regroup_rows(stepped)))
    return summed


VMEM = pl.BlockSpec(memory_space=pltpu.VMEM)
SMEM = pl.BlockSpec(memory_space=pltpu.SMEM)
HBM = pl.BlockSpec(memory_space=pltpu.HBM)
UNROLL = 2


def stencil(scales):
    size = TILES * N2
    shape = (size, 2 * size)
    row = lax.broadcasted_iota(jnp.int32, shape, 0)
    column = lax.bitwise_and(lax.broadcasted_iota(jnp.int32, shape, 1), size - 1)
    total = sum(scales[1:], scales[0])
    squares = [value * value for value in scales]
    square = sum(squares[1:], squares[0])
    drift = jnp.where(row == column, -total, 0.0)
    second = jnp.where(row == column, -2.0 * square, 0.0)
    for d, unit, count in ((1, N3 * N2, N1), (2, 1, N2), (3, N2, N3)):
        digit = lax.bitwise_and(lax.div(row, unit), count - 1)
        rest = row - digit * unit
        back = column == rest + lax.bitwise_and(digit + count - 1, count - 1) * unit
        ahead = column == rest + lax.bitwise_and(digit + 1, count - 1) * unit
        drift = drift + jnp.where(back, scales[d], 0.0)
        second = second + jnp.where(back, squares[d], 0.0) + jnp.where(ahead, squares[d], 0.0)
    return jnp.concatenate([second, drift], axis=0).astype(jnp.bfloat16)


def step_rows(src, dst, first, count, matrix, factors, products):
    s0, q0, s4, q4 = factors
    size = TILES * N2

    def rows_of(group):
        return range(first + group * UNROLL, first + min(count, (group + 1) * UNROLL))

    def multiply(group):
        value = jnp.concatenate([src[row].reshape(size, N4) for row in rows_of(group)], axis=1)
        high = value.astype(jnp.bfloat16)
        rest = (value - high.astype(jnp.float32)).astype(jnp.bfloat16)
        products[group % 2][:, : value.shape[1]] = jnp.dot(
            matrix[...], jnp.concatenate([high, rest], axis=0), preferred_element_type=jnp.float32
        )

    groups = -(-count // UNROLL)
    multiply(0)
    for group in range(groups):
        if group + 1 < groups:
            multiply(group + 1)
        product = products[group % 2]
        for i, row in enumerate(rows_of(group)):
            lanes = slice(i * N4, (i + 1) * N4)
            for t in range(TILES):
                u, below, above = src[row, t], src[row - 1, t], src[row + 1, t]
                left, right = pltpu.roll(u, 1, 1), pltpu.roll(u, N4 - 1, 1)
                second = product[t * N2 : (t + 1) * N2, lanes] + q0 * (below + above) + q4 * (left + right)
                drift = product[size + t * N2 : size + (t + 1) * N2, lanes] + s0 * below + s4 * left
                speed = ADVECT + (0.5 * ADVECT) * jnp.tanh(u)
                dst[row, t] = (u + DIFFUSE * second) + speed * drift


def interpolate(nodes, fine, middle):
    u0, u1, u2, u3, u4 = nodes
    v2 = jnp.where(middle, u2, 0.5 * (u0 + u4))
    v1 = jnp.where(fine, u1, 0.5 * (u0 + v2))
    v3 = jnp.where(fine, u3, 0.5 * (v2 + u4))
    return u0, v1, v2, v3


def spaces(rows):
    state = pltpu.VMEM((rows + LOW + HIGH, TILES, N2, N4), jnp.float32)
    size = TILES * N2
    product = pltpu.VMEM((2 * size, UNROLL * N4), jnp.float32)
    return [state, state, product, product, pltpu.VMEM((2 * size, 2 * size), jnp.bfloat16)]


def run_steps(bufs, rows, scales):
    states, products, matrix = bufs[0:2], bufs[2:4], bufs[4]
    matrix[...] = stencil(scales)
    factors = (scales[0], scales[0] * scales[0], scales[4], scales[4] * scales[4])
    for step in range(STEPS):
        count = rows + LOW + HIGH - 2 * (step + 1)
        step_rows(states[step % 2], states[(step + 1) % 2], step + 1, count, matrix, factors, products)
    return states[STEPS % 2]


def ends_kernel(field, last, first, sems):
    rows = field.shape[0]
    one = pltpu.make_async_copy(field.at[pl.ds(rows - LOW, LOW)], last, sems.at[0])
    two = pltpu.make_async_copy(field.at[pl.ds(0, HIGH)], first, sems.at[1])
    one.start()
    two.start()
    one.wait()
    two.wait()


def load_rows(ref, first, count, state, at):
    def body(i, carry):
        for n1 in range(N1):
            for n3 in range(N3):
                state[at + i, n1 * N3 + n3] = ref[first + i, pl.ds(n1 * N2 * N3 + n3, N2, stride=N3), :]
        return carry

    lax.fori_loop(0, count, body, 0)


def first_cycle(level, rows, outs, bufs):
    me, grids = lax.axis_index("grid"), lax.axis_size("grid")
    levels = [level[0, d] for d in range(5)]
    scales = [lax.shift_left(1, v).astype(jnp.float32) * 0.125 for v in levels]
    parity = lax.rem(levels[0] + levels[1] + levels[2] + levels[3] + levels[4], 2)
    weight = (1 - 2 * parity).astype(jnp.float32) * (1.0 / math.sqrt(grids))
    done = run_steps(bufs, rows, scales)
    fine, middle = levels[0] >= 3, levels[0] >= 2
    block = outs[0][1].shape[0] // TILES
    for first, out in outs:
        for quad in range(0, block, 4):
            base = LOW + first + quad
            for t in range(TILES):
                values = interpolate([done[base + i, t] for i in range(5)], fine, middle)
                for i, value in enumerate(values):
                    out[(quad + i) * TILES + t] = weight * value
        lane = lax.broadcasted_iota(jnp.int32, (N2, N4), 1)
        tile = jnp.zeros((N2, N4), jnp.float32)
        for d, value in enumerate(scales + [levels[0].astype(jnp.float32), weight]):
            tile = jnp.where(lane == d, value, tile)
        sublane = lax.broadcasted_iota(jnp.int32, (N2, N4), 0)
        out[block * TILES] = jnp.where(sublane == me, tile, 0.0)


def middle_kernel(level, field, middle, near, *bufs):
    rows = field.shape[0] // 2
    block = rows // 2
    load_rows(field, block - LOW, rows + LOW + HIGH, bufs[0], 0)
    side = lax.div(2 * lax.axis_index("grid"), lax.axis_size("grid"))
    upper = lax.rem(side + lax.axis_index("slab"), 2) == 0
    first = jnp.where(upper, block, 0)
    first_cycle(level, rows, ((first, middle), (block - first, near)), bufs)


def outer_kernel(later, level, before, field, after, out, *bufs):
    total = field.shape[0]
    block = out.shape[0] // TILES
    top = lax.rem(lax.axis_index("grid") + lax.axis_index("slab") + later, 2) == 0

    @pl.when(top)
    def _():
        load_rows(field, total - block - LOW, block + LOW, bufs[0], 0)
        load_rows(after, 0, HIGH, bufs[0], block + LOW)

    @pl.when(jnp.logical_not(top))
    def _():
        load_rows(before, 0, LOW, bufs[0], 0)
        load_rows(field, 0, block + HIGH, bufs[0], LOW)

    first_cycle(level, block, ((0, out),), bufs)


def second_kernel(rows, grids, before, own, after, out, total, wide, *bufs):
    extent = rows + LOW + HIGH
    for i in range(LOW * TILES):
        wide[i] = before[i]
    for i in range(rows * TILES):
        wide[LOW * TILES + i] = own[i]
    for i in range(HIGH * TILES):
        wide[(LOW + rows) * TILES + i] = after[i]
    total[...] = jnp.zeros_like(total)

    def grid(g, carry):
        spread = lambda d: jnp.broadcast_to(own[rows * TILES, pl.ds(g, 1), d : d + 1], (1, N4))
        scales = [spread(d) for d in range(5)]
        wide_of = lambda value: jnp.broadcast_to(value, (N2, N4))
        fine, middle, weight = wide_of(spread(5)) > 2.5, wide_of(spread(5)) > 1.5, wide_of(spread(6))
        start = bufs[0]
        for quad in range(0, extent - 1, 4):
            for t in range(TILES):
                values = interpolate([wide[(quad + i) * TILES + t] for i in range(5)], fine, middle)
                for i, value in enumerate(values):
                    start[quad + i, t] = value
        for t in range(TILES):
            start[extent - 1, t] = wide[(extent - 1) * TILES + t]
        done = run_steps(bufs, rows, scales)
        for quad in range(0, rows, 4):
            for t in range(TILES):
                values = interpolate([done[LOW + quad + i, t] for i in range(5)], fine, middle)
                for i, value in enumerate(values):
                    at = pl.ds(((quad + i) * TILES + t) * N2, N2)
                    total[at, :] = weight * value + total[at, :]
        return carry

    lax.fori_loop(0, grids, grid, 0)
    half = N2 // 2
    for n3 in range(N3):
        for n1 in range(N1):
            for n2 in range(N2):
                at = (n3 * N1 + n1) * 2 + n2 // half
                out[at, n2 % half] = total[pl.ds((n1 * N3 + n3) * N2 + n2, rows, stride=TILES * N2), :]


def hier_kernel(groups, matrix, rows, *outs):
    me = lax.axis_index("grid")
    lanes = rows.shape[3]
    count = matrix.shape[0] // groups
    for n in range(rows.shape[1]):
        whole = rows[:, n].reshape(matrix.shape[1], lanes)
        high = whole.astype(jnp.bfloat16)
        rest = (whole - high.astype(jnp.float32)).astype(jnp.bfloat16)
        for d, out in enumerate(outs):
            part = matrix[pl.ds(lax.rem(me + d, groups) * count, count), :]
            out[n] = jnp.dot(part, high, preferred_element_type=jnp.float32) + jnp.dot(
                part, rest, preferred_element_type=jnp.float32
            )


def place_kernel(groups, *refs):
    received, out = refs[:-1], refs[-1]
    me = lax.axis_index("grid")
    parts, count = received[0].shape[0], received[0].shape[1]
    for d, ref in enumerate(received):
        n3 = lax.rem(me + groups - d, groups)
        for n in range(parts):
            out[pl.ds(n * N3 + n3, count, stride=parts * N3), :] = ref[n]


def kernel(body, out_shape, in_specs, scratch=(), limit=4, flops=0):
    single = not isinstance(out_shape, (list, tuple))
    return pl.pallas_call(
        body,
        out_shape=out_shape,
        in_specs=in_specs,
        out_specs=VMEM if single else [VMEM] * len(out_shape),
        scratch_shapes=list(scratch),
        compiler_params=pltpu.CompilerParams(vmem_limit_bytes=limit << 20),
        cost_estimate=pl.CostEstimate(flops=flops, bytes_accessed=1 << 20, transcendentals=flops // 30),
    )


def fast_sizes(grids, slabs):
    rows = N0 // slabs
    return rows, rows // grids


def fast_fits(grids, slabs):
    _, block = fast_sizes(grids, slabs)
    return grids == 4 and grids == N3 and slabs == 2 * N1 and block >= HIGH and block % 4 == 0


def floats(*shape):
    return jax.ShapeDtypeStruct(shape, jnp.float32)


def local_fast(field, levels, owner):
    grids, slabs = lax.axis_size("grid"), lax.axis_size("slab")
    rows, block = fast_sizes(grids, slabs)
    state = field[0]

    up = [(i, (i + 1) % slabs) for i in range(slabs)]
    down = [(j, i) for i, j in up]
    last, first = kernel(
        ends_kernel,
        [floats(LOW, Q, N4), floats(HIGH, Q, N4)],
        [HBM],
        [pltpu.SemaphoreType.DMA((2,))],
    )(pltpu.with_memory_space_constraint(state, pltpu.HBM))
    before = lax.ppermute(last, "slab", up)
    after = lax.ppermute(first, "slab", down)

    piece = floats(block * TILES + 1, N2, N4)
    work = 8192 * 40
    middle, near = kernel(
        middle_kernel, [piece, piece], [SMEM, VMEM], spaces(rows // 2), limit=6, flops=80 * work
    )(levels, state)

    ready = lax.optimization_barrier((before, after, middle))

    def outer_block(later):
        return kernel(
            functools.partial(outer_kernel, later),
            piece,
            [SMEM, VMEM, VMEM, VMEM],
            spaces(block),
            limit=6,
            flops=48 * work,
        )(levels, ready[0], state, ready[1])

    edge = (lax.axis_index("grid") == 0) | (lax.axis_index("grid") == grids - 1)
    across = lax.ppermute(middle, "grid", [(1, 2), (2, 1)])
    first_out = outer_block(0)
    swapped = lax.ppermute(first_out, "grid", [(0, 1), (1, 0), (2, 3), (3, 2)])
    middle, near, _ = lax.optimization_barrier((middle, near, first_out))
    skipped = lax.ppermute(middle, "grid", [(0, 2), (3, 1)])
    inwards = lax.ppermute(near, "grid", [(0, 1), (3, 2)])
    second_out = outer_block(1)
    joined = swapped + second_out
    passed = lax.ppermute(joined, "grid", [(1, 3), (2, 0)])
    own = jnp.where(edge, joined, near) + across + skipped + inwards + passed

    chain = []
    for k in range(slabs):
        chain += [(g if k % 2 == 0 else grids - 1 - g) * slabs + k for g in range(grids)]
    forward = [(chain[i], chain[(i + 1) % len(chain)]) for i in range(len(chain))]
    backward = [(j, i) for i, j in forward]
    both = ("grid", "slab")
    before = lax.ppermute(own[(block - LOW) * TILES : block * TILES], both, forward)
    after = lax.ppermute(own[: HIGH * TILES], both, backward)

    half = N2 // 2
    sent = kernel(
        functools.partial(second_kernel, block, grids),
        floats(N3 * N1 * 2, half, block, N4),
        [VMEM, VMEM, VMEM],
        [
            pltpu.VMEM((block * TILES * N2, N4), jnp.float32),
            pltpu.VMEM(((block + LOW + HIGH) * TILES, N2, N4), jnp.float32),
        ]
        + spaces(block),
        limit=8,
        flops=400 * 8192 * 40,
    )(before, own, after)

    spread = lax.all_to_all(sent, both, split_axis=0, concat_axis=0, tiled=True)

    source = np.zeros(N0, np.int32)
    for place, device in enumerate(chain):
        source[device * block : (device + 1) * block] = place * block + np.arange(block)
    column = jnp.asarray(source)[None, :]
    row = owner[:, None]
    reach = jnp.where(row > 0, row & -row, 0)
    part = jnp.where(row > 0, -0.5, 0.0)
    matrix = (
        (column == row).astype(jnp.float32)
        + part * (column == row - reach)
        + part * (column == (row + reach) % N0)
    ).astype(jnp.bfloat16)
    group = N0 // grids
    hier = kernel(
        functools.partial(hier_kernel, grids), [floats(half, group, N4)] * grids, [VMEM, VMEM]
    )(matrix, spread)
    others = lax.optimization_barrier(tuple(hier[1:]))
    received = [hier[0]] + [
        lax.ppermute(value, "grid", [(i, (i + d) % grids) for i in range(grids)])
        for d, value in enumerate(others, 1)
    ]
    out = kernel(
        functools.partial(place_kernel, grids), floats(group * half * N3, N4), [VMEM] * grids
    )(*received)
    return out.reshape(group, Q // slabs, N4)


def local(field, levels, owner):
    if fast_fits(lax.axis_size("grid"), lax.axis_size("slab")):
        return local_fast(field, levels, owner)
    return local_general(field, levels, owner)


def solution(mesh):
    in_specs = (P(("copies", "grid"), "slab", None, None), P(("copies", "grid"), None), P("copies"))
    out_specs = P(("copies", "grid"), "slab", None)
    return jax.shard_map(local, mesh=mesh, in_specs=in_specs, out_specs=out_specs, check_vma=False)
```

```python
import functools
import math

import jax
import jax.numpy as jnp
import numpy as np
from jax import lax
from jax.experimental import pallas as pl
from jax.experimental.pallas import tpu as pltpu
from jax.sharding import PartitionSpec as P


N0 = 128
N1 = 2
N2 = 8
N3 = 4
N4 = 128
STEPS = 4
Q = 64

ADVECT = 0.08
DIFFUSE = 0.03

LOW = STEPS
HIGH = STEPS + 1
TILES = N1 * N3


def extended_2(value, sides, width):
    for axis, dim in sides:
        count, length = (lax.axis_size(axis), value.shape[dim])
        up = [(i, (i + 1) % count) for i in range(count)]
        down = [(j, i) for i, j in up]
        last = lax.slice_in_dim(value, length - width, length, axis=dim)
        first = lax.slice_in_dim(value, 0, width, axis=dim)
        before = lax.ppermute(last, axis, up)
        after = lax.ppermute(first, axis, down)
        value = jnp.concatenate([before, value, after], axis=dim)
    return value


def build_tables(count):
    depth = count.bit_length() - 1
    matrix = np.eye(count)
    inverse = np.zeros((count, count))
    inverse[0, 0] = 1.0
    level_rows = np.zeros(count, np.int32)
    for index in range(1, count):
        zeros = (index & -index).bit_length() - 1
        spacing = 1 << zeros
        matrix[index, index - spacing] -= 0.5
        matrix[index, (index + spacing) % count] -= 0.5
        level_rows[index] = depth - zeros
    for zeros in range(depth - 1, -1, -1):
        spacing = 1 << zeros
        for index in range(spacing, count, 2 * spacing):
            inverse[index] = 0.5 * (inverse[index - spacing] + inverse[(index + spacing) % count])
            inverse[index, index] += 1.0
    return (matrix.astype(np.float32), inverse.astype(np.float32), level_rows)


def advance(extended, scales, padded):
    length = extended.shape[padded] - 2
    centre = lax.slice_in_dim(extended, 1, length + 1, axis=padded)
    speed = 1.0 + 0.5 * jnp.tanh(centre)
    change = jnp.zeros_like(centre)
    for axis in range(5):
        if axis == padded:
            back = lax.slice_in_dim(extended, 0, length, axis=padded)
            ahead = lax.slice_in_dim(extended, 2, length + 2, axis=padded)
        else:
            back = jnp.roll(centre, 1, axis)
            ahead = jnp.roll(centre, -1, axis)
        change = (
            change
            - ADVECT * scales[axis] * speed * (centre - back)
            + DIFFUSE * scales[axis] ** 2 * (ahead - 2.0 * centre + back)
        )
    return centre + change


def regroup_rows(stepped):
    return lax.all_to_all(stepped, "slab", split_axis=1, concat_axis=0, tiled=True)


def local_general(field, levels, owner):
    matrix, inverse, level_rows = build_tables(N0)
    matrix = jnp.asarray(matrix)
    inverse = jnp.asarray(inverse)
    depth = N0.bit_length() - 1
    level_vec = levels[0]
    scales = jnp.exp2(level_vec.astype(jnp.float32)) / 8.0
    weight = jnp.where(jnp.sum(level_vec) % 2 == 0, 1.0, -1.0).astype(jnp.float32) / math.sqrt(
        lax.axis_size("grid")
    )
    keep = (jnp.asarray(level_rows) <= depth - 3 + level_vec[0]).astype(jnp.float32)[:, None, None]

    def evolve_rows(state):
        rows = state.shape[0]
        grid5 = state.reshape(rows, N1, N2, N3, N4)
        for _ in range(STEPS):
            extended = extended_2(grid5, (("slab", 0),), 1)
            grid5 = advance(extended, scales, 0)
        return grid5.reshape(rows, Q, N4)

    def hierarchise(whole):
        hier = jnp.dot(matrix, whole.reshape(N0, -1), precision=lax.Precision.HIGHEST)
        return weight * keep * hier.reshape(whole.shape)

    def reduce_terms(terms):
        return lax.psum_scatter(terms[owner], "grid", scatter_dimension=0, tiled=True)

    stepped = evolve_rows(field[0])
    summed = reduce_terms(hierarchise(regroup_rows(stepped)))
    ordered = lax.all_gather(summed, "grid", axis=0, tiled=True)
    position = jnp.zeros((N0,), jnp.int32).at[owner].set(jnp.arange(N0, dtype=jnp.int32))
    combined = ordered[position]
    masked = (keep * combined).reshape(N0, -1)
    nodal = jnp.dot(inverse, masked, precision=lax.Precision.HIGHEST).reshape(combined.shape)
    state = lax.all_to_all(nodal, "slab", split_axis=0, concat_axis=1, tiled=True)
    stepped = evolve_rows(state)
    summed = reduce_terms(hierarchise(regroup_rows(stepped)))
    return summed


VMEM = pl.BlockSpec(memory_space=pltpu.VMEM)
SMEM = pl.BlockSpec(memory_space=pltpu.SMEM)
HBM = pl.BlockSpec(memory_space=pltpu.HBM)
UNROLL = 2


def fill_tables(scales, left, right):
    size = TILES * N2
    squares = [value * value for value in scales]
    total = sum(scales[1:], scales[0])
    square = sum(squares[1:], squares[0])

    shape = (size, 2 * size)
    row = lax.broadcasted_iota(jnp.int32, shape, 0)
    column = lax.bitwise_and(lax.broadcasted_iota(jnp.int32, shape, 1), size - 1)
    drift = jnp.where(row == column, -total, 0.0)
    second = jnp.where(row == column, -2.0 * square, 0.0)
    for d, unit, count in ((1, N3 * N2, N1), (2, 1, N2), (3, N2, N3)):
        digit = lax.bitwise_and(lax.div(row, unit), count - 1)
        rest = row - digit * unit
        back = column == rest + lax.bitwise_and(digit + count - 1, count - 1) * unit
        ahead = column == rest + lax.bitwise_and(digit + 1, count - 1) * unit
        drift = drift + jnp.where(back, scales[d], 0.0)
        second = second + jnp.where(back, squares[d], 0.0) + jnp.where(ahead, squares[d], 0.0)
    left[...] = jnp.concatenate([second, drift], axis=0).astype(jnp.bfloat16)

    shape = (N4, N4)
    row = lax.broadcasted_iota(jnp.int32, shape, 0)
    column = lax.broadcasted_iota(jnp.int32, shape, 1)
    back = row == lax.bitwise_and(column + N4 - 1, N4 - 1)
    ahead = row == lax.bitwise_and(column + 1, N4 - 1)
    drift = jnp.where(back, scales[4], 0.0)
    second = jnp.where(back, squares[4], 0.0) + jnp.where(ahead, squares[4], 0.0)
    both = jnp.concatenate([second, drift], axis=1).astype(jnp.bfloat16)
    right[...] = jnp.concatenate([both, both], axis=0)


def step_rows(src, dst, first, count, tables, factors, products):
    left, right = tables
    s0, q0 = factors
    size = TILES * N2

    def rows_of(group):
        return range(first + group * UNROLL, first + min(count, (group + 1) * UNROLL))

    def multiply(group):
        values = [src[row].reshape(size, N4) for row in rows_of(group)]
        high = [value.astype(jnp.bfloat16) for value in values]
        rest = [(value - h.astype(jnp.float32)).astype(jnp.bfloat16) for value, h in zip(values, high)]
        across, along = products[group % 2]
        stacked = [jnp.concatenate(pair, axis=0) for pair in zip(high, rest)]
        across[:, : len(values) * N4] = jnp.dot(
            left[...], jnp.concatenate(stacked, axis=1), preferred_element_type=jnp.float32
        )
        beside = [jnp.concatenate(pair, axis=1) for pair in zip(high, rest)]
        along[: len(values) * size] = jnp.dot(
            jnp.concatenate(beside, axis=0), right[...], preferred_element_type=jnp.float32
        )

    groups = -(-count // UNROLL)
    multiply(0)
    for group in range(groups):
        if group + 1 < groups:
            multiply(group + 1)
        across, along = products[group % 2]
        for i, row in enumerate(rows_of(group)):
            lanes = slice(i * N4, (i + 1) * N4)
            for t in range(TILES):
                u, below, above = src[row, t], src[row - 1, t], src[row + 1, t]
                here = slice(t * N2, (t + 1) * N2)
                there = slice(size + t * N2, size + (t + 1) * N2)
                beside = slice(i * size + t * N2, i * size + (t + 1) * N2)
                second = (across[here, lanes] + along[beside, :N4]) + q0 * (below + above)
                drift = (across[there, lanes] + along[beside, N4:]) + s0 * below
                speed = ADVECT + (0.5 * ADVECT) * jnp.tanh(u)
                dst[row, t] = (u + DIFFUSE * second) + speed * drift


def interpolate(nodes, fine, middle):
    u0, u1, u2, u3, u4 = nodes
    v2 = jnp.where(middle, u2, 0.5 * (u0 + u4))
    v1 = jnp.where(fine, u1, 0.5 * (u0 + v2))
    v3 = jnp.where(fine, u3, 0.5 * (v2 + u4))
    return u0, v1, v2, v3


def spaces(rows):
    state = pltpu.VMEM((rows + LOW + HIGH, TILES, N2, N4), jnp.float32)
    size = TILES * N2
    across = pltpu.VMEM((2 * size, UNROLL * N4), jnp.float32)
    along = pltpu.VMEM((UNROLL * size, 2 * N4), jnp.float32)
    return [state, state, across, along, across, along]


def run_steps(bufs, rows, tables, s0):
    states, products = bufs[0:2], (bufs[2:4], bufs[4:6])
    for step in range(STEPS):
        count = rows + LOW + HIGH - 2 * (step + 1)
        step_rows(states[step % 2], states[(step + 1) % 2], step + 1, count, tables, (s0, s0 * s0), products)
    return states[STEPS % 2]


def ends_kernel(field, last, first, sems):
    rows = field.shape[0]
    one = pltpu.make_async_copy(field.at[pl.ds(rows - LOW, LOW)], last, sems.at[0])
    two = pltpu.make_async_copy(field.at[pl.ds(0, HIGH)], first, sems.at[1])
    one.start()
    two.start()
    one.wait()
    two.wait()


def load_rows(ref, first, count, state, at):
    def body(i, carry):
        for n1 in range(N1):
            for n3 in range(N3):
                state[at + i, n1 * N3 + n3] = ref[first + i, pl.ds(n1 * N2 * N3 + n3, N2, stride=N3), :]
        return carry

    lax.fori_loop(0, count, body, 0)


def scales_of(level):
    return [lax.shift_left(1, level[0, d]).astype(jnp.float32) * 0.125 for d in range(5)]


def first_cycle(level, tables, rows, outs, bufs):
    me, grids = lax.axis_index("grid"), lax.axis_size("grid")
    levels, scales = [level[0, d] for d in range(5)], scales_of(level)
    parity = lax.rem(levels[0] + levels[1] + levels[2] + levels[3] + levels[4], 2)
    weight = (1 - 2 * parity).astype(jnp.float32) * (1.0 / math.sqrt(grids))
    done = run_steps(bufs, rows, tables, scales[0])
    fine, middle = levels[0] >= 3, levels[0] >= 2
    block = outs[0][1].shape[0] // TILES
    for first, out in outs:
        for quad in range(0, block, 4):
            base = LOW + first + quad
            for t in range(TILES):
                values = interpolate([done[base + i, t] for i in range(5)], fine, middle)
                for i, value in enumerate(values):
                    out[(quad + i) * TILES + t] = weight * value
        lane = lax.broadcasted_iota(jnp.int32, (N2, N4), 1)
        tile = jnp.zeros((N2, N4), jnp.float32)
        for d, value in enumerate(scales + [levels[0].astype(jnp.float32), weight]):
            tile = jnp.where(lane == d, value, tile)
        sublane = lax.broadcasted_iota(jnp.int32, (N2, N4), 0)
        out[block * TILES] = jnp.where(sublane == me, tile, 0.0)


def middle_kernel(level, field, middle, near, left, right, *bufs):
    rows = field.shape[0] // 2
    block = rows // 2
    fill_tables(scales_of(level), left, right)
    load_rows(field, block - LOW, rows + LOW + HIGH, bufs[0], 0)
    side = lax.div(2 * lax.axis_index("grid"), lax.axis_size("grid"))
    upper = lax.rem(side + lax.axis_index("slab"), 2) == 0
    first = jnp.where(upper, block, 0)
    first_cycle(level, (left, right), rows, ((first, middle), (block - first, near)), bufs)


def outer_kernel(later, level, left, right, before, field, after, out, *bufs):
    total = field.shape[0]
    block = out.shape[0] // TILES
    top = lax.rem(lax.axis_index("grid") + lax.axis_index("slab") + later, 2) == 0

    @pl.when(top)
    def _():
        load_rows(field, total - block - LOW, block + LOW, bufs[0], 0)
        load_rows(after, 0, HIGH, bufs[0], block + LOW)

    @pl.when(jnp.logical_not(top))
    def _():
        load_rows(before, 0, LOW, bufs[0], 0)
        load_rows(field, 0, block + HIGH, bufs[0], LOW)

    first_cycle(level, (left, right), block, ((0, out),), bufs)


def sent_value(own, g, d):
    return jnp.broadcast_to(own[own.shape[0] - 1, pl.ds(g, 1), d : d + 1], (1, N4))


def tables_kernel(grids, own, left, right):
    def grid(g, carry):
        fill_tables([sent_value(own, g, d) for d in range(5)], left.at[g], right.at[g])
        return carry

    lax.fori_loop(0, grids, grid, 0)


def second_kernel(rows, grids, left, right, before, own, after, out, total, wide, *bufs):
    extent = rows + LOW + HIGH
    for i in range(LOW * TILES):
        wide[i] = before[i]
    for i in range(rows * TILES):
        wide[LOW * TILES + i] = own[i]
    for i in range(HIGH * TILES):
        wide[(LOW + rows) * TILES + i] = after[i]
    total[...] = jnp.zeros_like(total)

    def grid(g, carry):
        tile = lambda d: jnp.broadcast_to(sent_value(own, g, d), (N2, N4))
        fine, middle, weight = tile(5) > 2.5, tile(5) > 1.5, tile(6)
        start = bufs[0]
        for quad in range(0, extent - 1, 4):
            for t in range(TILES):
                values = interpolate([wide[(quad + i) * TILES + t] for i in range(5)], fine, middle)
                for i, value in enumerate(values):
                    start[quad + i, t] = value
        for t in range(TILES):
            start[extent - 1, t] = wide[(extent - 1) * TILES + t]
        done = run_steps(bufs, rows, (left.at[g], right.at[g]), tile(0))
        for quad in range(0, rows, 4):
            for t in range(TILES):
                values = interpolate([done[LOW + quad + i, t] for i in range(5)], fine, middle)
                for i, value in enumerate(values):
                    at = pl.ds(((quad + i) * TILES + t) * N2, N2)
                    total[at, :] = weight * value + total[at, :]
        return carry

    lax.fori_loop(0, grids, grid, 0)
    half = N2 // 2
    for n3 in range(N3):
        for n1 in range(N1):
            for n2 in range(N2):
                at = (n3 * N1 + n1) * 2 + n2 // half
                out[at, n2 % half] = total[pl.ds((n1 * N3 + n3) * N2 + n2, rows, stride=TILES * N2), :]


def hier_kernel(groups, matrix, rows, *outs):
    me = lax.axis_index("grid")
    lanes = rows.shape[3]
    count = matrix.shape[0] // groups
    for n in range(rows.shape[1]):
        whole = rows[:, n].reshape(matrix.shape[1], lanes)
        high = whole.astype(jnp.bfloat16)
        rest = (whole - high.astype(jnp.float32)).astype(jnp.bfloat16)
        for d, out in enumerate(outs):
            part = matrix[pl.ds(lax.rem(me + d, groups) * count, count), :]
            out[n] = jnp.dot(part, high, preferred_element_type=jnp.float32) + jnp.dot(
                part, rest, preferred_element_type=jnp.float32
            )


def place_kernel(groups, *refs):
    received, out = refs[:-1], refs[-1]
    me = lax.axis_index("grid")
    parts, count = received[0].shape[0], received[0].shape[1]
    for d, ref in enumerate(received):
        n3 = lax.rem(me + groups - d, groups)
        for n in range(parts):
            out[pl.ds(n * N3 + n3, count, stride=parts * N3), :] = ref[n]


def kernel(body, out_shape, in_specs, scratch=(), limit=4, flops=0):
    single = not isinstance(out_shape, (list, tuple))
    return pl.pallas_call(
        body,
        out_shape=out_shape,
        in_specs=in_specs,
        out_specs=VMEM if single else [VMEM] * len(out_shape),
        scratch_shapes=list(scratch),
        compiler_params=pltpu.CompilerParams(vmem_limit_bytes=limit << 20),
        cost_estimate=pl.CostEstimate(flops=flops, bytes_accessed=1 << 20, transcendentals=flops // 30),
    )


def fast_sizes(grids, slabs):
    rows = N0 // slabs
    return rows, rows // grids


def fast_fits(grids, slabs):
    _, block = fast_sizes(grids, slabs)
    return grids == 4 and grids == N3 and slabs == 2 * N1 and block >= HIGH and block % 4 == 0


def floats(*shape):
    return jax.ShapeDtypeStruct(shape, jnp.float32)


def local_fast(field, levels, owner):
    grids, slabs = lax.axis_size("grid"), lax.axis_size("slab")
    rows, block = fast_sizes(grids, slabs)
    state = field[0]

    up = [(i, (i + 1) % slabs) for i in range(slabs)]
    down = [(j, i) for i, j in up]
    last, first = kernel(
        ends_kernel,
        [floats(LOW, Q, N4), floats(HIGH, Q, N4)],
        [HBM],
        [pltpu.SemaphoreType.DMA((2,))],
    )(pltpu.with_memory_space_constraint(state, pltpu.HBM))
    before = lax.ppermute(last, "slab", up)
    after = lax.ppermute(first, "slab", down)

    piece = floats(block * TILES + 1, N2, N4)
    work = 8192 * 40
    size = 2 * TILES * N2

    def tables(*lead):
        shapes = (lead + (size, size), lead + (2 * N4, 2 * N4))
        return [jax.ShapeDtypeStruct(shape, jnp.bfloat16) for shape in shapes]

    middle, near, left, right = kernel(
        middle_kernel,
        [piece, piece] + tables(),
        [SMEM, VMEM],
        spaces(rows // 2),
        limit=6,
        flops=80 * work,
    )(levels, state)

    ready = lax.optimization_barrier((before, after, middle))

    def outer_block(later):
        return kernel(
            functools.partial(outer_kernel, later),
            piece,
            [SMEM] + [VMEM] * 5,
            spaces(block),
            limit=6,
            flops=48 * work,
        )(levels, left, right, ready[0], state, ready[1])

    edge = (lax.axis_index("grid") == 0) | (lax.axis_index("grid") == grids - 1)
    across = lax.ppermute(middle, "grid", [(1, 2), (2, 1)])
    first_out = outer_block(0)
    swapped = lax.ppermute(first_out, "grid", [(0, 1), (1, 0), (2, 3), (3, 2)])
    middle, near, _ = lax.optimization_barrier((middle, near, first_out))
    skipped = lax.ppermute(middle, "grid", [(0, 2), (3, 1)])
    inwards = lax.ppermute(near, "grid", [(0, 1), (3, 2)])
    second_out = outer_block(1)
    joined = swapped + second_out
    passed = lax.ppermute(joined, "grid", [(1, 3), (2, 0)])
    own = jnp.where(edge, joined, near) + across + skipped + inwards + passed

    chain = []
    for k in range(slabs):
        chain += [(g if k % 2 == 0 else grids - 1 - g) * slabs + k for g in range(grids)]
    forward = [(chain[i], chain[(i + 1) % len(chain)]) for i in range(len(chain))]
    backward = [(j, i) for i, j in forward]
    both = ("grid", "slab")
    before = lax.ppermute(own[(block - LOW) * TILES : block * TILES], both, forward)
    after = lax.ppermute(own[: HIGH * TILES], both, backward)

    left, right = kernel(
        functools.partial(tables_kernel, grids), tables(grids), [VMEM], flops=30 * work
    )(own)
    half = N2 // 2
    sent = kernel(
        functools.partial(second_kernel, block, grids),
        floats(N3 * N1 * 2, half, block, N4),
        [VMEM] * 5,
        [
            pltpu.VMEM((block * TILES * N2, N4), jnp.float32),
            pltpu.VMEM(((block + LOW + HIGH) * TILES, N2, N4), jnp.float32),
        ]
        + spaces(block),
        limit=8,
        flops=400 * 8192 * 40,
    )(left, right, before, own, after)

    spread = lax.all_to_all(sent, both, split_axis=0, concat_axis=0, tiled=True)

    source = np.zeros(N0, np.int32)
    for place, device in enumerate(chain):
        source[device * block : (device + 1) * block] = place * block + np.arange(block)
    column = jnp.asarray(source)[None, :]
    row = owner[:, None]
    reach = jnp.where(row > 0, row & -row, 0)
    part = jnp.where(row > 0, -0.5, 0.0)
    matrix = (
        (column == row).astype(jnp.float32)
        + part * (column == row - reach)
        + part * (column == (row + reach) % N0)
    ).astype(jnp.bfloat16)
    group = N0 // grids
    hier = kernel(
        functools.partial(hier_kernel, grids), [floats(half, group, N4)] * grids, [VMEM, VMEM]
    )(matrix, spread)
    others = lax.optimization_barrier(tuple(hier[1:]))
    received = [hier[0]] + [
        lax.ppermute(value, "grid", [(i, (i + d) % grids) for i in range(grids)])
        for d, value in enumerate(others, 1)
    ]
    out = kernel(
        functools.partial(place_kernel, grids), floats(group * half * N3, N4), [VMEM] * grids
    )(*received)
    return out.reshape(group, Q // slabs, N4)


def local(field, levels, owner):
    if fast_fits(lax.axis_size("grid"), lax.axis_size("slab")):
        return local_fast(field, levels, owner)
    return local_general(field, levels, owner)


def solution(mesh):
    in_specs = (P(("copies", "grid"), "slab", None, None), P(("copies", "grid"), None), P("copies"))
    out_specs = P(("copies", "grid"), "slab", None)
    return jax.shard_map(local, mesh=mesh, in_specs=in_specs, out_specs=out_specs, check_vma=False)
```

```python
import functools
import math

import jax
import jax.numpy as jnp
import numpy as np
from jax import lax
from jax.experimental import pallas as pl
from jax.experimental.pallas import tpu as pltpu
from jax.sharding import PartitionSpec as P


N0 = 128
N1 = 2
N2 = 8
N3 = 4
N4 = 128
STEPS = 4
Q = 64

ADVECT = 0.08
DIFFUSE = 0.03

LOW = STEPS
HIGH = STEPS + 1
TILES = N1 * N3


def extended_2(value, sides, width):
    for axis, dim in sides:
        count, length = (lax.axis_size(axis), value.shape[dim])
        up = [(i, (i + 1) % count) for i in range(count)]
        down = [(j, i) for i, j in up]
        last = lax.slice_in_dim(value, length - width, length, axis=dim)
        first = lax.slice_in_dim(value, 0, width, axis=dim)
        before = lax.ppermute(last, axis, up)
        after = lax.ppermute(first, axis, down)
        value = jnp.concatenate([before, value, after], axis=dim)
    return value


def build_tables(count):
    depth = count.bit_length() - 1
    matrix = np.eye(count)
    inverse = np.zeros((count, count))
    inverse[0, 0] = 1.0
    level_rows = np.zeros(count, np.int32)
    for index in range(1, count):
        zeros = (index & -index).bit_length() - 1
        spacing = 1 << zeros
        matrix[index, index - spacing] -= 0.5
        matrix[index, (index + spacing) % count] -= 0.5
        level_rows[index] = depth - zeros
    for zeros in range(depth - 1, -1, -1):
        spacing = 1 << zeros
        for index in range(spacing, count, 2 * spacing):
            inverse[index] = 0.5 * (inverse[index - spacing] + inverse[(index + spacing) % count])
            inverse[index, index] += 1.0
    return (matrix.astype(np.float32), inverse.astype(np.float32), level_rows)


def advance(extended, scales, padded):
    length = extended.shape[padded] - 2
    centre = lax.slice_in_dim(extended, 1, length + 1, axis=padded)
    speed = 1.0 + 0.5 * jnp.tanh(centre)
    change = jnp.zeros_like(centre)
    for axis in range(5):
        if axis == padded:
            back = lax.slice_in_dim(extended, 0, length, axis=padded)
            ahead = lax.slice_in_dim(extended, 2, length + 2, axis=padded)
        else:
            back = jnp.roll(centre, 1, axis)
            ahead = jnp.roll(centre, -1, axis)
        change = (
            change
            - ADVECT * scales[axis] * speed * (centre - back)
            + DIFFUSE * scales[axis] ** 2 * (ahead - 2.0 * centre + back)
        )
    return centre + change


def regroup_rows(stepped):
    return lax.all_to_all(stepped, "slab", split_axis=1, concat_axis=0, tiled=True)


def local_general(field, levels, owner):
    matrix, inverse, level_rows = build_tables(N0)
    matrix = jnp.asarray(matrix)
    inverse = jnp.asarray(inverse)
    depth = N0.bit_length() - 1
    level_vec = levels[0]
    scales = jnp.exp2(level_vec.astype(jnp.float32)) / 8.0
    weight = jnp.where(jnp.sum(level_vec) % 2 == 0, 1.0, -1.0).astype(jnp.float32) / math.sqrt(
        lax.axis_size("grid")
    )
    keep = (jnp.asarray(level_rows) <= depth - 3 + level_vec[0]).astype(jnp.float32)[:, None, None]

    def evolve_rows(state):
        rows = state.shape[0]
        grid5 = state.reshape(rows, N1, N2, N3, N4)
        for _ in range(STEPS):
            extended = extended_2(grid5, (("slab", 0),), 1)
            grid5 = advance(extended, scales, 0)
        return grid5.reshape(rows, Q, N4)

    def hierarchise(whole):
        hier = jnp.dot(matrix, whole.reshape(N0, -1), precision=lax.Precision.HIGHEST)
        return weight * keep * hier.reshape(whole.shape)

    def reduce_terms(terms):
        return lax.psum_scatter(terms[owner], "grid", scatter_dimension=0, tiled=True)

    stepped = evolve_rows(field[0])
    summed = reduce_terms(hierarchise(regroup_rows(stepped)))
    ordered = lax.all_gather(summed, "grid", axis=0, tiled=True)
    position = jnp.zeros((N0,), jnp.int32).at[owner].set(jnp.arange(N0, dtype=jnp.int32))
    combined = ordered[position]
    masked = (keep * combined).reshape(N0, -1)
    nodal = jnp.dot(inverse, masked, precision=lax.Precision.HIGHEST).reshape(combined.shape)
    state = lax.all_to_all(nodal, "slab", split_axis=0, concat_axis=1, tiled=True)
    stepped = evolve_rows(state)
    summed = reduce_terms(hierarchise(regroup_rows(stepped)))
    return summed


VMEM = pl.BlockSpec(memory_space=pltpu.VMEM)
SMEM = pl.BlockSpec(memory_space=pltpu.SMEM)
HBM = pl.BlockSpec(memory_space=pltpu.HBM)
UNROLL = 2


def fill_tables(scales, left):
    size = TILES * N2
    squares = [value * value for value in scales]
    total = sum(scales[1:], scales[0])
    square = sum(squares[1:], squares[0])
    shape = (size, 2 * size)
    row = lax.broadcasted_iota(jnp.int32, shape, 0)
    column = lax.bitwise_and(lax.broadcasted_iota(jnp.int32, shape, 1), size - 1)
    drift = jnp.where(row == column, -total, 0.0)
    second = jnp.where(row == column, -2.0 * square, 0.0)
    for d, unit, count in ((1, N3 * N2, N1), (2, 1, N2), (3, N2, N3)):
        digit = lax.bitwise_and(lax.div(row, unit), count - 1)
        rest = row - digit * unit
        back = column == rest + lax.bitwise_and(digit + count - 1, count - 1) * unit
        ahead = column == rest + lax.bitwise_and(digit + 1, count - 1) * unit
        drift = drift + jnp.where(back, scales[d], 0.0)
        second = second + jnp.where(back, squares[d], 0.0) + jnp.where(ahead, squares[d], 0.0)
    left[:, : 2 * size] = jnp.concatenate([second, drift], axis=0).astype(jnp.bfloat16)
    drift = jnp.where(row == column, scales[0], 0.0)
    second = jnp.where(row == column, squares[0], 0.0)
    left[:, 2 * size :] = jnp.concatenate([second, drift], axis=0).astype(jnp.bfloat16)


def step_rows(src, dst, first, count, left, factors, products):
    q0, s4, q4 = factors
    size = TILES * N2

    def rows_of(group):
        return range(first + group * UNROLL, first + min(count, (group + 1) * UNROLL))

    def parts(row):
        value = src[row].reshape(size, N4)
        high = value.astype(jnp.bfloat16)
        return jnp.concatenate([high, (value - high.astype(jnp.float32)).astype(jnp.bfloat16)], axis=0)

    last = [parts(first - 1)]

    def multiply(group):
        held = [parts(row) for row in rows_of(group)]
        below = last + held
        last[:] = [held[-1]]
        held = [jnp.concatenate(pair, axis=0) for pair in zip(held, below)]
        products[group % 2][:, : len(held) * N4] = jnp.dot(
            left[...], jnp.concatenate(held, axis=1), preferred_element_type=jnp.float32
        )

    groups = -(-count // UNROLL)
    multiply(0)
    for group in range(groups):
        if group + 1 < groups:
            multiply(group + 1)
        product = products[group % 2]
        for i, row in enumerate(rows_of(group)):
            lanes = slice(i * N4, (i + 1) * N4)
            for t in range(TILES):
                u, above = src[row, t], src[row + 1, t]
                back, ahead = pltpu.roll(u, 1, 1), pltpu.roll(u, N4 - 1, 1)
                second = product[t * N2 : (t + 1) * N2, lanes] + q0 * above
                drift = product[size + t * N2 : size + (t + 1) * N2, lanes] + s4 * back
                second = second + q4 * (back + ahead)
                speed = ADVECT + (0.5 * ADVECT) * jnp.tanh(u)
                dst[row, t] = (u + DIFFUSE * second) + speed * drift


def interpolate(nodes, fine, middle):
    u0, u1, u2, u3, u4 = nodes
    v2 = jnp.where(middle, u2, 0.5 * (u0 + u4))
    v1 = jnp.where(fine, u1, 0.5 * (u0 + v2))
    v3 = jnp.where(fine, u3, 0.5 * (v2 + u4))
    return u0, v1, v2, v3


def spaces(rows):
    state = pltpu.VMEM((rows + LOW + HIGH, TILES, N2, N4), jnp.float32)
    product = pltpu.VMEM((2 * TILES * N2, UNROLL * N4), jnp.float32)
    return [state, state, product, product]


def run_steps(bufs, rows, left, scales):
    states, products = bufs[0:2], bufs[2:4]
    factors = (scales[0] * scales[0], scales[4], scales[4] * scales[4])
    for step in range(STEPS):
        count = rows + LOW + HIGH - 2 * (step + 1)
        step_rows(states[step % 2], states[(step + 1) % 2], step + 1, count, left, factors, products)
    return states[STEPS % 2]


def ends_kernel(field, last, first, sems):
    rows = field.shape[0]
    one = pltpu.make_async_copy(field.at[pl.ds(rows - LOW, LOW)], last, sems.at[0])
    two = pltpu.make_async_copy(field.at[pl.ds(0, HIGH)], first, sems.at[1])
    one.start()
    two.start()
    one.wait()
    two.wait()


def load_rows(ref, first, count, state, at):
    def body(i, carry):
        for n1 in range(N1):
            for n3 in range(N3):
                state[at + i, n1 * N3 + n3] = ref[first + i, pl.ds(n1 * N2 * N3 + n3, N2, stride=N3), :]
        return carry

    lax.fori_loop(0, count, body, 0)


def scales_of(level):
    return [lax.shift_left(1, level[0, d]).astype(jnp.float32) * 0.125 for d in range(5)]


def first_cycle(level, left, rows, outs, bufs):
    me, grids = lax.axis_index("grid"), lax.axis_size("grid")
    levels, scales = [level[0, d] for d in range(5)], scales_of(level)
    parity = lax.rem(levels[0] + levels[1] + levels[2] + levels[3] + levels[4], 2)
    weight = (1 - 2 * parity).astype(jnp.float32) * (1.0 / math.sqrt(grids))
    done = run_steps(bufs, rows, left, scales)
    fine, middle = levels[0] >= 3, levels[0] >= 2
    block = outs[0][1].shape[0] // TILES
    for first, out in outs:
        for quad in range(0, block, 4):
            base = LOW + first + quad
            for t in range(TILES):
                values = interpolate([done[base + i, t] for i in range(5)], fine, middle)
                for i, value in enumerate(values):
                    out[(quad + i) * TILES + t] = weight * value
        lane = lax.broadcasted_iota(jnp.int32, (N2, N4), 1)
        tile = jnp.zeros((N2, N4), jnp.float32)
        for d, value in enumerate(scales + [levels[0].astype(jnp.float32), weight]):
            tile = jnp.where(lane == d, value, tile)
        sublane = lax.broadcasted_iota(jnp.int32, (N2, N4), 0)
        out[block * TILES] = jnp.where(sublane == me, tile, 0.0)


def middle_kernel(level, field, middle, near, left, *bufs):
    rows = field.shape[0] // 2
    block = rows // 2
    fill_tables(scales_of(level), left)
    load_rows(field, block - LOW, rows + LOW + HIGH, bufs[0], 0)
    side = lax.div(2 * lax.axis_index("grid"), lax.axis_size("grid"))
    upper = lax.rem(side + lax.axis_index("slab"), 2) == 0
    first = jnp.where(upper, block, 0)
    first_cycle(level, left, rows, ((first, middle), (block - first, near)), bufs)


def outer_kernel(later, level, left, before, field, after, out, *bufs):
    total = field.shape[0]
    block = out.shape[0] // TILES
    top = lax.rem(lax.axis_index("grid") + lax.axis_index("slab") + later, 2) == 0

    @pl.when(top)
    def _():
        load_rows(field, total - block - LOW, block + LOW, bufs[0], 0)
        load_rows(after, 0, HIGH, bufs[0], block + LOW)

    @pl.when(jnp.logical_not(top))
    def _():
        load_rows(before, 0, LOW, bufs[0], 0)
        load_rows(field, 0, block + HIGH, bufs[0], LOW)

    first_cycle(level, left, block, ((0, out),), bufs)


def sent_value(own, g, d):
    return jnp.broadcast_to(own[own.shape[0] - 1, pl.ds(g, 1), d : d + 1], (1, N4))


def tables_kernel(grids, own, left):
    def grid(g, carry):
        fill_tables([sent_value(own, g, d) for d in range(5)], left.at[g])
        return carry

    lax.fori_loop(0, grids, grid, 0)


def second_kernel(rows, grids, left, before, own, after, out, total, wide, *bufs):
    extent = rows + LOW + HIGH
    for i in range(LOW * TILES):
        wide[i] = before[i]
    for i in range(rows * TILES):
        wide[LOW * TILES + i] = own[i]
    for i in range(HIGH * TILES):
        wide[(LOW + rows) * TILES + i] = after[i]
    total[...] = jnp.zeros_like(total)

    def grid(g, carry):
        tile = lambda d: jnp.broadcast_to(sent_value(own, g, d), (N2, N4))
        fine, middle, weight = tile(5) > 2.5, tile(5) > 1.5, tile(6)
        start = bufs[0]
        for quad in range(0, extent - 1, 4):
            for t in range(TILES):
                values = interpolate([wide[(quad + i) * TILES + t] for i in range(5)], fine, middle)
                for i, value in enumerate(values):
                    start[quad + i, t] = value
        for t in range(TILES):
            start[extent - 1, t] = wide[(extent - 1) * TILES + t]
        done = run_steps(bufs, rows, left.at[g], [tile(d) for d in range(5)])
        for quad in range(0, rows, 4):
            for t in range(TILES):
                values = interpolate([done[LOW + quad + i, t] for i in range(5)], fine, middle)
                for i, value in enumerate(values):
                    at = pl.ds(((quad + i) * TILES + t) * N2, N2)
                    total[at, :] = weight * value + total[at, :]
        return carry

    lax.fori_loop(0, grids, grid, 0)
    half = N2 // 2
    for n3 in range(N3):
        for n1 in range(N1):
            for n2 in range(N2):
                at = (n3 * N1 + n1) * 2 + n2 // half
                out[at, n2 % half] = total[pl.ds((n1 * N3 + n3) * N2 + n2, rows, stride=TILES * N2), :]


def hier_kernel(groups, matrix, rows, *outs):
    me = lax.axis_index("grid")
    lanes = rows.shape[3]
    count = matrix.shape[0] // groups
    for n in range(rows.shape[1]):
        whole = rows[:, n].reshape(matrix.shape[1], lanes)
        high = whole.astype(jnp.bfloat16)
        rest = (whole - high.astype(jnp.float32)).astype(jnp.bfloat16)
        for d, out in enumerate(outs):
            part = matrix[pl.ds(lax.rem(me + d, groups) * count, count), :]
            out[n] = jnp.dot(part, high, preferred_element_type=jnp.float32) + jnp.dot(
                part, rest, preferred_element_type=jnp.float32
            )


def place_kernel(groups, *refs):
    received, out = refs[:-1], refs[-1]
    me = lax.axis_index("grid")
    parts, count = received[0].shape[0], received[0].shape[1]
    for d, ref in enumerate(received):
        n3 = lax.rem(me + groups - d, groups)
        for n in range(parts):
            out[pl.ds(n * N3 + n3, count, stride=parts * N3), :] = ref[n]


def kernel(body, out_shape, in_specs, scratch=(), limit=4, flops=0):
    single = not isinstance(out_shape, (list, tuple))
    return pl.pallas_call(
        body,
        out_shape=out_shape,
        in_specs=in_specs,
        out_specs=VMEM if single else [VMEM] * len(out_shape),
        scratch_shapes=list(scratch),
        compiler_params=pltpu.CompilerParams(vmem_limit_bytes=limit << 20),
        cost_estimate=pl.CostEstimate(flops=flops, bytes_accessed=1 << 20, transcendentals=flops // 30),
    )


def fast_sizes(grids, slabs):
    rows = N0 // slabs
    return rows, rows // grids


def fast_fits(grids, slabs):
    _, block = fast_sizes(grids, slabs)
    return grids == 4 and grids == N3 and slabs == 2 * N1 and block >= HIGH and block % 4 == 0


def floats(*shape):
    return jax.ShapeDtypeStruct(shape, jnp.float32)


def local_fast(field, levels, owner):
    grids, slabs = lax.axis_size("grid"), lax.axis_size("slab")
    rows, block = fast_sizes(grids, slabs)
    state = field[0]

    up = [(i, (i + 1) % slabs) for i in range(slabs)]
    down = [(j, i) for i, j in up]
    last, first = kernel(
        ends_kernel,
        [floats(LOW, Q, N4), floats(HIGH, Q, N4)],
        [HBM],
        [pltpu.SemaphoreType.DMA((2,))],
    )(pltpu.with_memory_space_constraint(state, pltpu.HBM))
    before = lax.ppermute(last, "slab", up)
    after = lax.ppermute(first, "slab", down)

    piece = floats(block * TILES + 1, N2, N4)
    work = 8192 * 40
    size = 2 * TILES * N2

    def table(*lead):
        return jax.ShapeDtypeStruct(lead + (size, 2 * size), jnp.bfloat16)

    middle, near, left = kernel(
        middle_kernel,
        [piece, piece, table()],
        [SMEM, VMEM],
        spaces(rows // 2),
        limit=6,
        flops=80 * work,
    )(levels, state)

    ready = lax.optimization_barrier((before, after, middle))

    def outer_block(later):
        return kernel(
            functools.partial(outer_kernel, later),
            piece,
            [SMEM] + [VMEM] * 4,
            spaces(block),
            limit=6,
            flops=48 * work,
        )(levels, left, ready[0], state, ready[1])

    edge = (lax.axis_index("grid") == 0) | (lax.axis_index("grid") == grids - 1)
    across = lax.ppermute(middle, "grid", [(1, 2), (2, 1)])
    first_out = outer_block(0)
    swapped = lax.ppermute(first_out, "grid", [(0, 1), (1, 0), (2, 3), (3, 2)])
    middle, near, _ = lax.optimization_barrier((middle, near, first_out))
    skipped = lax.ppermute(middle, "grid", [(0, 2), (3, 1)])
    inwards = lax.ppermute(near, "grid", [(0, 1), (3, 2)])
    second_out = outer_block(1)
    joined = swapped + second_out
    passed = lax.ppermute(joined, "grid", [(1, 3), (2, 0)])
    own = jnp.where(edge, joined, near) + across + skipped + inwards + passed

    chain = []
    for k in range(slabs):
        chain += [(g if k % 2 == 0 else grids - 1 - g) * slabs + k for g in range(grids)]
    forward = [(chain[i], chain[(i + 1) % len(chain)]) for i in range(len(chain))]
    backward = [(j, i) for i, j in forward]
    both = ("grid", "slab")
    before = lax.ppermute(own[(block - LOW) * TILES : block * TILES], both, forward)
    after = lax.ppermute(own[: HIGH * TILES], both, backward)

    left = kernel(
        functools.partial(tables_kernel, grids), table(grids), [VMEM], flops=30 * work
    )(own)
    half = N2 // 2
    sent = kernel(
        functools.partial(second_kernel, block, grids),
        floats(N3 * N1 * 2, half, block, N4),
        [VMEM] * 4,
        [
            pltpu.VMEM((block * TILES * N2, N4), jnp.float32),
            pltpu.VMEM(((block + LOW + HIGH) * TILES, N2, N4), jnp.float32),
        ]
        + spaces(block),
        limit=8,
        flops=400 * 8192 * 40,
    )(left, before, own, after)

    spread = lax.all_to_all(sent, both, split_axis=0, concat_axis=0, tiled=True)

    source = np.zeros(N0, np.int32)
    for place, device in enumerate(chain):
        source[device * block : (device + 1) * block] = place * block + np.arange(block)
    column = jnp.asarray(source)[None, :]
    row = owner[:, None]
    reach = jnp.where(row > 0, row & -row, 0)
    part = jnp.where(row > 0, -0.5, 0.0)
    matrix = (
        (column == row).astype(jnp.float32)
        + part * (column == row - reach)
        + part * (column == (row + reach) % N0)
    ).astype(jnp.bfloat16)
    group = N0 // grids
    hier = kernel(
        functools.partial(hier_kernel, grids), [floats(half, group, N4)] * grids, [VMEM, VMEM]
    )(matrix, spread)
    others = lax.optimization_barrier(tuple(hier[1:]))
    received = [hier[0]] + [
        lax.ppermute(value, "grid", [(i, (i + d) % grids) for i in range(grids)])
        for d, value in enumerate(others, 1)
    ]
    out = kernel(
        functools.partial(place_kernel, grids), floats(group * half * N3, N4), [VMEM] * grids
    )(*received)
    return out.reshape(group, Q // slabs, N4)


def local(field, levels, owner):
    if fast_fits(lax.axis_size("grid"), lax.axis_size("slab")):
        return local_fast(field, levels, owner)
    return local_general(field, levels, owner)


def solution(mesh):
    in_specs = (P(("copies", "grid"), "slab", None, None), P(("copies", "grid"), None), P("copies"))
    out_specs = P(("copies", "grid"), "slab", None)
    return jax.shard_map(local, mesh=mesh, in_specs=in_specs, out_specs=out_specs, check_vma=False)
```

```python
import functools
import math

import jax
import jax.numpy as jnp
import numpy as np
from jax import lax
from jax.experimental import pallas as pl
from jax.experimental.pallas import tpu as pltpu
from jax.sharding import PartitionSpec as P


N0 = 128
N1 = 2
N2 = 8
N3 = 4
N4 = 128
STEPS = 4
Q = 64

ADVECT = 0.08
DIFFUSE = 0.03

LOW = STEPS
HIGH = STEPS + 1
TILES = N1 * N3


def extended_2(value, sides, width):
    for axis, dim in sides:
        count, length = (lax.axis_size(axis), value.shape[dim])
        up = [(i, (i + 1) % count) for i in range(count)]
        down = [(j, i) for i, j in up]
        last = lax.slice_in_dim(value, length - width, length, axis=dim)
        first = lax.slice_in_dim(value, 0, width, axis=dim)
        before = lax.ppermute(last, axis, up)
        after = lax.ppermute(first, axis, down)
        value = jnp.concatenate([before, value, after], axis=dim)
    return value


def build_tables(count):
    depth = count.bit_length() - 1
    matrix = np.eye(count)
    inverse = np.zeros((count, count))
    inverse[0, 0] = 1.0
    level_rows = np.zeros(count, np.int32)
    for index in range(1, count):
        zeros = (index & -index).bit_length() - 1
        spacing = 1 << zeros
        matrix[index, index - spacing] -= 0.5
        matrix[index, (index + spacing) % count] -= 0.5
        level_rows[index] = depth - zeros
    for zeros in range(depth - 1, -1, -1):
        spacing = 1 << zeros
        for index in range(spacing, count, 2 * spacing):
            inverse[index] = 0.5 * (inverse[index - spacing] + inverse[(index + spacing) % count])
            inverse[index, index] += 1.0
    return (matrix.astype(np.float32), inverse.astype(np.float32), level_rows)


def advance(extended, scales, padded):
    length = extended.shape[padded] - 2
    centre = lax.slice_in_dim(extended, 1, length + 1, axis=padded)
    speed = 1.0 + 0.5 * jnp.tanh(centre)
    change = jnp.zeros_like(centre)
    for axis in range(5):
        if axis == padded:
            back = lax.slice_in_dim(extended, 0, length, axis=padded)
            ahead = lax.slice_in_dim(extended, 2, length + 2, axis=padded)
        else:
            back = jnp.roll(centre, 1, axis)
            ahead = jnp.roll(centre, -1, axis)
        change = (
            change
            - ADVECT * scales[axis] * speed * (centre - back)
            + DIFFUSE * scales[axis] ** 2 * (ahead - 2.0 * centre + back)
        )
    return centre + change


def regroup_rows(stepped):
    return lax.all_to_all(stepped, "slab", split_axis=1, concat_axis=0, tiled=True)


def local_general(field, levels, owner):
    matrix, inverse, level_rows = build_tables(N0)
    matrix = jnp.asarray(matrix)
    inverse = jnp.asarray(inverse)
    depth = N0.bit_length() - 1
    level_vec = levels[0]
    scales = jnp.exp2(level_vec.astype(jnp.float32)) / 8.0
    weight = jnp.where(jnp.sum(level_vec) % 2 == 0, 1.0, -1.0).astype(jnp.float32) / math.sqrt(
        lax.axis_size("grid")
    )
    keep = (jnp.asarray(level_rows) <= depth - 3 + level_vec[0]).astype(jnp.float32)[:, None, None]

    def evolve_rows(state):
        rows = state.shape[0]
        grid5 = state.reshape(rows, N1, N2, N3, N4)
        for _ in range(STEPS):
            extended = extended_2(grid5, (("slab", 0),), 1)
            grid5 = advance(extended, scales, 0)
        return grid5.reshape(rows, Q, N4)

    def hierarchise(whole):
        hier = jnp.dot(matrix, whole.reshape(N0, -1), precision=lax.Precision.HIGHEST)
        return weight * keep * hier.reshape(whole.shape)

    def reduce_terms(terms):
        return lax.psum_scatter(terms[owner], "grid", scatter_dimension=0, tiled=True)

    stepped = evolve_rows(field[0])
    summed = reduce_terms(hierarchise(regroup_rows(stepped)))
    ordered = lax.all_gather(summed, "grid", axis=0, tiled=True)
    position = jnp.zeros((N0,), jnp.int32).at[owner].set(jnp.arange(N0, dtype=jnp.int32))
    combined = ordered[position]
    masked = (keep * combined).reshape(N0, -1)
    nodal = jnp.dot(inverse, masked, precision=lax.Precision.HIGHEST).reshape(combined.shape)
    state = lax.all_to_all(nodal, "slab", split_axis=0, concat_axis=1, tiled=True)
    stepped = evolve_rows(state)
    summed = reduce_terms(hierarchise(regroup_rows(stepped)))
    return summed


VMEM = pl.BlockSpec(memory_space=pltpu.VMEM)
SMEM = pl.BlockSpec(memory_space=pltpu.SMEM)
HBM = pl.BlockSpec(memory_space=pltpu.HBM)
UNROLL = 2


def fill_tables(scales, left):
    size = TILES * N2
    squares = [value * value for value in scales]
    total = sum(scales[1:], scales[0])
    square = sum(squares[1:], squares[0])
    shape = (size, 2 * size)
    row = lax.broadcasted_iota(jnp.int32, shape, 0)
    column = lax.bitwise_and(lax.broadcasted_iota(jnp.int32, shape, 1), size - 1)
    drift = jnp.where(row == column, -total, 0.0)
    second = jnp.where(row == column, -2.0 * square, 0.0)
    for d, unit, count in ((1, N3 * N2, N1), (2, 1, N2), (3, N2, N3)):
        digit = lax.bitwise_and(lax.div(row, unit), count - 1)
        rest = row - digit * unit
        back = column == rest + lax.bitwise_and(digit + count - 1, count - 1) * unit
        ahead = column == rest + lax.bitwise_and(digit + 1, count - 1) * unit
        drift = drift + jnp.where(back, scales[d], 0.0)
        second = second + jnp.where(back, squares[d], 0.0) + jnp.where(ahead, squares[d], 0.0)
    left[:, : 2 * size] = jnp.concatenate([second, drift], axis=0).astype(jnp.bfloat16)
    drift = jnp.where(row == column, scales[0], 0.0)
    second = jnp.where(row == column, squares[0], 0.0)
    left[:, 2 * size :] = jnp.concatenate([second, drift], axis=0).astype(jnp.bfloat16)


def step_rows(src, dst, first, count, left, factors, products):
    q0, s4, q4 = factors
    size = TILES * N2

    def rows_of(group):
        return range(first + group * UNROLL, first + min(count, (group + 1) * UNROLL))

    def parts(row):
        value = src[row].reshape(size, N4)
        high = value.astype(jnp.bfloat16)
        return jnp.concatenate([high, (value - high.astype(jnp.float32)).astype(jnp.bfloat16)], axis=0)

    last = [parts(first - 1)]

    def multiply(group):
        held = [parts(row) for row in rows_of(group)]
        below = last + held
        last[:] = [held[-1]]
        held = [jnp.concatenate(pair, axis=0) for pair in zip(held, below)]
        products[group % 2][:, : len(held) * N4] = jnp.dot(
            left[...], jnp.concatenate(held, axis=1), preferred_element_type=jnp.float32
        )

    groups = -(-count // UNROLL)
    multiply(0)
    for group in range(groups):
        if group + 1 < groups:
            multiply(group + 1)
        product = products[group % 2]
        for i, row in enumerate(rows_of(group)):
            lanes = slice(i * N4, (i + 1) * N4)
            for t in range(TILES):
                u, above = src[row, t], src[row + 1, t]
                back, ahead = pltpu.roll(u, 1, 1), pltpu.roll(u, N4 - 1, 1)
                second = product[t * N2 : (t + 1) * N2, lanes] + q0 * above
                drift = product[size + t * N2 : size + (t + 1) * N2, lanes] + s4 * back
                second = second + q4 * (back + ahead)
                speed = ADVECT + (0.5 * ADVECT) * jnp.tanh(u)
                dst[row, t] = (u + DIFFUSE * second) + speed * drift


def interpolate(nodes, fine, middle):
    u0, u1, u2, u3, u4 = nodes
    v2 = jnp.where(middle, u2, 0.5 * (u0 + u4))
    v1 = jnp.where(fine, u1, 0.5 * (u0 + v2))
    v3 = jnp.where(fine, u3, 0.5 * (v2 + u4))
    return u0, v1, v2, v3


def spaces(rows):
    state = pltpu.VMEM((rows + LOW + HIGH, TILES, N2, N4), jnp.float32)
    product = pltpu.VMEM((2 * TILES * N2, UNROLL * N4), jnp.float32)
    return [state, state, product, product]


def run_steps(bufs, rows, left, scales):
    states, products = bufs[0:2], bufs[2:4]
    factors = (scales[0] * scales[0], scales[4], scales[4] * scales[4])
    for step in range(STEPS):
        count = rows + LOW + HIGH - 2 * (step + 1)
        step_rows(states[step % 2], states[(step + 1) % 2], step + 1, count, left, factors, products)
    return states[STEPS % 2]


def ends_kernel(field, last, first, sems):
    rows = field.shape[0]
    one = pltpu.make_async_copy(field.at[pl.ds(rows - LOW, LOW)], last, sems.at[0])
    two = pltpu.make_async_copy(field.at[pl.ds(0, HIGH)], first, sems.at[1])
    one.start()
    two.start()
    one.wait()
    two.wait()


def load_rows(ref, first, count, state, at):
    def body(i, carry):
        for n1 in range(N1):
            for n3 in range(N3):
                state[at + i, n1 * N3 + n3] = ref[first + i, pl.ds(n1 * N2 * N3 + n3, N2, stride=N3), :]
        return carry

    lax.fori_loop(0, count, body, 0)


def scales_of(level):
    return [lax.shift_left(1, level[0, d]).astype(jnp.float32) * 0.125 for d in range(5)]


def first_cycle(level, left, rows, outs, bufs):
    me, grids = lax.axis_index("grid"), lax.axis_size("grid")
    levels, scales = [level[0, d] for d in range(5)], scales_of(level)
    parity = lax.rem(levels[0] + levels[1] + levels[2] + levels[3] + levels[4], 2)
    weight = (1 - 2 * parity).astype(jnp.float32) * (1.0 / math.sqrt(grids))
    done = run_steps(bufs, rows, left, scales)
    fine, middle = levels[0] >= 3, levels[0] >= 2
    block = outs[0][1].shape[0] // TILES
    for first, out in outs:
        for quad in range(0, block, 4):
            base = LOW + first + quad
            for t in range(TILES):
                values = interpolate([done[base + i, t] for i in range(5)], fine, middle)
                for i, value in enumerate(values):
                    out[(quad + i) * TILES + t] = weight * value
        lane = lax.broadcasted_iota(jnp.int32, (N2, N4), 1)
        tile = jnp.zeros((N2, N4), jnp.float32)
        for d, value in enumerate(scales + [levels[0].astype(jnp.float32), weight]):
            tile = jnp.where(lane == d, value, tile)
        sublane = lax.broadcasted_iota(jnp.int32, (N2, N4), 0)
        out[block * TILES] = jnp.where(sublane == me, tile, 0.0)


def middle_kernel(level, field, middle, near, left, *bufs):
    rows = field.shape[0] // 2
    block = rows // 2
    fill_tables(scales_of(level), left)
    load_rows(field, block - LOW, rows + LOW + HIGH, bufs[0], 0)
    side = lax.div(2 * lax.axis_index("grid"), lax.axis_size("grid"))
    upper = lax.rem(side + lax.axis_index("slab"), 2) == 0
    first = jnp.where(upper, block, 0)
    first_cycle(level, left, rows, ((first, middle), (block - first, near)), bufs)


def outer_kernel(later, level, left, before, field, after, out, *bufs):
    total = field.shape[0]
    block = out.shape[0] // TILES
    top = lax.rem(lax.axis_index("grid") + lax.axis_index("slab") + later, 2) == 0

    @pl.when(top)
    def _():
        load_rows(field, total - block - LOW, block + LOW, bufs[0], 0)
        load_rows(after, 0, HIGH, bufs[0], block + LOW)

    @pl.when(jnp.logical_not(top))
    def _():
        load_rows(before, 0, LOW, bufs[0], 0)
        load_rows(field, 0, block + HIGH, bufs[0], LOW)

    first_cycle(level, left, block, ((0, out),), bufs)


def sent_value(own, g, d):
    return jnp.broadcast_to(own[own.shape[0] - 1, pl.ds(g, 1), d : d + 1], (1, N4))


def tables_kernel(grids, own, left):
    def grid(g, carry):
        fill_tables([sent_value(own, g, d) for d in range(5)], left.at[g])
        return carry

    lax.fori_loop(0, grids, grid, 0)


def second_kernel(rows, grids, left, before, own, after, *refs):
    outs, total, bufs = refs[:-5], refs[-5], refs[-4:]
    extent = rows + LOW + HIGH

    def given(row, t):
        if row < LOW:
            return before[row * TILES + t]
        if row < LOW + rows:
            return own[(row - LOW) * TILES + t]
        return after[(row - LOW - rows) * TILES + t]

    total[...] = jnp.zeros_like(total)

    def grid(g, carry):
        tile = lambda d: jnp.broadcast_to(sent_value(own, g, d), (N2, N4))
        fine, middle, weight = tile(5) > 2.5, tile(5) > 1.5, tile(6)
        start = bufs[0]
        for quad in range(0, extent - 1, 4):
            for t in range(TILES):
                values = interpolate([given(quad + i, t) for i in range(5)], fine, middle)
                for i, value in enumerate(values):
                    start[quad + i, t] = value
        for t in range(TILES):
            start[extent - 1, t] = given(extent - 1, t)
        done = run_steps(bufs, rows, left.at[g], [tile(d) for d in range(5)])
        for quad in range(0, rows, 4):
            for t in range(TILES):
                values = interpolate([done[LOW + quad + i, t] for i in range(5)], fine, middle)
                for i, value in enumerate(values):
                    at = pl.ds(((quad + i) * TILES + t) * N2, N2)
                    total[at, :] = weight * value + total[at, :]
        return carry

    lax.fori_loop(0, grids, grid, 0)
    half = N2 // 2
    for d, out in enumerate(outs):
        slab = lax.bitwise_xor(lax.axis_index("slab"), d)
        first = lax.div(slab, 2) * (N3 * N2) + lax.rem(slab, 2) * half
        for n3 in range(N3):
            for n in range(half):
                out[n3, n] = total[pl.ds(first + n3 * N2 + n, rows, stride=TILES * N2), :]


def regroup_kernel(groups, *refs):
    received, outs = refs[: len(refs) // 2], refs[len(refs) // 2 :]
    me = lax.axis_index("grid")
    for e, out in enumerate(outs):
        for d, ref in enumerate(received):
            out[d] = ref[lax.rem(me + e, groups)]


def hier_kernel(groups, matrix, *refs):
    received, outs = refs[:groups], refs[groups:]
    me = lax.axis_index("grid")
    lanes = received[0].shape[3]
    count = matrix.shape[0] // groups
    for n in range(received[0].shape[1]):
        whole = jnp.concatenate([ref[:, n].reshape(-1, lanes) for ref in received], axis=0)
        high = whole.astype(jnp.bfloat16)
        rest = (whole - high.astype(jnp.float32)).astype(jnp.bfloat16)
        for d, out in enumerate(outs):
            part = matrix[pl.ds(lax.rem(me + d, groups) * count, count), :]
            out[n] = jnp.dot(part, high, preferred_element_type=jnp.float32) + jnp.dot(
                part, rest, preferred_element_type=jnp.float32
            )


def place_kernel(groups, *refs):
    received, out = refs[:-1], refs[-1]
    me = lax.axis_index("grid")
    parts, count = received[0].shape[0], received[0].shape[1]
    for d, ref in enumerate(received):
        n3 = lax.rem(me + groups - d, groups)
        for n in range(parts):
            out[pl.ds(n * N3 + n3, count, stride=parts * N3), :] = ref[n]


def kernel(body, out_shape, in_specs, scratch=(), limit=4, flops=0):
    single = not isinstance(out_shape, (list, tuple))
    return pl.pallas_call(
        body,
        out_shape=out_shape,
        in_specs=in_specs,
        out_specs=VMEM if single else [VMEM] * len(out_shape),
        scratch_shapes=list(scratch),
        compiler_params=pltpu.CompilerParams(vmem_limit_bytes=limit << 20),
        cost_estimate=pl.CostEstimate(flops=flops, bytes_accessed=1 << 20, transcendentals=flops // 30),
    )


def fast_sizes(grids, slabs):
    rows = N0 // slabs
    return rows, rows // grids


def fast_fits(grids, slabs):
    _, block = fast_sizes(grids, slabs)
    return grids == 4 and grids == N3 and slabs == 2 * N1 and block >= HIGH and block % 4 == 0


def floats(*shape):
    return jax.ShapeDtypeStruct(shape, jnp.float32)


def local_fast(field, levels, owner):
    grids, slabs = lax.axis_size("grid"), lax.axis_size("slab")
    rows, block = fast_sizes(grids, slabs)
    state = field[0]

    up = [(i, (i + 1) % slabs) for i in range(slabs)]
    down = [(j, i) for i, j in up]
    last, first = kernel(
        ends_kernel,
        [floats(LOW, Q, N4), floats(HIGH, Q, N4)],
        [HBM],
        [pltpu.SemaphoreType.DMA((2,))],
    )(pltpu.with_memory_space_constraint(state, pltpu.HBM))
    before = lax.ppermute(last, "slab", up)
    after = lax.ppermute(first, "slab", down)

    piece = floats(block * TILES + 1, N2, N4)
    work = 8192 * 40
    size = 2 * TILES * N2

    def table(*lead):
        return jax.ShapeDtypeStruct(lead + (size, 2 * size), jnp.bfloat16)

    middle, near, left = kernel(
        middle_kernel,
        [piece, piece, table()],
        [SMEM, VMEM],
        spaces(rows // 2),
        limit=6,
        flops=80 * work,
    )(levels, state)

    ready = lax.optimization_barrier((before, after, middle))

    def outer_block(later):
        return kernel(
            functools.partial(outer_kernel, later),
            piece,
            [SMEM] + [VMEM] * 4,
            spaces(block),
            limit=6,
            flops=48 * work,
        )(levels, left, ready[0], state, ready[1])

    edge = (lax.axis_index("grid") == 0) | (lax.axis_index("grid") == grids - 1)
    across = lax.ppermute(middle, "grid", [(1, 2), (2, 1)])
    first_out = outer_block(0)
    swapped = lax.ppermute(first_out, "grid", [(0, 1), (1, 0), (2, 3), (3, 2)])
    middle, near, _ = lax.optimization_barrier((middle, near, first_out))
    skipped = lax.ppermute(middle, "grid", [(0, 2), (3, 1)])
    inwards = lax.ppermute(near, "grid", [(0, 1), (3, 2)])
    second_out = outer_block(1)
    joined = swapped + second_out
    passed = lax.ppermute(joined, "grid", [(1, 3), (2, 0)])
    own = jnp.where(edge, joined, near) + across + skipped + inwards + passed

    chain = []
    for k in range(slabs):
        chain += [(g if k % 2 == 0 else grids - 1 - g) * slabs + k for g in range(grids)]
    forward = [(chain[i], chain[(i + 1) % len(chain)]) for i in range(len(chain))]
    backward = [(j, i) for i, j in forward]
    both = ("grid", "slab")
    before = lax.ppermute(own[(block - LOW) * TILES : block * TILES], both, forward)
    after = lax.ppermute(own[: HIGH * TILES], both, backward)

    left = kernel(
        functools.partial(tables_kernel, grids), table(grids), [VMEM], flops=30 * work
    )(own)
    half = N2 // 2
    sent = kernel(
        functools.partial(second_kernel, block, grids),
        [floats(N3, half, block, N4)] * slabs,
        [VMEM] * 4,
        [pltpu.VMEM((block * TILES * N2, N4), jnp.float32)] + spaces(block),
        limit=8,
        flops=400 * 8192 * 40,
    )(left, before, own, after)

    def shared(values, axis, partner):
        members = range(lax.axis_size(axis))
        others = lax.optimization_barrier(tuple(values[1:]))
        return [values[0]] + [
            lax.ppermute(value, axis, [(i, partner(i, d)) for i in members]) for d, value in enumerate(others, 1)
        ]

    ahead = lambda i, d: (i + d) % grids
    by_slab = shared(sent, "slab", lambda i, d: i ^ d)
    ready = kernel(
        functools.partial(regroup_kernel, grids),
        [floats(slabs, half, block, N4)] * grids,
        [VMEM] * slabs,
    )(*by_slab)
    by_grid = shared(ready, "grid", ahead)

    me, at = lax.axis_index("grid"), lax.axis_index("slab")
    place = jnp.arange(N0, dtype=jnp.int32)
    source = (me - place // (slabs * block)) % grids
    slab = at ^ (place // block % slabs)
    source = jnp.where(slab % 2 == 0, source, grids - 1 - source)
    column = ((slab * grids + source) * block + place % block)[None, :]
    row = owner[:, None]
    reach = jnp.where(row > 0, row & -row, 0)
    half_of = jnp.where(row > 0, -0.5, 0.0)
    matrix = (
        (column == row).astype(jnp.float32)
        + half_of * (column == row - reach)
        + half_of * (column == (row + reach) % N0)
    ).astype(jnp.bfloat16)
    group = N0 // grids
    hier = kernel(
        functools.partial(hier_kernel, grids),
        [floats(half, group, N4)] * grids,
        [VMEM] * (1 + grids),
    )(matrix, *by_grid)
    received = shared(hier, "grid", ahead)
    out = kernel(
        functools.partial(place_kernel, grids), floats(group * half * N3, N4), [VMEM] * grids
    )(*received)
    return out.reshape(group, Q // slabs, N4)


def local(field, levels, owner):
    if fast_fits(lax.axis_size("grid"), lax.axis_size("slab")):
        return local_fast(field, levels, owner)
    return local_general(field, levels, owner)


def solution(mesh):
    in_specs = (P(("copies", "grid"), "slab", None, None), P(("copies", "grid"), None), P("copies"))
    out_specs = P(("copies", "grid"), "slab", None)
    return jax.shard_map(local, mesh=mesh, in_specs=in_specs, out_specs=out_specs, check_vma=False)
```

```python
import functools
import math

import jax
import jax.numpy as jnp
import numpy as np
from jax import lax
from jax.experimental import pallas as pl
from jax.experimental.pallas import tpu as pltpu
from jax.sharding import PartitionSpec as P


N0 = 128
N1 = 2
N2 = 8
N3 = 4
N4 = 128
STEPS = 4
Q = 64

ADVECT = 0.08
DIFFUSE = 0.03

LOW = STEPS
HIGH = STEPS + 1
TILES = N1 * N3


def extended_2(value, sides, width):
    for axis, dim in sides:
        count, length = (lax.axis_size(axis), value.shape[dim])
        up = [(i, (i + 1) % count) for i in range(count)]
        down = [(j, i) for i, j in up]
        last = lax.slice_in_dim(value, length - width, length, axis=dim)
        first = lax.slice_in_dim(value, 0, width, axis=dim)
        before = lax.ppermute(last, axis, up)
        after = lax.ppermute(first, axis, down)
        value = jnp.concatenate([before, value, after], axis=dim)
    return value


def build_tables(count):
    depth = count.bit_length() - 1
    matrix = np.eye(count)
    inverse = np.zeros((count, count))
    inverse[0, 0] = 1.0
    level_rows = np.zeros(count, np.int32)
    for index in range(1, count):
        zeros = (index & -index).bit_length() - 1
        spacing = 1 << zeros
        matrix[index, index - spacing] -= 0.5
        matrix[index, (index + spacing) % count] -= 0.5
        level_rows[index] = depth - zeros
    for zeros in range(depth - 1, -1, -1):
        spacing = 1 << zeros
        for index in range(spacing, count, 2 * spacing):
            inverse[index] = 0.5 * (inverse[index - spacing] + inverse[(index + spacing) % count])
            inverse[index, index] += 1.0
    return (matrix.astype(np.float32), inverse.astype(np.float32), level_rows)


def advance(extended, scales, padded):
    length = extended.shape[padded] - 2
    centre = lax.slice_in_dim(extended, 1, length + 1, axis=padded)
    speed = 1.0 + 0.5 * jnp.tanh(centre)
    change = jnp.zeros_like(centre)
    for axis in range(5):
        if axis == padded:
            back = lax.slice_in_dim(extended, 0, length, axis=padded)
            ahead = lax.slice_in_dim(extended, 2, length + 2, axis=padded)
        else:
            back = jnp.roll(centre, 1, axis)
            ahead = jnp.roll(centre, -1, axis)
        change = (
            change
            - ADVECT * scales[axis] * speed * (centre - back)
            + DIFFUSE * scales[axis] ** 2 * (ahead - 2.0 * centre + back)
        )
    return centre + change


def regroup_rows(stepped):
    return lax.all_to_all(stepped, "slab", split_axis=1, concat_axis=0, tiled=True)


def local_general(field, levels, owner):
    matrix, inverse, level_rows = build_tables(N0)
    matrix = jnp.asarray(matrix)
    inverse = jnp.asarray(inverse)
    depth = N0.bit_length() - 1
    level_vec = levels[0]
    scales = jnp.exp2(level_vec.astype(jnp.float32)) / 8.0
    weight = jnp.where(jnp.sum(level_vec) % 2 == 0, 1.0, -1.0).astype(jnp.float32) / math.sqrt(
        lax.axis_size("grid")
    )
    keep = (jnp.asarray(level_rows) <= depth - 3 + level_vec[0]).astype(jnp.float32)[:, None, None]

    def evolve_rows(state):
        rows = state.shape[0]
        grid5 = state.reshape(rows, N1, N2, N3, N4)
        for _ in range(STEPS):
            extended = extended_2(grid5, (("slab", 0),), 1)
            grid5 = advance(extended, scales, 0)
        return grid5.reshape(rows, Q, N4)

    def hierarchise(whole):
        hier = jnp.dot(matrix, whole.reshape(N0, -1), precision=lax.Precision.HIGHEST)
        return weight * keep * hier.reshape(whole.shape)

    def reduce_terms(terms):
        return lax.psum_scatter(terms[owner], "grid", scatter_dimension=0, tiled=True)

    stepped = evolve_rows(field[0])
    summed = reduce_terms(hierarchise(regroup_rows(stepped)))
    ordered = lax.all_gather(summed, "grid", axis=0, tiled=True)
    position = jnp.zeros((N0,), jnp.int32).at[owner].set(jnp.arange(N0, dtype=jnp.int32))
    combined = ordered[position]
    masked = (keep * combined).reshape(N0, -1)
    nodal = jnp.dot(inverse, masked, precision=lax.Precision.HIGHEST).reshape(combined.shape)
    state = lax.all_to_all(nodal, "slab", split_axis=0, concat_axis=1, tiled=True)
    stepped = evolve_rows(state)
    summed = reduce_terms(hierarchise(regroup_rows(stepped)))
    return summed


VMEM = pl.BlockSpec(memory_space=pltpu.VMEM)
SMEM = pl.BlockSpec(memory_space=pltpu.SMEM)
HBM = pl.BlockSpec(memory_space=pltpu.HBM)
UNROLL = 2


def fill_tables(scales, left):
    size = TILES * N2
    squares = [value * value for value in scales]
    total = sum(scales[1:], scales[0])
    square = sum(squares[1:], squares[0])
    shape = (size, 2 * size)
    row = lax.broadcasted_iota(jnp.int32, shape, 0)
    column = lax.bitwise_and(lax.broadcasted_iota(jnp.int32, shape, 1), size - 1)
    drift = jnp.where(row == column, -total, 0.0)
    second = jnp.where(row == column, -2.0 * square, 0.0)
    for d, unit, count in ((1, N3 * N2, N1), (2, 1, N2), (3, N2, N3)):
        digit = lax.bitwise_and(lax.div(row, unit), count - 1)
        rest = row - digit * unit
        back = column == rest + lax.bitwise_and(digit + count - 1, count - 1) * unit
        ahead = column == rest + lax.bitwise_and(digit + 1, count - 1) * unit
        drift = drift + jnp.where(back, scales[d], 0.0)
        second = second + jnp.where(back, squares[d], 0.0) + jnp.where(ahead, squares[d], 0.0)
    left[:, : 2 * size] = jnp.concatenate([second, drift], axis=0).astype(jnp.bfloat16)
    drift = jnp.where(row == column, scales[0], 0.0)
    second = jnp.where(row == column, squares[0], 0.0)
    left[:, 2 * size :] = jnp.concatenate([second, drift], axis=0).astype(jnp.bfloat16)


def step_rows(src, dst, first, count, left, factors, products):
    q0, s4, q4 = factors
    size = TILES * N2

    def rows_of(group):
        return range(first + group * UNROLL, first + min(count, (group + 1) * UNROLL))

    def parts(row):
        value = src[row].reshape(size, N4)
        high = value.astype(jnp.bfloat16)
        return jnp.concatenate([high, (value - high.astype(jnp.float32)).astype(jnp.bfloat16)], axis=0)

    last = [parts(first - 1)]

    def multiply(group):
        held = [parts(row) for row in rows_of(group)]
        below = last + held
        last[:] = [held[-1]]
        held = [jnp.concatenate(pair, axis=0) for pair in zip(held, below)]
        products[group % 2][:, : len(held) * N4] = jnp.dot(
            left[...], jnp.concatenate(held, axis=1), preferred_element_type=jnp.float32
        )

    groups = -(-count // UNROLL)
    multiply(0)
    for group in range(groups):
        if group + 1 < groups:
            multiply(group + 1)
        product = products[group % 2]
        for i, row in enumerate(rows_of(group)):
            lanes = slice(i * N4, (i + 1) * N4)
            for t in range(TILES):
                u, above = src[row, t], src[row + 1, t]
                back, ahead = pltpu.roll(u, 1, 1), pltpu.roll(u, N4 - 1, 1)
                second = product[t * N2 : (t + 1) * N2, lanes] + q0 * above
                drift = product[size + t * N2 : size + (t + 1) * N2, lanes] + s4 * back
                second = second + q4 * (back + ahead)
                speed = ADVECT + (0.5 * ADVECT) * jnp.tanh(u)
                dst[row, t] = (u + DIFFUSE * second) + speed * drift


def interpolate(nodes, fine, middle):
    u0, u1, u2, u3, u4 = nodes
    v2 = jnp.where(middle, u2, 0.5 * (u0 + u4))
    v1 = jnp.where(fine, u1, 0.5 * (u0 + v2))
    v3 = jnp.where(fine, u3, 0.5 * (v2 + u4))
    return u0, v1, v2, v3


def spaces(rows):
    state = pltpu.VMEM((rows + LOW + HIGH, TILES, N2, N4), jnp.float32)
    product = pltpu.VMEM((2 * TILES * N2, UNROLL * N4), jnp.float32)
    return [state, state, product, product]


def run_steps(bufs, rows, left, scales):
    states, products = bufs[0:2], bufs[2:4]
    factors = (scales[0] * scales[0], scales[4], scales[4] * scales[4])
    for step in range(STEPS):
        count = rows + LOW + HIGH - 2 * (step + 1)
        step_rows(states[step % 2], states[(step + 1) % 2], step + 1, count, left, factors, products)
    return states[STEPS % 2]


def ends_kernel(field, last, first, sems):
    rows = field.shape[0]
    one = pltpu.make_async_copy(field.at[pl.ds(rows - LOW, LOW)], last, sems.at[0])
    two = pltpu.make_async_copy(field.at[pl.ds(0, HIGH)], first, sems.at[1])
    one.start()
    two.start()
    one.wait()
    two.wait()


def load_rows(ref, first, count, state, at):
    def body(i, carry):
        for n1 in range(N1):
            for n3 in range(N3):
                state[at + i, n1 * N3 + n3] = ref[first + i, pl.ds(n1 * N2 * N3 + n3, N2, stride=N3), :]
        return carry

    lax.fori_loop(0, count, body, 0)


def scales_of(level):
    return [lax.shift_left(1, level[0, d]).astype(jnp.float32) * 0.125 for d in range(5)]


def first_cycle(level, left, rows, outs, bufs):
    me, grids = lax.axis_index("grid"), lax.axis_size("grid")
    levels, scales = [level[0, d] for d in range(5)], scales_of(level)
    parity = lax.rem(levels[0] + levels[1] + levels[2] + levels[3] + levels[4], 2)
    weight = (1 - 2 * parity).astype(jnp.float32) * (1.0 / math.sqrt(grids))
    done = run_steps(bufs, rows, left, scales)
    fine, middle = levels[0] >= 3, levels[0] >= 2
    block = outs[0][1].shape[0] // TILES
    for first, out in outs:
        for quad in range(0, block, 4):
            base = LOW + first + quad
            for t in range(TILES):
                values = interpolate([done[base + i, t] for i in range(5)], fine, middle)
                for i, value in enumerate(values):
                    out[(quad + i) * TILES + t] = weight * value
        lane = lax.broadcasted_iota(jnp.int32, (N2, N4), 1)
        tile = jnp.zeros((N2, N4), jnp.float32)
        for d, value in enumerate(scales + [levels[0].astype(jnp.float32), weight]):
            tile = jnp.where(lane == d, value, tile)
        sublane = lax.broadcasted_iota(jnp.int32, (N2, N4), 0)
        out[block * TILES] = jnp.where(sublane == me, tile, 0.0)


def middle_kernel(level, field, middle, near, left, *bufs):
    rows = field.shape[0] // 2
    block = rows // 2
    fill_tables(scales_of(level), left)
    load_rows(field, block - LOW, rows + LOW + HIGH, bufs[0], 0)
    side = lax.div(2 * lax.axis_index("grid"), lax.axis_size("grid"))
    upper = lax.rem(side + lax.axis_index("slab"), 2) == 0
    first = jnp.where(upper, block, 0)
    first_cycle(level, left, rows, ((first, middle), (block - first, near)), bufs)


def outer_kernel(later, level, left, before, field, after, out, *bufs):
    total = field.shape[0]
    block = out.shape[0] // TILES
    top = lax.rem(lax.axis_index("grid") + lax.axis_index("slab") + later, 2) == 0

    @pl.when(top)
    def _():
        load_rows(field, total - block - LOW, block + LOW, bufs[0], 0)
        load_rows(after, 0, HIGH, bufs[0], block + LOW)

    @pl.when(jnp.logical_not(top))
    def _():
        load_rows(before, 0, LOW, bufs[0], 0)
        load_rows(field, 0, block + HIGH, bufs[0], LOW)

    first_cycle(level, left, block, ((0, out),), bufs)


def sent_value(own, g, d):
    return jnp.broadcast_to(own[own.shape[0] - 1, pl.ds(g, 1), d : d + 1], (1, N4))


def tables_kernel(grids, own, left):
    def grid(g, carry):
        fill_tables([sent_value(own, g, d) for d in range(5)], left.at[g])
        return carry

    lax.fori_loop(0, grids, grid, 0)


def second_kernel(rows, grids, left, before, own, after, *refs):
    outs, total, bufs = refs[:-5], refs[-5], refs[-4:]
    extent = rows + LOW + HIGH

    def given(row, t):
        if row < LOW:
            return before[row * TILES + t]
        if row < LOW + rows:
            return own[(row - LOW) * TILES + t]
        return after[(row - LOW - rows) * TILES + t]

    total[...] = jnp.zeros_like(total)

    def grid(g, carry):
        tile = lambda d: jnp.broadcast_to(sent_value(own, g, d), (N2, N4))
        fine, middle, weight = tile(5) > 2.5, tile(5) > 1.5, tile(6)
        start = bufs[0]
        for quad in range(0, extent - 1, 4):
            for t in range(TILES):
                values = interpolate([given(quad + i, t) for i in range(5)], fine, middle)
                for i, value in enumerate(values):
                    start[quad + i, t] = value
        for t in range(TILES):
            start[extent - 1, t] = given(extent - 1, t)
        done = run_steps(bufs, rows, left.at[g], [tile(d) for d in range(5)])
        for quad in range(0, rows, 4):
            for t in range(TILES):
                values = interpolate([done[LOW + quad + i, t] for i in range(5)], fine, middle)
                for i, value in enumerate(values):
                    at = pl.ds(((quad + i) * TILES + t) * N2, N2)
                    total[at, :] = weight * value + total[at, :]
        return carry

    lax.fori_loop(0, grids, grid, 0)
    half = N2 // 2
    for d, out in enumerate(outs):
        slab = lax.bitwise_xor(lax.axis_index("slab"), d)
        first = lax.div(slab, 2) * (N3 * N2) + lax.rem(slab, 2) * half
        for n3 in range(N3):
            for n in range(half):
                out[n3, n] = total[pl.ds(first + n3 * N2 + n, rows, stride=TILES * N2), :]


def regroup_kernel(groups, *refs):
    received, outs = refs[:-groups], refs[-groups:]
    me = lax.axis_index("grid")
    for e, out in enumerate(outs):
        for d, ref in enumerate(received):
            out[d] = ref[lax.rem(me + e, groups)]


def hier_kernel(groups, matrix, *refs):
    received, outs = refs[: 2 * groups], refs[2 * groups :]
    me = lax.axis_index("grid")
    lanes = received[0].shape[3]
    count = matrix.shape[0] // groups
    for n in range(received[0].shape[1]):
        pairs = [(received[d], received[groups + d]) for d in range(groups)]
        whole = jnp.concatenate([ref[:, n].reshape(-1, lanes) for pair in pairs for ref in pair], axis=0)
        high = whole.astype(jnp.bfloat16)
        rest = (whole - high.astype(jnp.float32)).astype(jnp.bfloat16)
        for d, out in enumerate(outs):
            part = matrix[pl.ds(lax.rem(me + d, groups) * count, count), :]
            out[n] = jnp.dot(part, high, preferred_element_type=jnp.float32) + jnp.dot(
                part, rest, preferred_element_type=jnp.float32
            )


def place_kernel(groups, *refs):
    received, out = refs[:-1], refs[-1]
    me = lax.axis_index("grid")
    parts, count = received[0].shape[0], received[0].shape[1]
    for d, ref in enumerate(received):
        n3 = lax.rem(me + groups - d, groups)
        for n in range(parts):
            out[pl.ds(n * N3 + n3, count, stride=parts * N3), :] = ref[n]


def kernel(body, out_shape, in_specs, scratch=(), limit=4, flops=0):
    single = not isinstance(out_shape, (list, tuple))
    return pl.pallas_call(
        body,
        out_shape=out_shape,
        in_specs=in_specs,
        out_specs=VMEM if single else [VMEM] * len(out_shape),
        scratch_shapes=list(scratch),
        compiler_params=pltpu.CompilerParams(vmem_limit_bytes=limit << 20),
        cost_estimate=pl.CostEstimate(flops=flops, bytes_accessed=1 << 20, transcendentals=flops // 30),
    )


def fast_sizes(grids, slabs):
    rows = N0 // slabs
    return rows, rows // grids


def fast_fits(grids, slabs):
    _, block = fast_sizes(grids, slabs)
    return grids == 4 and grids == N3 and slabs == 2 * N1 and block >= HIGH and block % 4 == 0


def floats(*shape):
    return jax.ShapeDtypeStruct(shape, jnp.float32)


def local_fast(field, levels, owner):
    grids, slabs = lax.axis_size("grid"), lax.axis_size("slab")
    rows, block = fast_sizes(grids, slabs)
    state = field[0]

    up = [(i, (i + 1) % slabs) for i in range(slabs)]
    down = [(j, i) for i, j in up]
    last, first = kernel(
        ends_kernel,
        [floats(LOW, Q, N4), floats(HIGH, Q, N4)],
        [HBM],
        [pltpu.SemaphoreType.DMA((2,))],
    )(pltpu.with_memory_space_constraint(state, pltpu.HBM))
    before = lax.ppermute(last, "slab", up)
    after = lax.ppermute(first, "slab", down)

    piece = floats(block * TILES + 1, N2, N4)
    work = 8192 * 40
    size = 2 * TILES * N2

    def table(*lead):
        return jax.ShapeDtypeStruct(lead + (size, 2 * size), jnp.bfloat16)

    middle, near, left = kernel(
        middle_kernel,
        [piece, piece, table()],
        [SMEM, VMEM],
        spaces(rows // 2),
        limit=6,
        flops=80 * work,
    )(levels, state)

    ready = lax.optimization_barrier((before, after, middle))

    def outer_block(later):
        return kernel(
            functools.partial(outer_kernel, later),
            piece,
            [SMEM] + [VMEM] * 4,
            spaces(block),
            limit=6,
            flops=48 * work,
        )(levels, left, ready[0], state, ready[1])

    edge = (lax.axis_index("grid") == 0) | (lax.axis_index("grid") == grids - 1)
    across = lax.ppermute(middle, "grid", [(1, 2), (2, 1)])
    first_out = outer_block(0)
    swapped = lax.ppermute(first_out, "grid", [(0, 1), (1, 0), (2, 3), (3, 2)])
    middle, near, _ = lax.optimization_barrier((middle, near, first_out))
    skipped = lax.ppermute(middle, "grid", [(0, 2), (3, 1)])
    inwards = lax.ppermute(near, "grid", [(0, 1), (3, 2)])
    second_out = outer_block(1)
    joined = swapped + second_out
    passed = lax.ppermute(joined, "grid", [(1, 3), (2, 0)])
    own = jnp.where(edge, joined, near) + across + skipped + inwards + passed

    chain = []
    for k in range(slabs):
        chain += [(g if k % 2 == 0 else grids - 1 - g) * slabs + k for g in range(grids)]
    forward = [(chain[i], chain[(i + 1) % len(chain)]) for i in range(len(chain))]
    backward = [(j, i) for i, j in forward]
    both = ("grid", "slab")
    before = lax.ppermute(own[(block - LOW) * TILES : block * TILES], both, forward)
    after = lax.ppermute(own[: HIGH * TILES], both, backward)

    left = kernel(
        functools.partial(tables_kernel, grids), table(grids), [VMEM], flops=30 * work
    )(own)
    half = N2 // 2
    sent = kernel(
        functools.partial(second_kernel, block, grids),
        [floats(N3, half, block, N4)] * slabs,
        [VMEM] * 4,
        [pltpu.VMEM((block * TILES * N2, N4), jnp.float32)] + spaces(block),
        limit=8,
        flops=400 * 8192 * 40,
    )(left, before, own, after)

    def exchanged(value, axis, partner, d):
        pairs = [(i, partner(i, d)) for i in range(lax.axis_size(axis))]
        return lax.ppermute(value, axis, pairs)

    other = lambda i, d: i ^ d
    ahead = lambda i, d: (i + d) % grids
    far_parts = [exchanged(sent[d], "slab", other, d) for d in (2, 3)]
    near_parts = [sent[0], exchanged(sent[1], "slab", other, 1)]
    by_grid = []
    for parts in (near_parts, far_parts):
        ready = kernel(
            functools.partial(regroup_kernel, grids),
            [floats(len(parts), half, block, N4)] * grids,
            [VMEM] * len(parts),
        )(*parts)
        by_grid += [ready[0]] + [exchanged(ready[d], "grid", ahead, d) for d in range(1, grids)]

    me, at = lax.axis_index("grid"), lax.axis_index("slab")
    place = jnp.arange(N0, dtype=jnp.int32)
    source = (me - place // (slabs * block)) % grids
    slab = at ^ (place // block % slabs)
    source = jnp.where(slab % 2 == 0, source, grids - 1 - source)
    column = ((slab * grids + source) * block + place % block)[None, :]
    row = owner[:, None]
    reach = jnp.where(row > 0, row & -row, 0)
    half_of = jnp.where(row > 0, -0.5, 0.0)
    matrix = (
        (column == row).astype(jnp.float32)
        + half_of * (column == row - reach)
        + half_of * (column == (row + reach) % N0)
    ).astype(jnp.bfloat16)
    group = N0 // grids
    hier = kernel(
        functools.partial(hier_kernel, grids),
        [floats(half, group, N4)] * grids,
        [VMEM] * (1 + 2 * grids),
    )(matrix, *by_grid)
    received = [hier[0]] + [exchanged(hier[d], "grid", ahead, d) for d in range(1, grids)]
    out = kernel(
        functools.partial(place_kernel, grids), floats(group * half * N3, N4), [VMEM] * grids
    )(*received)
    return out.reshape(group, Q // slabs, N4)


def local(field, levels, owner):
    if fast_fits(lax.axis_size("grid"), lax.axis_size("slab")):
        return local_fast(field, levels, owner)
    return local_general(field, levels, owner)


def solution(mesh):
    in_specs = (P(("copies", "grid"), "slab", None, None), P(("copies", "grid"), None), P("copies"))
    out_specs = P(("copies", "grid"), "slab", None)
    return jax.shard_map(local, mesh=mesh, in_specs=in_specs, out_specs=out_specs, check_vma=False)
```

```python
import functools
import math

import jax
import jax.numpy as jnp
import numpy as np
from jax import lax
from jax.experimental import pallas as pl
from jax.experimental.pallas import tpu as pltpu
from jax.sharding import PartitionSpec as P


N0 = 128
N1 = 2
N2 = 8
N3 = 4
N4 = 128
STEPS = 4
Q = 64

ADVECT = 0.08
DIFFUSE = 0.03

LOW = STEPS
HIGH = STEPS + 1
TILES = N1 * N3


def extended_2(value, sides, width):
    for axis, dim in sides:
        count, length = (lax.axis_size(axis), value.shape[dim])
        up = [(i, (i + 1) % count) for i in range(count)]
        down = [(j, i) for i, j in up]
        last = lax.slice_in_dim(value, length - width, length, axis=dim)
        first = lax.slice_in_dim(value, 0, width, axis=dim)
        before = lax.ppermute(last, axis, up)
        after = lax.ppermute(first, axis, down)
        value = jnp.concatenate([before, value, after], axis=dim)
    return value


def build_tables(count):
    depth = count.bit_length() - 1
    matrix = np.eye(count)
    inverse = np.zeros((count, count))
    inverse[0, 0] = 1.0
    level_rows = np.zeros(count, np.int32)
    for index in range(1, count):
        zeros = (index & -index).bit_length() - 1
        spacing = 1 << zeros
        matrix[index, index - spacing] -= 0.5
        matrix[index, (index + spacing) % count] -= 0.5
        level_rows[index] = depth - zeros
    for zeros in range(depth - 1, -1, -1):
        spacing = 1 << zeros
        for index in range(spacing, count, 2 * spacing):
            inverse[index] = 0.5 * (inverse[index - spacing] + inverse[(index + spacing) % count])
            inverse[index, index] += 1.0
    return (matrix.astype(np.float32), inverse.astype(np.float32), level_rows)


def advance(extended, scales, padded):
    length = extended.shape[padded] - 2
    centre = lax.slice_in_dim(extended, 1, length + 1, axis=padded)
    speed = 1.0 + 0.5 * jnp.tanh(centre)
    change = jnp.zeros_like(centre)
    for axis in range(5):
        if axis == padded:
            back = lax.slice_in_dim(extended, 0, length, axis=padded)
            ahead = lax.slice_in_dim(extended, 2, length + 2, axis=padded)
        else:
            back = jnp.roll(centre, 1, axis)
            ahead = jnp.roll(centre, -1, axis)
        change = (
            change
            - ADVECT * scales[axis] * speed * (centre - back)
            + DIFFUSE * scales[axis] ** 2 * (ahead - 2.0 * centre + back)
        )
    return centre + change


def regroup_rows(stepped):
    return lax.all_to_all(stepped, "slab", split_axis=1, concat_axis=0, tiled=True)


def local_general(field, levels, owner):
    matrix, inverse, level_rows = build_tables(N0)
    matrix = jnp.asarray(matrix)
    inverse = jnp.asarray(inverse)
    depth = N0.bit_length() - 1
    level_vec = levels[0]
    scales = jnp.exp2(level_vec.astype(jnp.float32)) / 8.0
    weight = jnp.where(jnp.sum(level_vec) % 2 == 0, 1.0, -1.0).astype(jnp.float32) / math.sqrt(
        lax.axis_size("grid")
    )
    keep = (jnp.asarray(level_rows) <= depth - 3 + level_vec[0]).astype(jnp.float32)[:, None, None]

    def evolve_rows(state):
        rows = state.shape[0]
        grid5 = state.reshape(rows, N1, N2, N3, N4)
        for _ in range(STEPS):
            extended = extended_2(grid5, (("slab", 0),), 1)
            grid5 = advance(extended, scales, 0)
        return grid5.reshape(rows, Q, N4)

    def hierarchise(whole):
        hier = jnp.dot(matrix, whole.reshape(N0, -1), precision=lax.Precision.HIGHEST)
        return weight * keep * hier.reshape(whole.shape)

    def reduce_terms(terms):
        return lax.psum_scatter(terms[owner], "grid", scatter_dimension=0, tiled=True)

    stepped = evolve_rows(field[0])
    summed = reduce_terms(hierarchise(regroup_rows(stepped)))
    ordered = lax.all_gather(summed, "grid", axis=0, tiled=True)
    position = jnp.zeros((N0,), jnp.int32).at[owner].set(jnp.arange(N0, dtype=jnp.int32))
    combined = ordered[position]
    masked = (keep * combined).reshape(N0, -1)
    nodal = jnp.dot(inverse, masked, precision=lax.Precision.HIGHEST).reshape(combined.shape)
    state = lax.all_to_all(nodal, "slab", split_axis=0, concat_axis=1, tiled=True)
    stepped = evolve_rows(state)
    summed = reduce_terms(hierarchise(regroup_rows(stepped)))
    return summed


VMEM = pl.BlockSpec(memory_space=pltpu.VMEM)
SMEM = pl.BlockSpec(memory_space=pltpu.SMEM)
HBM = pl.BlockSpec(memory_space=pltpu.HBM)
UNROLL = 2


def fill_tables(scales, left):
    size = TILES * N2
    squares = [value * value for value in scales]
    total = sum(scales[1:], scales[0])
    square = sum(squares[1:], squares[0])
    shape = (size, 2 * size)
    row = lax.broadcasted_iota(jnp.int32, shape, 0)
    column = lax.bitwise_and(lax.broadcasted_iota(jnp.int32, shape, 1), size - 1)
    drift = jnp.where(row == column, -total, 0.0)
    second = jnp.where(row == column, -2.0 * square, 0.0)
    for d, unit, count in ((1, N3 * N2, N1), (2, 1, N2), (3, N2, N3)):
        digit = lax.bitwise_and(lax.div(row, unit), count - 1)
        rest = row - digit * unit
        back = column == rest + lax.bitwise_and(digit + count - 1, count - 1) * unit
        ahead = column == rest + lax.bitwise_and(digit + 1, count - 1) * unit
        drift = drift + jnp.where(back, scales[d], 0.0)
        second = second + jnp.where(back, squares[d], 0.0) + jnp.where(ahead, squares[d], 0.0)
    left[:, : 2 * size] = jnp.concatenate([second, drift], axis=0).astype(jnp.bfloat16)
    drift = jnp.where(row == column, scales[0], 0.0)
    second = jnp.where(row == column, squares[0], 0.0)
    left[:, 2 * size :] = jnp.concatenate([second, drift], axis=0).astype(jnp.bfloat16)


def step_rows(src, dst, first, count, left, factors, products):
    q0, s4, q4 = factors
    size = TILES * N2

    def rows_of(group):
        return range(first + group * UNROLL, first + min(count, (group + 1) * UNROLL))

    def parts(row):
        value = src[row].reshape(size, N4)
        high = value.astype(jnp.bfloat16)
        return jnp.concatenate([high, (value - high.astype(jnp.float32)).astype(jnp.bfloat16)], axis=0)

    last = [parts(first - 1)]

    def multiply(group):
        held = [parts(row) for row in rows_of(group)]
        below = last + held
        last[:] = [held[-1]]
        held = [jnp.concatenate(pair, axis=0) for pair in zip(held, below)]
        products[group % 2][:, : len(held) * N4] = jnp.dot(
            left[...], jnp.concatenate(held, axis=1), preferred_element_type=jnp.float32
        )

    groups = -(-count // UNROLL)
    multiply(0)
    for group in range(groups):
        if group + 1 < groups:
            multiply(group + 1)
        product = products[group % 2]
        for i, row in enumerate(rows_of(group)):
            lanes = slice(i * N4, (i + 1) * N4)
            for t in range(TILES):
                u, above = src[row, t], src[row + 1, t]
                back, ahead = pltpu.roll(u, 1, 1), pltpu.roll(u, N4 - 1, 1)
                second = product[t * N2 : (t + 1) * N2, lanes] + q0 * above
                drift = product[size + t * N2 : size + (t + 1) * N2, lanes] + s4 * back
                second = second + q4 * (back + ahead)
                speed = ADVECT + (0.5 * ADVECT) * jnp.tanh(u)
                dst[row, t] = (u + DIFFUSE * second) + speed * drift


def interpolate(nodes, fine, middle):
    u0, u1, u2, u3, u4 = nodes
    v2 = jnp.where(middle, u2, 0.5 * (u0 + u4))
    v1 = jnp.where(fine, u1, 0.5 * (u0 + v2))
    v3 = jnp.where(fine, u3, 0.5 * (v2 + u4))
    return u0, v1, v2, v3


def spaces(rows):
    state = pltpu.VMEM((rows + LOW + HIGH, TILES, N2, N4), jnp.float32)
    product = pltpu.VMEM((2 * TILES * N2, UNROLL * N4), jnp.float32)
    return [state, state, product, product]


def run_steps(bufs, rows, left, scales):
    states, products = bufs[0:2], bufs[2:4]
    factors = (scales[0] * scales[0], scales[4], scales[4] * scales[4])
    for step in range(STEPS):
        count = rows + LOW + HIGH - 2 * (step + 1)
        step_rows(states[step % 2], states[(step + 1) % 2], step + 1, count, left, factors, products)
    return states[STEPS % 2]


def ends_kernel(field, last, first, sems):
    rows = field.shape[0]
    one = pltpu.make_async_copy(field.at[pl.ds(rows - LOW, LOW)], last, sems.at[0])
    two = pltpu.make_async_copy(field.at[pl.ds(0, HIGH)], first, sems.at[1])
    one.start()
    two.start()
    one.wait()
    two.wait()


def load_rows(ref, first, count, state, at):
    def body(i, carry):
        for n1 in range(N1):
            for n3 in range(N3):
                state[at + i, n1 * N3 + n3] = ref[first + i, pl.ds(n1 * N2 * N3 + n3, N2, stride=N3), :]
        return carry

    lax.fori_loop(0, count, body, 0)


def scales_of(level):
    return [lax.shift_left(1, level[0, d]).astype(jnp.float32) * 0.125 for d in range(5)]


def first_cycle(level, left, rows, outs, bufs):
    me, grids = lax.axis_index("grid"), lax.axis_size("grid")
    levels, scales = [level[0, d] for d in range(5)], scales_of(level)
    parity = lax.rem(levels[0] + levels[1] + levels[2] + levels[3] + levels[4], 2)
    weight = (1 - 2 * parity).astype(jnp.float32) * (1.0 / math.sqrt(grids))
    done = run_steps(bufs, rows, left, scales)
    fine, middle = levels[0] >= 3, levels[0] >= 2
    block = outs[0][1].shape[0] // TILES
    for first, out in outs:
        for quad in range(0, block, 4):
            base = LOW + first + quad
            for t in range(TILES):
                values = interpolate([done[base + i, t] for i in range(5)], fine, middle)
                for i, value in enumerate(values):
                    out[(quad + i) * TILES + t] = weight * value
        lane = lax.broadcasted_iota(jnp.int32, (N2, N4), 1)
        tile = jnp.zeros((N2, N4), jnp.float32)
        for d, value in enumerate(scales + [levels[0].astype(jnp.float32), weight]):
            tile = jnp.where(lane == d, value, tile)
        sublane = lax.broadcasted_iota(jnp.int32, (N2, N4), 0)
        out[block * TILES] = jnp.where(sublane == me, tile, 0.0)


def middle_kernel(level, field, middle, near, left, *bufs):
    rows = field.shape[0] // 2
    block = rows // 2
    fill_tables(scales_of(level), left)
    load_rows(field, block - LOW, rows + LOW + HIGH, bufs[0], 0)
    side = lax.div(2 * lax.axis_index("grid"), lax.axis_size("grid"))
    upper = lax.rem(side + lax.axis_index("slab"), 2) == 0
    first = jnp.where(upper, block, 0)
    first_cycle(level, left, rows, ((first, middle), (block - first, near)), bufs)


def outer_kernel(later, level, left, before, field, after, out, *bufs):
    total = field.shape[0]
    block = out.shape[0] // TILES
    top = lax.rem(lax.axis_index("grid") + lax.axis_index("slab") + later, 2) == 0

    @pl.when(top)
    def _():
        load_rows(field, total - block - LOW, block + LOW, bufs[0], 0)
        load_rows(after, 0, HIGH, bufs[0], block + LOW)

    @pl.when(jnp.logical_not(top))
    def _():
        load_rows(before, 0, LOW, bufs[0], 0)
        load_rows(field, 0, block + HIGH, bufs[0], LOW)

    first_cycle(level, left, block, ((0, out),), bufs)


def sent_value(own, g, d):
    return jnp.broadcast_to(own[own.shape[0] - 1, pl.ds(g, 1), d : d + 1], (1, N4))


def tables_kernel(grids, own, left):
    def grid(g, carry):
        fill_tables([sent_value(own, g, d) for d in range(5)], left.at[g])
        return carry

    lax.fori_loop(0, grids, grid, 0)


def second_kernel(rows, grids, left, before, own, after, *refs):
    outs, total, bufs = refs[:-5], refs[-5], refs[-4:]
    extent = rows + LOW + HIGH

    def given(row, t):
        if row < LOW:
            return before[row * TILES + t]
        if row < LOW + rows:
            return own[(row - LOW) * TILES + t]
        return after[(row - LOW - rows) * TILES + t]

    total[...] = jnp.zeros_like(total)

    def grid(g, carry):
        tile = lambda d: jnp.broadcast_to(sent_value(own, g, d), (N2, N4))
        fine, middle, weight = tile(5) > 2.5, tile(5) > 1.5, tile(6)
        start = bufs[0]
        for quad in range(0, extent - 1, 4):
            for t in range(TILES):
                values = interpolate([given(quad + i, t) for i in range(5)], fine, middle)
                for i, value in enumerate(values):
                    start[quad + i, t] = value
        for t in range(TILES):
            start[extent - 1, t] = given(extent - 1, t)
        done = run_steps(bufs, rows, left.at[g], [tile(d) for d in range(5)])
        for quad in range(0, rows, 4):
            for t in range(TILES):
                values = interpolate([done[LOW + quad + i, t] for i in range(5)], fine, middle)
                for i, value in enumerate(values):
                    at = pl.ds(((quad + i) * TILES + t) * N2, N2)
                    total[at, :] = weight * value + total[at, :]
        return carry

    lax.fori_loop(0, grids, grid, 0)
    half = N2 // 2
    for d, out in enumerate(outs):
        slab = lax.bitwise_xor(lax.axis_index("slab"), d)
        first = lax.div(slab, 2) * (N3 * N2) + lax.rem(slab, 2) * half
        for n3 in range(N3):
            for n in range(half):
                out[n3, n] = total[pl.ds(first + n3 * N2 + n, rows, stride=TILES * N2), :]


def regroup_kernel(groups, *refs):
    received, outs = refs[: len(refs) // 2], refs[len(refs) // 2 :]
    me = lax.axis_index("grid")
    for e, out in enumerate(outs):
        for d, ref in enumerate(received):
            out[d] = ref[lax.rem(me + e, groups)]


def hier_kernel(groups, matrix, *refs):
    received, outs = refs[:groups], refs[groups:]
    me = lax.axis_index("grid")
    lanes = received[0].shape[3]
    count = matrix.shape[0] // groups
    for n in range(received[0].shape[1]):
        whole = jnp.concatenate([ref[:, n].reshape(-1, lanes) for ref in received], axis=0)
        high = whole.astype(jnp.bfloat16)
        rest = (whole - high.astype(jnp.float32)).astype(jnp.bfloat16)
        for d, out in enumerate(outs):
            part = matrix[pl.ds(lax.rem(me + d, groups) * count, count), :]
            out[n] = jnp.dot(part, high, preferred_element_type=jnp.float32) + jnp.dot(
                part, rest, preferred_element_type=jnp.float32
            )


def place_kernel(groups, *refs):
    received, out = refs[:-1], refs[-1]
    me = lax.axis_index("grid")
    parts, count = received[0].shape[0], received[0].shape[1]
    for d, ref in enumerate(received):
        n3 = lax.rem(me + groups - d, groups)
        for n in range(parts):
            out[pl.ds(n * N3 + n3, count, stride=parts * N3), :] = ref[n]


def kernel(body, out_shape, in_specs, scratch=(), limit=4, flops=0):
    single = not isinstance(out_shape, (list, tuple))
    return pl.pallas_call(
        body,
        out_shape=out_shape,
        in_specs=in_specs,
        out_specs=VMEM if single else [VMEM] * len(out_shape),
        scratch_shapes=list(scratch),
        compiler_params=pltpu.CompilerParams(vmem_limit_bytes=limit << 20),
        cost_estimate=pl.CostEstimate(flops=flops, bytes_accessed=1 << 20, transcendentals=flops // 30),
    )


def fast_sizes(grids, slabs):
    rows = N0 // slabs
    return rows, rows // grids


def fast_fits(grids, slabs):
    _, block = fast_sizes(grids, slabs)
    return grids == 4 and grids == N3 and slabs == 2 * N1 and block >= HIGH and block % 4 == 0


def floats(*shape):
    return jax.ShapeDtypeStruct(shape, jnp.float32)


def local_fast(field, levels, owner):
    grids, slabs = lax.axis_size("grid"), lax.axis_size("slab")
    rows, block = fast_sizes(grids, slabs)
    state = field[0]

    up = [(i, (i + 1) % slabs) for i in range(slabs)]
    down = [(j, i) for i, j in up]
    last, first = kernel(
        ends_kernel,
        [floats(LOW, Q, N4), floats(HIGH, Q, N4)],
        [HBM],
        [pltpu.SemaphoreType.DMA((2,))],
    )(pltpu.with_memory_space_constraint(state, pltpu.HBM))
    before = lax.ppermute(last, "slab", up)
    after = lax.ppermute(first, "slab", down)

    piece = floats(block * TILES + 1, N2, N4)
    work = 8192 * 40
    size = 2 * TILES * N2

    def table(*lead):
        return jax.ShapeDtypeStruct(lead + (size, 2 * size), jnp.bfloat16)

    middle, near, left = kernel(
        middle_kernel,
        [piece, piece, table()],
        [SMEM, VMEM],
        spaces(rows // 2),
        limit=6,
        flops=80 * work,
    )(levels, state)

    ready = lax.optimization_barrier((before, after, middle))

    def outer_block(later):
        return kernel(
            functools.partial(outer_kernel, later),
            piece,
            [SMEM] + [VMEM] * 4,
            spaces(block),
            limit=6,
            flops=48 * work,
        )(levels, left, ready[0], state, ready[1])

    edge = (lax.axis_index("grid") == 0) | (lax.axis_index("grid") == grids - 1)
    across = lax.ppermute(middle, "grid", [(1, 2), (2, 1)])
    first_out = outer_block(0)
    swapped = lax.ppermute(first_out, "grid", [(0, 1), (1, 0), (2, 3), (3, 2)])
    middle, near, _ = lax.optimization_barrier((middle, near, first_out))
    skipped = lax.ppermute(middle, "grid", [(0, 2), (3, 1)])
    inwards = lax.ppermute(near, "grid", [(0, 1), (3, 2)])
    second_out = outer_block(1)
    joined = swapped + second_out
    passed = lax.ppermute(joined, "grid", [(1, 3), (2, 0)])
    own = jnp.where(edge, joined, near) + across + skipped + inwards + passed

    chain = []
    for k in range(slabs):
        chain += [(g if k % 2 == 0 else grids - 1 - g) * slabs + k for g in range(grids)]
    forward = [(chain[i], chain[(i + 1) % len(chain)]) for i in range(len(chain))]
    backward = [(j, i) for i, j in forward]
    both = ("grid", "slab")
    before = lax.ppermute(own[(block - LOW) * TILES : block * TILES], both, forward)
    after = lax.ppermute(own[: HIGH * TILES], both, backward)

    left = kernel(
        functools.partial(tables_kernel, grids), table(grids), [VMEM], flops=30 * work
    )(own)
    half = N2 // 2
    sent = kernel(
        functools.partial(second_kernel, block, grids),
        [floats(N3, half, block, N4)] * slabs,
        [VMEM] * 4,
        [pltpu.VMEM((block * TILES * N2, N4), jnp.float32)] + spaces(block),
        limit=8,
        flops=400 * 8192 * 40,
    )(left, before, own, after)

    def shared(values, axis, partner):
        members = range(lax.axis_size(axis))
        received = [values[0]]
        for d, value in enumerate(values[1:], 1):
            received.append(lax.ppermute(value, axis, [(i, partner(i, d)) for i in members]))
        return received

    ahead = lambda i, d: (i + d) % grids
    by_slab = shared(sent, "slab", lambda i, d: i ^ d)
    ready = kernel(
        functools.partial(regroup_kernel, grids),
        [floats(slabs, half, block, N4)] * grids,
        [VMEM] * slabs,
    )(*by_slab)
    by_grid = shared(ready, "grid", ahead)

    me, at = lax.axis_index("grid"), lax.axis_index("slab")
    place = jnp.arange(N0, dtype=jnp.int32)
    source = (me - place // (slabs * block)) % grids
    slab = at ^ (place // block % slabs)
    source = jnp.where(slab % 2 == 0, source, grids - 1 - source)
    column = ((slab * grids + source) * block + place % block)[None, :]
    row = owner[:, None]
    reach = jnp.where(row > 0, row & -row, 0)
    half_of = jnp.where(row > 0, -0.5, 0.0)
    matrix = (
        (column == row).astype(jnp.float32)
        + half_of * (column == row - reach)
        + half_of * (column == (row + reach) % N0)
    ).astype(jnp.bfloat16)
    group = N0 // grids
    hier = kernel(
        functools.partial(hier_kernel, grids),
        [floats(half, group, N4)] * grids,
        [VMEM] * (1 + grids),
    )(matrix, *by_grid)
    received = shared(hier, "grid", ahead)
    out = kernel(
        functools.partial(place_kernel, grids), floats(group * half * N3, N4), [VMEM] * grids
    )(*received)
    return out.reshape(group, Q // slabs, N4)


def local(field, levels, owner):
    if fast_fits(lax.axis_size("grid"), lax.axis_size("slab")):
        return local_fast(field, levels, owner)
    return local_general(field, levels, owner)


def solution(mesh):
    in_specs = (P(("copies", "grid"), "slab", None, None), P(("copies", "grid"), None), P("copies"))
    out_specs = P(("copies", "grid"), "slab", None)
    return jax.shard_map(local, mesh=mesh, in_specs=in_specs, out_specs=out_specs, check_vma=False)
```

```python
import functools
import math

import jax
import jax.numpy as jnp
import numpy as np
from jax import lax
from jax.experimental import pallas as pl
from jax.experimental.pallas import tpu as pltpu
from jax.sharding import PartitionSpec as P


N0 = 128
N1 = 2
N2 = 8
N3 = 4
N4 = 128
STEPS = 4
Q = 64

ADVECT = 0.08
DIFFUSE = 0.03

LOW = STEPS
HIGH = STEPS + 1
TILES = N1 * N3


def extended_2(value, sides, width):
    for axis, dim in sides:
        count, length = (lax.axis_size(axis), value.shape[dim])
        up = [(i, (i + 1) % count) for i in range(count)]
        down = [(j, i) for i, j in up]
        last = lax.slice_in_dim(value, length - width, length, axis=dim)
        first = lax.slice_in_dim(value, 0, width, axis=dim)
        before = lax.ppermute(last, axis, up)
        after = lax.ppermute(first, axis, down)
        value = jnp.concatenate([before, value, after], axis=dim)
    return value


def build_tables(count):
    depth = count.bit_length() - 1
    matrix = np.eye(count)
    inverse = np.zeros((count, count))
    inverse[0, 0] = 1.0
    level_rows = np.zeros(count, np.int32)
    for index in range(1, count):
        zeros = (index & -index).bit_length() - 1
        spacing = 1 << zeros
        matrix[index, index - spacing] -= 0.5
        matrix[index, (index + spacing) % count] -= 0.5
        level_rows[index] = depth - zeros
    for zeros in range(depth - 1, -1, -1):
        spacing = 1 << zeros
        for index in range(spacing, count, 2 * spacing):
            inverse[index] = 0.5 * (inverse[index - spacing] + inverse[(index + spacing) % count])
            inverse[index, index] += 1.0
    return (matrix.astype(np.float32), inverse.astype(np.float32), level_rows)


def advance(extended, scales, padded):
    length = extended.shape[padded] - 2
    centre = lax.slice_in_dim(extended, 1, length + 1, axis=padded)
    speed = 1.0 + 0.5 * jnp.tanh(centre)
    change = jnp.zeros_like(centre)
    for axis in range(5):
        if axis == padded:
            back = lax.slice_in_dim(extended, 0, length, axis=padded)
            ahead = lax.slice_in_dim(extended, 2, length + 2, axis=padded)
        else:
            back = jnp.roll(centre, 1, axis)
            ahead = jnp.roll(centre, -1, axis)
        change = (
            change
            - ADVECT * scales[axis] * speed * (centre - back)
            + DIFFUSE * scales[axis] ** 2 * (ahead - 2.0 * centre + back)
        )
    return centre + change


def regroup_rows(stepped):
    return lax.all_to_all(stepped, "slab", split_axis=1, concat_axis=0, tiled=True)


def local_general(field, levels, owner):
    matrix, inverse, level_rows = build_tables(N0)
    matrix = jnp.asarray(matrix)
    inverse = jnp.asarray(inverse)
    depth = N0.bit_length() - 1
    level_vec = levels[0]
    scales = jnp.exp2(level_vec.astype(jnp.float32)) / 8.0
    weight = jnp.where(jnp.sum(level_vec) % 2 == 0, 1.0, -1.0).astype(jnp.float32) / math.sqrt(
        lax.axis_size("grid")
    )
    keep = (jnp.asarray(level_rows) <= depth - 3 + level_vec[0]).astype(jnp.float32)[:, None, None]

    def evolve_rows(state):
        rows = state.shape[0]
        grid5 = state.reshape(rows, N1, N2, N3, N4)
        for _ in range(STEPS):
            extended = extended_2(grid5, (("slab", 0),), 1)
            grid5 = advance(extended, scales, 0)
        return grid5.reshape(rows, Q, N4)

    def hierarchise(whole):
        hier = jnp.dot(matrix, whole.reshape(N0, -1), precision=lax.Precision.HIGHEST)
        return weight * keep * hier.reshape(whole.shape)

    def reduce_terms(terms):
        return lax.psum_scatter(terms[owner], "grid", scatter_dimension=0, tiled=True)

    stepped = evolve_rows(field[0])
    summed = reduce_terms(hierarchise(regroup_rows(stepped)))
    ordered = lax.all_gather(summed, "grid", axis=0, tiled=True)
    position = jnp.zeros((N0,), jnp.int32).at[owner].set(jnp.arange(N0, dtype=jnp.int32))
    combined = ordered[position]
    masked = (keep * combined).reshape(N0, -1)
    nodal = jnp.dot(inverse, masked, precision=lax.Precision.HIGHEST).reshape(combined.shape)
    state = lax.all_to_all(nodal, "slab", split_axis=0, concat_axis=1, tiled=True)
    stepped = evolve_rows(state)
    summed = reduce_terms(hierarchise(regroup_rows(stepped)))
    return summed


VMEM = pl.BlockSpec(memory_space=pltpu.VMEM)
SMEM = pl.BlockSpec(memory_space=pltpu.SMEM)
HBM = pl.BlockSpec(memory_space=pltpu.HBM)
UNROLL = 2


def fill_tables(scales, left):
    size = TILES * N2
    squares = [value * value for value in scales]
    total = sum(scales[1:], scales[0])
    square = sum(squares[1:], squares[0])
    shape = (size, 2 * size)
    row = lax.broadcasted_iota(jnp.int32, shape, 0)
    column = lax.bitwise_and(lax.broadcasted_iota(jnp.int32, shape, 1), size - 1)
    drift = jnp.where(row == column, -total, 0.0)
    second = jnp.where(row == column, -2.0 * square, 0.0)
    for d, unit, count in ((1, N3 * N2, N1), (2, 1, N2), (3, N2, N3)):
        digit = lax.bitwise_and(lax.div(row, unit), count - 1)
        rest = row - digit * unit
        back = column == rest + lax.bitwise_and(digit + count - 1, count - 1) * unit
        ahead = column == rest + lax.bitwise_and(digit + 1, count - 1) * unit
        drift = drift + jnp.where(back, scales[d], 0.0)
        second = second + jnp.where(back, squares[d], 0.0) + jnp.where(ahead, squares[d], 0.0)
    left[:, : 2 * size] = jnp.concatenate([second, drift], axis=0).astype(jnp.bfloat16)
    drift = jnp.where(row == column, scales[0], 0.0)
    second = jnp.where(row == column, squares[0], 0.0)
    left[:, 2 * size :] = jnp.concatenate([second, drift], axis=0).astype(jnp.bfloat16)


def step_rows(src, dst, first, count, left, factors, products):
    q0, s4, q4 = factors
    size = TILES * N2

    def rows_of(group):
        return range(first + group * UNROLL, first + min(count, (group + 1) * UNROLL))

    def parts(row):
        value = src[row].reshape(size, N4)
        high = value.astype(jnp.bfloat16)
        return jnp.concatenate([high, (value - high.astype(jnp.float32)).astype(jnp.bfloat16)], axis=0)

    last = [parts(first - 1)]

    def multiply(group):
        held = [parts(row) for row in rows_of(group)]
        below = last + held
        last[:] = [held[-1]]
        held = [jnp.concatenate(pair, axis=0) for pair in zip(held, below)]
        products[group % 2][:, : len(held) * N4] = jnp.dot(
            left[...], jnp.concatenate(held, axis=1), preferred_element_type=jnp.float32
        )

    groups = -(-count // UNROLL)
    multiply(0)
    for group in range(groups):
        if group + 1 < groups:
            multiply(group + 1)
        product = products[group % 2]
        for i, row in enumerate(rows_of(group)):
            lanes = slice(i * N4, (i + 1) * N4)
            for t in range(TILES):
                u, above = src[row, t], src[row + 1, t]
                back, ahead = pltpu.roll(u, 1, 1), pltpu.roll(u, N4 - 1, 1)
                second = product[t * N2 : (t + 1) * N2, lanes] + q0 * above
                drift = product[size + t * N2 : size + (t + 1) * N2, lanes] + s4 * back
                second = second + q4 * (back + ahead)
                speed = ADVECT + (0.5 * ADVECT) * jnp.tanh(u)
                dst[row, t] = (u + DIFFUSE * second) + speed * drift


def interpolate(nodes, fine, middle):
    u0, u1, u2, u3, u4 = nodes
    v2 = jnp.where(middle, u2, 0.5 * (u0 + u4))
    v1 = jnp.where(fine, u1, 0.5 * (u0 + v2))
    v3 = jnp.where(fine, u3, 0.5 * (v2 + u4))
    return u0, v1, v2, v3


def spaces(rows):
    state = pltpu.VMEM((rows + LOW + HIGH, TILES, N2, N4), jnp.float32)
    product = pltpu.VMEM((2 * TILES * N2, UNROLL * N4), jnp.float32)
    return [state, state, product, product]


def run_steps(bufs, rows, left, scales):
    states, products = bufs[0:2], bufs[2:4]
    factors = (scales[0] * scales[0], scales[4], scales[4] * scales[4])
    for step in range(STEPS):
        count = rows + LOW + HIGH - 2 * (step + 1)
        step_rows(states[step % 2], states[(step + 1) % 2], step + 1, count, left, factors, products)
    return states[STEPS % 2]


def ends_kernel(field, last, first, sems):
    rows = field.shape[0]
    one = pltpu.make_async_copy(field.at[pl.ds(rows - LOW, LOW)], last, sems.at[0])
    two = pltpu.make_async_copy(field.at[pl.ds(0, HIGH)], first, sems.at[1])
    one.start()
    two.start()
    one.wait()
    two.wait()


def load_rows(ref, first, count, state, at):
    def body(i, carry):
        for n1 in range(N1):
            for n3 in range(N3):
                state[at + i, n1 * N3 + n3] = ref[first + i, pl.ds(n1 * N2 * N3 + n3, N2, stride=N3), :]
        return carry

    lax.fori_loop(0, count, body, 0)


def scales_of(level):
    return [lax.shift_left(1, level[0, d]).astype(jnp.float32) * 0.125 for d in range(5)]


def first_cycle(level, left, rows, outs, bufs):
    me, grids = lax.axis_index("grid"), lax.axis_size("grid")
    levels, scales = [level[0, d] for d in range(5)], scales_of(level)
    parity = lax.rem(levels[0] + levels[1] + levels[2] + levels[3] + levels[4], 2)
    weight = (1 - 2 * parity).astype(jnp.float32) * (1.0 / math.sqrt(grids))
    done = run_steps(bufs, rows, left, scales)
    fine, middle = levels[0] >= 3, levels[0] >= 2
    block = outs[0][1].shape[0] // TILES
    for first, out in outs:
        for quad in range(0, block, 4):
            base = LOW + first + quad
            for t in range(TILES):
                values = interpolate([done[base + i, t] for i in range(5)], fine, middle)
                for i, value in enumerate(values):
                    out[(quad + i) * TILES + t] = weight * value
        lane = lax.broadcasted_iota(jnp.int32, (N2, N4), 1)
        tile = jnp.zeros((N2, N4), jnp.float32)
        for d, value in enumerate(scales + [levels[0].astype(jnp.float32), weight]):
            tile = jnp.where(lane == d, value, tile)
        sublane = lax.broadcasted_iota(jnp.int32, (N2, N4), 0)
        out[block * TILES] = jnp.where(sublane == me, tile, 0.0)


def middle_kernel(level, field, middle, near, left, *bufs):
    rows = field.shape[0] // 2
    block = rows // 2
    fill_tables(scales_of(level), left)
    load_rows(field, block - LOW, rows + LOW + HIGH, bufs[0], 0)
    side = lax.div(2 * lax.axis_index("grid"), lax.axis_size("grid"))
    upper = lax.rem(side + lax.axis_index("slab"), 2) == 0
    first = jnp.where(upper, block, 0)
    first_cycle(level, left, rows, ((first, middle), (block - first, near)), bufs)


def outer_kernel(later, level, left, before, field, after, out, *bufs):
    total = field.shape[0]
    block = out.shape[0] // TILES
    top = lax.rem(lax.axis_index("grid") + lax.axis_index("slab") + later, 2) == 0

    @pl.when(top)
    def _():
        load_rows(field, total - block - LOW, block + LOW, bufs[0], 0)
        load_rows(after, 0, HIGH, bufs[0], block + LOW)

    @pl.when(jnp.logical_not(top))
    def _():
        load_rows(before, 0, LOW, bufs[0], 0)
        load_rows(field, 0, block + HIGH, bufs[0], LOW)

    first_cycle(level, left, block, ((0, out),), bufs)


def sent_value(own, g, d):
    return jnp.broadcast_to(own[own.shape[0] - 1, pl.ds(g, 1), d : d + 1], (1, N4))


def tables_kernel(grids, own, left):
    def grid(g, carry):
        fill_tables([sent_value(own, g, d) for d in range(5)], left.at[g])
        return carry

    lax.fori_loop(0, grids, grid, 0)


def second_kernel(rows, grids, left, before, own, after, *refs):
    outs, total, bufs = refs[:-5], refs[-5], refs[-4:]
    extent = rows + LOW + HIGH

    def given(row, t):
        if row < LOW:
            return before[row * TILES + t]
        if row < LOW + rows:
            return own[(row - LOW) * TILES + t]
        return after[(row - LOW - rows) * TILES + t]

    total[...] = jnp.zeros_like(total)

    def grid(g, carry):
        tile = lambda d: jnp.broadcast_to(sent_value(own, g, d), (N2, N4))
        fine, middle, weight = tile(5) > 2.5, tile(5) > 1.5, tile(6)
        start = bufs[0]
        for quad in range(0, extent - 1, 4):
            for t in range(TILES):
                values = interpolate([given(quad + i, t) for i in range(5)], fine, middle)
                for i, value in enumerate(values):
                    start[quad + i, t] = value
        for t in range(TILES):
            start[extent - 1, t] = given(extent - 1, t)
        done = run_steps(bufs, rows, left.at[g], [tile(d) for d in range(5)])
        for quad in range(0, rows, 4):
            for t in range(TILES):
                values = interpolate([done[LOW + quad + i, t] for i in range(5)], fine, middle)
                for i, value in enumerate(values):
                    at = pl.ds(((quad + i) * TILES + t) * N2, N2)
                    total[at, :] = weight * value + total[at, :]
        return carry

    lax.fori_loop(0, grids, grid, 0)
    half = N2 // 2
    for d, out in enumerate(outs):
        slab = lax.bitwise_xor(lax.axis_index("slab"), d)
        first = lax.div(slab, 2) * (N3 * N2) + lax.rem(slab, 2) * half
        for n3 in range(N3):
            for n in range(half):
                out[n3, n] = total[pl.ds(first + n3 * N2 + n, rows, stride=TILES * N2), :]


def regroup_kernel(groups, *refs):
    received, outs = refs[:-groups], refs[-groups:]
    me = lax.axis_index("grid")
    for e, out in enumerate(outs):
        for d, ref in enumerate(received):
            out[d] = ref[lax.rem(me + e, groups)]


def hier_kernel(groups, matrix, *refs):
    received, outs = refs[: 2 * groups], refs[2 * groups :]
    me = lax.axis_index("grid")
    lanes = received[0].shape[3]
    count = matrix.shape[0] // groups
    for n in range(received[0].shape[1]):
        pairs = [(received[d], received[groups + d]) for d in range(groups)]
        whole = jnp.concatenate([ref[:, n].reshape(-1, lanes) for pair in pairs for ref in pair], axis=0)
        high = whole.astype(jnp.bfloat16)
        rest = (whole - high.astype(jnp.float32)).astype(jnp.bfloat16)
        for d, out in enumerate(outs):
            part = matrix[pl.ds(lax.rem(me + d, groups) * count, count), :]
            out[n] = jnp.dot(part, high, preferred_element_type=jnp.float32) + jnp.dot(
                part, rest, preferred_element_type=jnp.float32
            )


def place_kernel(groups, *refs):
    received, out, held, sems = refs[:-3], refs[-3], refs[-2], refs[-1]
    me = lax.axis_index("grid")
    parts, count = received[0].shape[0], received[0].shape[1]
    chunks, stride = sems.shape[0], parts * N3
    step = count // chunks
    copies = []
    for c in range(chunks):
        for d, ref in enumerate(received):
            n3 = lax.rem(me + groups - d, groups)
            for n in range(parts):
                at = pl.ds(c * step * stride + n * N3 + n3, step, stride=stride)
                held[at, :] = ref[n, c * step : (c + 1) * step, :]
        span = pl.ds(c * step * stride, step * stride)
        copies.append(pltpu.make_async_copy(held.at[span], out.at[span], sems.at[c]))
        copies[-1].start()
    for copy in copies:
        copy.wait()


def kernel(body, out_shape, in_specs, scratch=(), limit=4, flops=0, space=VMEM):
    single = not isinstance(out_shape, (list, tuple))
    return pl.pallas_call(
        body,
        out_shape=out_shape,
        in_specs=in_specs,
        out_specs=space if single else [space] * len(out_shape),
        scratch_shapes=list(scratch),
        compiler_params=pltpu.CompilerParams(vmem_limit_bytes=limit << 20),
        cost_estimate=pl.CostEstimate(flops=flops, bytes_accessed=1 << 20, transcendentals=flops // 30),
    )


def fast_sizes(grids, slabs):
    rows = N0 // slabs
    return rows, rows // grids


def fast_fits(grids, slabs):
    _, block = fast_sizes(grids, slabs)
    return grids == 4 and grids == N3 and slabs == 2 * N1 and block >= HIGH and block % 4 == 0


def floats(*shape):
    return jax.ShapeDtypeStruct(shape, jnp.float32)


def local_fast(field, levels, owner):
    grids, slabs = lax.axis_size("grid"), lax.axis_size("slab")
    rows, block = fast_sizes(grids, slabs)
    state = field[0]

    up = [(i, (i + 1) % slabs) for i in range(slabs)]
    down = [(j, i) for i, j in up]
    last, first = kernel(
        ends_kernel,
        [floats(LOW, Q, N4), floats(HIGH, Q, N4)],
        [HBM],
        [pltpu.SemaphoreType.DMA((2,))],
    )(pltpu.with_memory_space_constraint(state, pltpu.HBM))
    before = lax.ppermute(last, "slab", up)
    after = lax.ppermute(first, "slab", down)

    piece = floats(block * TILES + 1, N2, N4)
    work = 8192 * 40
    size = 2 * TILES * N2

    def table(*lead):
        return jax.ShapeDtypeStruct(lead + (size, 2 * size), jnp.bfloat16)

    middle, near, left = kernel(
        middle_kernel,
        [piece, piece, table()],
        [SMEM, VMEM],
        spaces(rows // 2),
        limit=6,
        flops=80 * work,
    )(levels, state)

    ready = lax.optimization_barrier((before, after, middle))

    def outer_block(later):
        return kernel(
            functools.partial(outer_kernel, later),
            piece,
            [SMEM] + [VMEM] * 4,
            spaces(block),
            limit=6,
            flops=48 * work,
        )(levels, left, ready[0], state, ready[1])

    edge = (lax.axis_index("grid") == 0) | (lax.axis_index("grid") == grids - 1)
    across = lax.ppermute(middle, "grid", [(1, 2), (2, 1)])
    first_out = outer_block(0)
    swapped = lax.ppermute(first_out, "grid", [(0, 1), (1, 0), (2, 3), (3, 2)])
    middle, near, _ = lax.optimization_barrier((middle, near, first_out))
    skipped = lax.ppermute(middle, "grid", [(0, 2), (3, 1)])
    inwards = lax.ppermute(near, "grid", [(0, 1), (3, 2)])
    second_out = outer_block(1)
    joined = swapped + second_out
    passed = lax.ppermute(joined, "grid", [(1, 3), (2, 0)])
    own = jnp.where(edge, joined, near) + across + skipped + inwards + passed

    chain = []
    for k in range(slabs):
        chain += [(g if k % 2 == 0 else grids - 1 - g) * slabs + k for g in range(grids)]
    forward = [(chain[i], chain[(i + 1) % len(chain)]) for i in range(len(chain))]
    backward = [(j, i) for i, j in forward]
    both = ("grid", "slab")
    before = lax.ppermute(own[(block - LOW) * TILES : block * TILES], both, forward)
    after = lax.ppermute(own[: HIGH * TILES], both, backward)

    left = kernel(
        functools.partial(tables_kernel, grids), table(grids), [VMEM], flops=30 * work
    )(own)
    half = N2 // 2
    sent = kernel(
        functools.partial(second_kernel, block, grids),
        [floats(N3, half, block, N4)] * slabs,
        [VMEM] * 4,
        [pltpu.VMEM((block * TILES * N2, N4), jnp.float32)] + spaces(block),
        limit=8,
        flops=400 * 8192 * 40,
    )(left, before, own, after)

    def exchanged(value, axis, partner, d):
        pairs = [(i, partner(i, d)) for i in range(lax.axis_size(axis))]
        return lax.ppermute(value, axis, pairs)

    other = lambda i, d: i ^ d
    ahead = lambda i, d: (i + d) % grids
    far_parts = [exchanged(sent[d], "slab", other, d) for d in (2, 3)]
    near_parts = [sent[0], exchanged(sent[1], "slab", other, 1)]
    by_grid = []
    for parts in (near_parts, far_parts):
        ready = kernel(
            functools.partial(regroup_kernel, grids),
            [floats(len(parts), half, block, N4)] * grids,
            [VMEM] * len(parts),
        )(*parts)
        by_grid += [ready[0]] + [exchanged(ready[d], "grid", ahead, d) for d in range(1, grids)]

    me, at = lax.axis_index("grid"), lax.axis_index("slab")
    place = jnp.arange(N0, dtype=jnp.int32)
    source = (me - place // (slabs * block)) % grids
    slab = at ^ (place // block % slabs)
    source = jnp.where(slab % 2 == 0, source, grids - 1 - source)
    column = ((slab * grids + source) * block + place % block)[None, :]
    row = owner[:, None]
    reach = jnp.where(row > 0, row & -row, 0)
    half_of = jnp.where(row > 0, -0.5, 0.0)
    matrix = (
        (column == row).astype(jnp.float32)
        + half_of * (column == row - reach)
        + half_of * (column == (row + reach) % N0)
    ).astype(jnp.bfloat16)
    group = N0 // grids
    hier = kernel(
        functools.partial(hier_kernel, grids),
        [floats(half, group, N4)] * grids,
        [VMEM] * (1 + 2 * grids),
    )(matrix, *by_grid)
    received = [hier[0]] + [exchanged(hier[d], "grid", ahead, d) for d in range(1, grids)]
    out = kernel(
        functools.partial(place_kernel, grids),
        floats(group * half * N3, N4),
        [VMEM] * grids,
        [pltpu.VMEM((group * half * N3, N4), jnp.float32), pltpu.SemaphoreType.DMA((4,))],
        space=HBM,
    )(*received)
    return out.reshape(group, Q // slabs, N4)


def local(field, levels, owner):
    if fast_fits(lax.axis_size("grid"), lax.axis_size("slab")):
        return local_fast(field, levels, owner)
    return local_general(field, levels, owner)


def solution(mesh):
    in_specs = (P(("copies", "grid"), "slab", None, None), P(("copies", "grid"), None), P("copies"))
    out_specs = P(("copies", "grid"), "slab", None)
    return jax.shard_map(local, mesh=mesh, in_specs=in_specs, out_specs=out_specs, check_vma=False)
```
